32 devices in a mesh: dp: 8 (over y, x, core), mp: 4 (over z).
Axes of the slice: x: 2, y: 2, z: 4, core: 2. Of those that a mesh axis runs over, the one named last changes fastest.
Arguments:
- hidden_in: bfloat16 [16384, 2048], P('dp', 'mp')
- positions: int32 [16384], P('dp'), may hold values from 0 to 1023, as said below
- head_counts: int32 [4], replicated, may hold values from 4 to 6, as said below
- attention_gain: float32 [2048], P('mp'), may hold values from 0.5 to 1.5
- query_projection_weight: bfloat16 [2048, 1536], P(None, 'mp'), may hold values from -0.125 to 0.125
- key_weight: bfloat16 [2048, 320], replicated, may hold values from -0.125 to 0.125
- value_weight: bfloat16 [2048, 320], replicated, may hold values from -0.125 to 0.125
- query_gain: float32 [64], replicated, may hold values from 0.25 to 1.75
- key_gain: float32 [64], replicated, may hold values from 0.25 to 1.75
- output_weight: bfloat16 [1536, 2048], P(None, 'mp'), may hold values from -0.75 to 0.75
- feedforward_gain: float32 [2048], P('mp'), may hold values from 0.5 to 1.5
- gate_weight: bfloat16 [2048, 4096], P(None, 'mp'), may hold values from -0.125 to 0.125
- up_weight: bfloat16 [2048, 4096], P(None, 'mp'), may hold values from -0.125 to 0.125
- down_projection_weight: bfloat16 [4096, 2048], P('mp'), may hold values from -0.125 to 0.125
- cotangent: bfloat16 [16384, 2048], P('dp', 'mp'), may hold values from -6 to 6
Outputs:
- output: bfloat16 [16384, 2048], P('dp', 'mp')
- input_gradient: float32 [16384, 2048], P('dp', 'mp')
- attention_gain_gradient: float32 [2048], P('mp')
- query_weight_gradient: float32 [2048, 1536], P(None, 'mp')
- key_weight_gradient: float32 [2048, 320], replicated
- value_weight_gradient: float32 [2048, 320], replicated
- query_gain_gradient: float32 [64], replicated
- key_gain_gradient: float32 [64], replicated
- output_projection_gradient: float32 [1536, 2048], P(None, 'mp')
- feedforward_gain_gradient: float32 [2048], P('mp')
- gate_weight_gradient: float32 [2048, 4096], P(None, 'mp')
- up_weight_gradient: float32 [2048, 4096], P(None, 'mp')
- down_weight_gradient: float32 [4096, 2048], P('mp')
The draws below stay inside these ranges and needn't reach their ends.
Inputs may be any that keep to these rules, and one draw needn't show every extreme that they name: `head_counts`: the counts sum to 20; index m's live heads follow those of lower indices; the largest count is 6 in every draw. `positions`: position ids count up by one along each sequence of 1024 tokens and restart at zero at its start and at up to three points inside it; the first sequence of all has no restart inside it.
All inputs are finite; a program needn't handle non-finite values.
Results may differ from the reference program's by a relative error of at most 0.025.
Values may be sent and summed in bfloat16 or wider, within the bound.
No kernel may reach another device: no remote copies, remote signals or barrier semaphores. Data moves between devices by JAX's collectives and lax.ppermute only.
A program may use at most 256 MiB of HBM per device.

```python
import math
import jax
import jax.numpy as jnp
from jax import lax

D = 2048
QH = 20
KVH = 5
HD = 64
FF = 4096
SEQ_DEV = 2
LEN = 1024
TOKENS = 16384
HMAX = 6
SLOTS = 24
QPG = 4
BLK = 512
NBLK = 2
N_DP = 8
N_MP = 4


def draw_hidden_in(key, part):
    noise_key = jax.random.fold_in(key, 11)
    column_key = jax.random.fold_in(key, 12)
    row_key = jax.random.fold_in(key, 13)
    rising = 0.35 * jnp.exp(math.log(3.0) * jnp.arange(D, dtype=jnp.float32) / D)
    columns = rising * jnp.exp(jax.random.uniform(column_key, (D,), jnp.float32, -0.55, 0.55))
    noise = jnp.clip(jax.random.normal(noise_key, (TOKENS, D), jnp.float32), -6.0, 6.0)
    rows = jnp.exp(jax.random.uniform(row_key, (TOKENS, 1), jnp.float32, math.log(0.3), math.log(3.0)))
    return (noise * rows * columns[None, :]).astype(jnp.bfloat16)


def draw_positions(key, part):
    seqs = TOKENS // LEN
    cuts = jax.random.randint(jax.random.fold_in(key, 21), (seqs, 3, 1), 1, LEN)
    first = (jnp.arange(seqs, dtype=jnp.int32) == 0)[:, None, None]
    cuts = jnp.where(first, LEN, cuts)
    index = jnp.arange(LEN, dtype=jnp.int32)
    last = jnp.max(jnp.where(cuts <= index[None, None, :], cuts, 0), axis=1)
    return (index[None, :] - last).reshape(TOKENS).astype(jnp.int32)


def draw_head_counts(key, part):
    base = QH // N_MP
    extra = QH % N_MP
    order = jax.random.permutation(jax.random.fold_in(key, 31), N_MP)
    if extra > 0:
        counts = base + jnp.where(order < extra, 1, 0)
    else:
        flag = jax.random.randint(jax.random.fold_in(key, 32), (), 0, 2)
        halves = jnp.where(order < N_MP // 2, 1, -1)
        single = jnp.where(order == 0, 1, jnp.where(order == 1, -1, 0))
        counts = base + jnp.where(flag == 0, halves, single)
    return counts.astype(jnp.int32)


def block_levels(rng, shape, cuts, least, high):
    level, own = 1.0, jax.random.fold_in(rng, 6)
    for axis_at, parts in cuts:
        draws = jnp.exp(jax.random.uniform(jax.random.fold_in(own, axis_at), (parts,), jnp.float32, least / len(cuts), high / len(cuts)))
        level = level * jnp.repeat(draws, shape[axis_at] // parts).reshape([-1 if axis == axis_at else 1 for axis in range(len(shape))])
    return level


def normal_values(rng, dims, deviation, most, cuts=(), kind=jnp.bfloat16):
    factor_of = block_levels(rng, dims, cuts, -0.22, 0.18) if cuts else 1.0
    drawn = jax.random.normal(rng, dims, jnp.float32) * deviation * factor_of
    return jnp.minimum(jnp.maximum(drawn, -most), most).astype(kind)


def setup_inputs(seed: int = 0) -> dict:
    key_list = jax.random.split(jax.random.key(seed), 16)
    hidden_in = draw_hidden_in(jax.random.fold_in(key_list[15], 71), 0)
    positions = draw_positions(jax.random.fold_in(key_list[15], 71), 0)
    head_counts = draw_head_counts(jax.random.fold_in(key_list[15], 71), 0)
    attention_gain = jnp.clip(1.0 + 0.1 * jax.random.normal(key_list[3], (D,), jnp.float32), 0.5, 1.5)
    query_projection_weight = normal_values(key_list[4], (D, SLOTS * HD), D ** -0.5, 0.125, ((1, 4),))
    key_weight = normal_values(key_list[5], (D, KVH * HD), D ** -0.5, 0.125)
    value_weight = normal_values(key_list[6], (D, KVH * HD), D ** -0.5, 0.125)
    query_gain = jnp.clip(1.0 + 0.15 * jax.random.normal(key_list[7], (HD,), jnp.float32), 0.25, 1.75)
    key_gain = jnp.clip(1.0 + 0.15 * jax.random.normal(key_list[8], (HD,), jnp.float32), 0.25, 1.75)
    output_weight = normal_values(key_list[9], (SLOTS * HD, D), HD ** -0.5, 0.75, ((1, 4),))
    feedforward_gain = jnp.clip(1.0 + 0.1 * jax.random.normal(key_list[10], (D,), jnp.float32), 0.5, 1.5)
    gate_weight = normal_values(key_list[11], (D, FF), D ** -0.5, 0.125, ((1, 4),))
    up_weight = normal_values(key_list[12], (D, FF), D ** -0.5, 0.125, ((1, 4),))
    down_projection_weight = normal_values(key_list[13], (FF, D), (FF // 2) ** -0.5, 0.125, ((0, 4),))
    cotangent = normal_values(key_list[14], (TOKENS, D), 1.0, 6.0, ((0, 8), (1, 4)))
    return dict(hidden_in=hidden_in, positions=positions, head_counts=head_counts, attention_gain=attention_gain, query_projection_weight=query_projection_weight, key_weight=key_weight, value_weight=value_weight, query_gain=query_gain, key_gain=key_gain, output_weight=output_weight, feedforward_gain=feedforward_gain, gate_weight=gate_weight, up_weight=up_weight, down_projection_weight=down_projection_weight, cotangent=cotangent)


epsilon = 1e-05
rope_base = 10000.0
masked_score = -1e+30
top_precision_mode = lax.Precision.HIGHEST

@jax.custom_vjp
def low(v):
    return lax.optimization_barrier(v.astype(jnp.bfloat16)).astype(jnp.float32)

@jax.custom_vjp
def low_back(v):
    return v

def low_keep(v):
    return (low(v), None)

def low_pass(kept, grad):
    return (grad,)

def back_keep(v):
    return (v, None)

def back_low(kept, grad):
    return (low(grad),)
low.defvjp(low_keep, low_pass)
low_back.defvjp(back_keep, back_low)

def rotary_tables(positions):
    half = HD // 2
    inverse = jnp.exp(-math.log(rope_base) * (2.0 * jnp.arange(half, dtype=jnp.float32)) / HD)
    angles = positions.astype(jnp.float32)[..., None] * inverse
    angles = jnp.concatenate([angles, angles], axis=-1)
    return (jnp.cos(angles), jnp.sin(angles))

def rotate(vectors, cosine, sine):
    half = vectors.shape[-1] // 2
    turned = jnp.concatenate([-vectors[..., half:], vectors[..., :half]], axis=-1)
    return vectors * cosine + turned * sine

def head_norm(vectors, gain):
    return vectors * lax.rsqrt(lax.optimization_barrier(jnp.mean(vectors * vectors, axis=-1, keepdims=True)) + epsilon) * gain

def slot_tables(head_counts):
    offsets = jnp.cumsum(head_counts) - head_counts
    within = jnp.arange(HMAX, dtype=jnp.int32)
    heads = offsets[:, None] + within[None, :]
    live = within[None, :] < head_counts[:, None]
    groups = jnp.minimum(heads // QPG, KVH - 1)
    return (groups.reshape(SLOTS).astype(jnp.int32), live.reshape(SLOTS).astype(jnp.float32))

def project(left_operand, right_operand):
    return jnp.einsum('cno,oj->cnj', left_operand, right_operand, precision=top_precision_mode)

def layer(inputs, cosine, sine, params, groups, live):
    attention_gain, query_projection_weight, key_weight, value_weight, query_gain, key_gain, output_weight, feedforward_gain, gate_weight, up_weight, down_projection_weight = params
    seqs = inputs.shape[0]
    scale = 1.0 / math.sqrt(HD)
    first_rms = lax.rsqrt(lax.optimization_barrier(jnp.mean(inputs * inputs, axis=-1, keepdims=True)) + epsilon)
    normed = low(inputs * first_rms * attention_gain)
    queries = low_back(project(normed, query_projection_weight)).reshape(seqs, LEN, SLOTS, HD)
    keys = low_back(project(normed, key_weight)).reshape(seqs, LEN, KVH, HD)
    values = low_back(low(project(normed, value_weight))).reshape(seqs, LEN, KVH, HD)
    turned_queries = low(rotate(head_norm(queries, query_gain), cosine[:, :, None], sine[:, :, None]))
    turned_keys = low(rotate(head_norm(keys, key_gain), cosine[:, :, None], sine[:, :, None]))
    query_heads = jnp.transpose(turned_queries, (0, 2, 1, 3))
    key_heads = jnp.transpose(turned_keys, (0, 2, 1, 3))[:, groups]
    value_heads = jnp.transpose(values, (0, 2, 1, 3))[:, groups]
    blocks = jnp.moveaxis(query_heads.reshape(seqs, SLOTS, NBLK, BLK, HD), 2, 0)
    starts = jnp.arange(NBLK, dtype=jnp.int32) * BLK

    def attend(block_args):
        block, start = block_args
        raw = jnp.einsum('shid,shjd->shij', block, key_heads, precision=top_precision_mode)
        scores = low_back(raw * scale)
        rows = start + jnp.arange(BLK, dtype=jnp.int32)
        cols = jnp.arange(LEN, dtype=jnp.int32)
        allowed = cols[None, :] <= rows[:, None]
        scores = jnp.where(allowed, scores, masked_score)
        peak = lax.optimization_barrier(jnp.max(scores, axis=-1, keepdims=True))
        weights = jnp.exp(scores - peak)
        probs = low(weights / lax.optimization_barrier(jnp.sum(weights, axis=-1, keepdims=True)))
        return jnp.einsum('shij,shjd->shid', probs, value_heads, precision=top_precision_mode)
    mixed = lax.map(jax.checkpoint(attend), (blocks, starts))
    mixed = jnp.moveaxis(mixed, 0, 2).reshape(seqs, SLOTS, LEN, HD)
    mixed = low_back(low(mixed)) * live[None, :, None, None]
    mixed = jnp.transpose(mixed, (0, 2, 1, 3)).reshape(seqs, LEN, SLOTS * HD)
    branch = low_back(project(mixed, output_weight))
    middle = inputs + branch
    second_rms = lax.rsqrt(lax.optimization_barrier(jnp.mean(middle * middle, axis=-1, keepdims=True)) + epsilon)
    normed_two = low(middle * second_rms * feedforward_gain)
    gate = low_back(project(normed_two, gate_weight))
    up = low_back(project(normed_two, up_weight))
    hidden = low(jax.nn.silu(gate) * up)
    return middle + low_back(project(hidden, down_projection_weight))

def reference(hidden_in, positions, head_counts, attention_gain, query_projection_weight, key_weight, value_weight, query_gain, key_gain, output_weight, feedforward_gain, gate_weight, up_weight, down_projection_weight, cotangent):
    groups, live = slot_tables(head_counts)
    params = (attention_gain.astype(jnp.float32), query_projection_weight.astype(jnp.float32), key_weight.astype(jnp.float32), value_weight.astype(jnp.float32), query_gain.astype(jnp.float32), key_gain.astype(jnp.float32), output_weight.astype(jnp.float32), feedforward_gain.astype(jnp.float32), gate_weight.astype(jnp.float32), up_weight.astype(jnp.float32), down_projection_weight.astype(jnp.float32))
    inputs = hidden_in.astype(jnp.float32).reshape(N_DP, SEQ_DEV, LEN, D)
    cosine, sine = rotary_tables(positions.reshape(N_DP, SEQ_DEV, LEN))
    cots = cotangent.astype(jnp.float32).reshape(N_DP, SEQ_DEV, LEN, D)
    zeros = jax.tree.map(jnp.zeros_like, params)

    def step(totals, group_data):
        block_in, block_cos, block_sin, block_cot = group_data

        def forward(values_in, weights):
            return layer(values_in, block_cos, block_sin, weights, groups, live)
        result, pullback = jax.vjp(forward, block_in, params)
        input_grad, weight_grads = pullback(block_cot)
        totals = jax.tree.map(lambda a, b: a + b, totals, weight_grads)
        return (totals, (result, input_grad))
    totals, (results, input_grads) = lax.scan(step, zeros, (inputs, cosine, sine, cots))
    return (results.reshape(TOKENS, D).astype(jnp.bfloat16), input_grads.reshape(TOKENS, D), totals[0], totals[1], totals[2], totals[3], totals[4], totals[5], totals[6], totals[7], totals[8], totals[9], totals[10])
```

```python
import functools
import math

import jax
import jax.numpy as jnp
from jax import lax
from jax.experimental import pallas as pl
from jax.experimental.pallas import tpu as pltpu
from jax.sharding import PartitionSpec as P

D = 2048
QH = 20
KVH = 5
QPG = QH // KVH
HD = 64
LEN = 1024
HALF = LEN // 2

epsilon = 1e-05
rope_base = 10000.0
masked_score = -1e30
low = jnp.bfloat16
full = jnp.float32


def dot(left, right, left_axis, right_axis):
    return lax.dot_general(
        left, right, (((left_axis,), (right_axis,)), ((), ())), preferred_element_type=full
    )


def swap(pieces, axis):
    n = len(pieces)
    return [pieces[0]] + [
        lax.ppermute(pieces[k], axis, [(i, i ^ k) for i in range(n)]) for k in range(1, n)
    ]


def by_rank(blocks, rank):
    bit = 1
    while bit < len(blocks):
        flag = (rank & bit) != 0
        blocks = [jnp.where(flag, blocks[j ^ bit], blocks[j]) for j in range(len(blocks))]
        bit *= 2
    return blocks


def rotary_tables(positions):
    half = HD // 2
    inverse = jnp.exp(-math.log(rope_base) * (2.0 * jnp.arange(half, dtype=full)) / HD)
    angles = inverse[:, None] * positions.astype(full)[None, :]
    cosine, sine = jnp.cos(angles), jnp.sin(angles)
    return jnp.concatenate([cosine, cosine], 0), jnp.concatenate([sine, sine], 0)


def turn(raw, gain, cosine, sine):
    half = HD // 2
    rms = lax.rsqrt(jnp.mean(raw * raw, axis=1, keepdims=True) + epsilon)
    normed = raw * rms * gain[None, :, None]
    turned = jnp.concatenate([-normed[:, half:], normed[:, :half]], axis=1)
    return normed * cosine[None] + turned * sine[None]


def mm(left, right):
    return jnp.dot(left, right, preferred_element_type=full)


def scores_of(key, query, start, first):
    scores = mm(key, query)
    if first is None:
        return scores
    rows = lax.broadcasted_iota(jnp.int32, scores.shape, 0)
    cols = lax.broadcasted_iota(jnp.int32, scores.shape, 1)
    return jnp.where(rows - cols <= start - first, scores, masked_score)


PARTS = (((0, 0),), ((0, None), (HALF, HALF)))


def attend_kernel(starts, q_ref, k_ref, v_ref, o_ref, sums_ref):
    chunk = q_ref.shape[2] // 2
    scale = 1.0 / math.sqrt(HD)
    key = k_ref[0].astype(full).T.astype(low)
    for part, pieces in enumerate(PARTS):
        span = pl.ds(part * chunk, chunk)
        for head in range(QPG):
            query = q_ref[head, :, span] * jnp.asarray(scale, low)
            scores = [
                scores_of(key[at : at + HALF], query, starts[part], first) for at, first in pieces
            ]
            peak = functools.reduce(
                jnp.maximum, [jnp.max(s, axis=0, keepdims=True) for s in scores]
            )
            total = jnp.zeros_like(peak)
            result = jnp.zeros((HD, chunk), full)
            for (at, _), s in zip(pieces, scores):
                weights = jnp.exp(s - peak)
                total += jnp.sum(weights, axis=0, keepdims=True)
                result += mm(v_ref[0, :, at : at + HALF], weights.astype(low))
            o_ref[head, :, span] = (result / total).astype(low)
            sums_ref[0, head : head + 1, span] = peak + jnp.log(total)


def attend_back_kernel(
    starts, q_ref, k_ref, v_ref, g_ref, sums_ref, dq_ref, dk_ref, dv_ref, dk_acc, dv_acc
):
    chunk = q_ref.shape[2] // 2
    scale = 1.0 / math.sqrt(HD)
    key = k_ref[0].astype(full).T.astype(low)
    value = v_ref[0].astype(full).T.astype(low)
    dk_acc[...] = jnp.zeros_like(dk_acc)
    dv_acc[...] = jnp.zeros_like(dv_acc)
    for part, pieces in enumerate(PARTS):
        span = pl.ds(part * chunk, chunk)
        for head in range(QPG):
            query = q_ref[head, :, span] * jnp.asarray(scale, low)
            grad = g_ref[head, :, span]
            query_rows = query.astype(full).T.astype(low)
            grad_rows = grad.astype(full).T.astype(low)
            sums = sums_ref[0, head : head + 1, span]
            delta = jnp.zeros((1, chunk), full)
            kept = []
            for at, first in pieces:
                probs = jnp.exp(
                    scores_of(key[at : at + HALF], query, starts[part], first) - sums
                )
                product = probs * mm(value[at : at + HALF], grad)
                delta += jnp.sum(product, axis=0, keepdims=True)
                kept.append((probs, product))
            dq = jnp.zeros((HD, chunk), full)
            for (at, _), (probs, product) in zip(pieces, kept):
                score_grad = (product - probs * delta).astype(low)
                dq += mm(k_ref[0, :, at : at + HALF], score_grad)
                dk_acc[at : at + HALF, :] += mm(score_grad, query_rows)
                dv_acc[at : at + HALF, :] += mm(probs.astype(low), grad_rows)
            dq_ref[head, :, span] = dq * scale
    dk_ref[0] = dk_acc[...].T
    dv_ref[0] = dv_acc[...].T


def attention_specs(tokens):
    heads = pl.BlockSpec((QPG, HD, tokens), lambda g, s: (g, 0, 0))
    keys = pl.BlockSpec((1, HD, LEN), lambda g, s: (g, 0, 0))
    sums = pl.BlockSpec((1, QPG, tokens), lambda g, s: (g, 0, 0))
    return heads, keys, sums


def attend(starts, queries, keys, values):
    tokens = queries.shape[2]
    heads, whole, sums = attention_specs(tokens)
    pairs = QH * (tokens // 2) * (LEN + HALF)
    return pl.pallas_call(
        attend_kernel,
        out_shape=(
            jax.ShapeDtypeStruct((QH, HD, tokens), low),
            jax.ShapeDtypeStruct((KVH, QPG, tokens), full),
        ),
        grid_spec=pltpu.PrefetchScalarGridSpec(
            num_scalar_prefetch=1,
            grid=(KVH,),
            in_specs=[heads, whole, whole],
            out_specs=[heads, sums],
        ),
        compiler_params=pltpu.CompilerParams(vmem_limit_bytes=40 << 20),
        cost_estimate=pl.CostEstimate(
            flops=pairs * HD * 16, bytes_accessed=8 << 20, transcendentals=pairs
        ),
    )(starts, queries, keys, values)


def attend_back(starts, queries, keys, values, grads, sums_in):
    tokens = queries.shape[2]
    heads, whole, sums = attention_specs(tokens)
    pairs = QH * (tokens // 2) * (LEN + HALF)
    return pl.pallas_call(
        attend_back_kernel,
        out_shape=(
            jax.ShapeDtypeStruct((QH, HD, tokens), full),
            jax.ShapeDtypeStruct((KVH, HD, LEN), full),
            jax.ShapeDtypeStruct((KVH, HD, LEN), full),
        ),
        grid_spec=pltpu.PrefetchScalarGridSpec(
            num_scalar_prefetch=1,
            grid=(KVH,),
            in_specs=[heads, whole, whole, heads, sums],
            out_specs=[heads, whole, whole],
            scratch_shapes=[pltpu.VMEM((LEN, HD), full), pltpu.VMEM((LEN, HD), full)],
        ),
        compiler_params=pltpu.CompilerParams(vmem_limit_bytes=40 << 20),
        cost_estimate=pl.CostEstimate(
            flops=pairs * HD * 40, bytes_accessed=16 << 20, transcendentals=pairs
        ),
    )(starts, queries, keys, values, grads, sums_in)


def norm_backward(values, rms, gain, normed_grad):
    weighted = normed_grad * gain
    dotted = jnp.sum(weighted * values, axis=1, keepdims=True)
    grad = weighted * rms - values * (rms * rms * rms) * dotted / D
    return grad, jnp.sum(normed_grad * values * rms, axis=0)


def on_device(
    hidden_in,
    positions,
    head_counts,
    attention_gain,
    query_projection_weight,
    key_weight,
    value_weight,
    query_gain,
    key_gain,
    output_weight,
    feedforward_gain,
    gate_weight,
    up_weight,
    down_projection_weight,
    cotangent,
):
    groups = lax.axis_size("dp")
    parts = lax.axis_size("mp")
    group = lax.axis_index("dp")
    rank = lax.axis_index("mp")
    tokens, share = hidden_in.shape
    seqs = tokens // LEN
    ring = parts // seqs
    mine = tokens // parts
    chunk = mine // 2
    units = gate_weight.shape[1] // groups
    slots = query_projection_weight.shape[1]
    place = rank % ring
    ranks = range(parts)

    lower = jnp.arange(parts)[None, :] < jnp.arange(parts)[:, None]
    offsets = jnp.sum(jnp.where(lower, head_counts[None, :], 0), axis=1)

    def selection(order):
        within = jnp.arange(slots, dtype=jnp.int32)
        column = offsets[order][:, None] * HD + within[None, :]
        column = jnp.where(within[None, :] < head_counts[order][:, None] * HD, column, -1)
        return (
            column.reshape(-1)[:, None] == jnp.arange(QH * HD, dtype=jnp.int32)[None, :]
        ).astype(low)

    select_near = selection(rank ^ jnp.arange(parts, dtype=jnp.int32))
    select = selection(jnp.arange(parts, dtype=jnp.int32))

    def rows_of(array, other):
        base = (other // ring) * LEN
        at = other % ring
        first = lax.dynamic_slice_in_dim(array, base + at * chunk, chunk, 0)
        last = lax.dynamic_slice_in_dim(array, base + (2 * ring - 1 - at) * chunk, chunk, 0)
        return jnp.concatenate([first, last], 0)

    def to_tokens(array):
        got = swap([rows_of(array, rank ^ k) for k in ranks], "mp")
        return jnp.concatenate(by_rank(got, rank), axis=1)

    def to_features(array, kind):
        array = array.astype(low)
        pieces = by_rank([array[:, j * share : (j + 1) * share] for j in ranks], rank)
        got = by_rank(swap(pieces, "mp"), rank)
        rows = []
        for seq in range(seqs):
            near = got[seq * ring : (seq + 1) * ring]
            rows += [block[:chunk] for block in near]
            rows += [block[chunk:] for block in near[::-1]]
        return jnp.concatenate(rows, 0).astype(kind)

    def everyone(piece):
        return jnp.concatenate(by_rank(swap([piece] * parts, "mp"), rank), axis=0)

    inputs = to_tokens(hidden_in).astype(full)
    gains = everyone(jnp.stack([attention_gain, feedforward_gain], 1)).T
    attention_gain_all, feedforward_gain_all = gains[0], gains[1]

    rows = D // groups
    query_slice = lax.dynamic_slice_in_dim(query_projection_weight, group * rows, rows, 0)
    query_slice = jnp.concatenate(swap([query_slice] * parts, "mp"), axis=1)
    query_slice = mm(query_slice, select_near).astype(low)
    query_all = lax.all_gather(query_slice, "dp", axis=0, tiled=True)
    heads_here = QH * HD // groups
    chosen = lax.dynamic_slice_in_dim(select, group * heads_here, heads_here, 1)
    output_slice = dot(chosen, output_weight, 0, 0).astype(low)
    output_slice = jnp.concatenate(
        by_rank(swap([output_slice] * parts, "mp"), rank), axis=1
    )
    output_all = lax.all_gather(output_slice, "dp", axis=0, tiled=True)

    def near(piece, axis):
        return jnp.concatenate(swap([piece] * parts, "mp"), axis=axis)

    gate_here = near(lax.dynamic_slice_in_dim(gate_weight, group * units, units, 1), 1)
    up_here = near(lax.dynamic_slice_in_dim(up_weight, group * units, units, 1), 1)
    down_here = near(lax.dynamic_slice_in_dim(down_projection_weight, group * units, units, 0), 0)

    cotangent_mine = to_tokens(cotangent)
    cotangent_full = lax.all_gather(cotangent_mine, "dp", axis=0, tiled=True)

    cosine, sine = rotary_tables(rows_of(positions, rank))
    first_rms = lax.rsqrt(jnp.mean(inputs * inputs, axis=1, keepdims=True) + epsilon)
    normed = (inputs * first_rms * attention_gain_all).astype(low)
    keys = dot(key_weight, normed, 0, 1).reshape(KVH, HD, mine)
    values_mine = dot(value_weight, normed, 0, 1).astype(low).reshape(KVH, HD, mine)
    turned_keys, key_pull = jax.vjp(lambda v, g: turn(v, g, cosine, sine), keys, key_gain)
    pair_mine = jnp.concatenate([turned_keys.astype(low), values_mine], 0)

    near_pairs = [pair_mine] + [
        lax.ppermute(pair_mine, "mp", [(i, i ^ k) for i in ranks]) for k in range(1, ring)
    ]
    near_pairs = by_rank(near_pairs, place)
    pair = jnp.concatenate(
        [p[:, :, :chunk] for p in near_pairs] + [p[:, :, chunk:] for p in near_pairs[::-1]], axis=2
    )
    key_heads, value_heads = pair[:KVH], pair[KVH:]

    queries = dot(query_all, normed, 0, 1).reshape(QH, HD, mine)
    turned_queries, query_pull = jax.vjp(
        lambda v, g: turn(v, g, cosine, sine), queries, query_gain
    )
    turned_queries = turned_queries.astype(low)
    starts = jnp.stack([place * chunk, (2 * ring - 1 - place) * chunk]).astype(jnp.int32)
    mixed, row_totals = attend(starts, turned_queries, key_heads, value_heads)
    mixed = mixed.reshape(QH * HD, mine)
    middle = inputs + dot(mixed, output_all, 0, 0)

    second_rms = lax.rsqrt(jnp.mean(middle * middle, axis=1, keepdims=True) + epsilon)
    second_normed = (middle * second_rms * feedforward_gain_all).astype(low)
    second_full = lax.all_gather(second_normed, "dp", axis=0, tiled=True)
    gate = mm(second_full, gate_here)
    up = mm(second_full, up_here)
    sigma = jax.nn.sigmoid(gate)
    swish = gate * sigma
    hidden = (swish * up).astype(low)
    hidden_grad = dot(cotangent_full, down_here, 1, 1)
    gate_grad = (hidden_grad * up * sigma * (1.0 + gate * (1.0 - sigma))).astype(low)
    up_grad = (hidden_grad * swish).astype(low)
    normed_two_terms = dot(gate_grad, gate_here, 1, 1) + dot(up_grad, up_here, 1, 1)
    normed_two_grad = lax.psum_scatter(
        normed_two_terms.astype(low), "dp", scatter_dimension=0, tiled=True
    ).astype(full)
    down_terms = mm(hidden, down_here)
    down_sum = lax.psum_scatter(
        down_terms.astype(low), "dp", scatter_dimension=0, tiled=True
    ).astype(full)
    output = to_features(middle + down_sum, low)

    def reduce_units(grad, axis):
        pieces = [lax.slice_in_dim(grad, k * units, (k + 1) * units, axis=axis) for k in ranks]
        got = swap(pieces, "mp")
        return sum(piece.astype(full) for piece in got).astype(low)

    def columns_back(piece):
        wide = lax.all_gather(piece, "dp", axis=0, tiled=False)
        return jnp.transpose(wide, (1, 0, 2)).reshape(D, -1).astype(full)

    down_grad = reduce_units(dot(hidden, cotangent_full, 0, 0).astype(low), 0)
    down_grad = lax.all_gather(down_grad, "dp", axis=0, tiled=True).astype(full)
    gate_weight_grad = columns_back(reduce_units(dot(second_full, gate_grad, 0, 0).astype(low), 1))
    up_weight_grad = columns_back(reduce_units(dot(second_full, up_grad, 0, 0).astype(low), 1))

    middle_part, feedforward_gain_grad = norm_backward(
        middle, second_rms, feedforward_gain_all, normed_two_grad
    )
    middle_grad = cotangent_mine.astype(full) + middle_part
    branch_grad = middle_grad.astype(low)

    output_grad = mm(mixed, branch_grad).astype(low)
    output_grad = lax.psum_scatter(output_grad, "dp", scatter_dimension=0, tiled=True)
    pieces = by_rank([output_grad[:, j * share : (j + 1) * share] for j in ranks], rank)
    output_grad = sum(piece.astype(full) for piece in swap(pieces, "mp")).astype(low)
    output_grad = lax.all_gather(output_grad, "dp", axis=0, tiled=True)
    output_weight_grad = mm(select, output_grad)

    mixed_grad = dot(output_all, branch_grad, 1, 1).astype(low).reshape(QH, HD, mine)
    query_rot_grad, key_rot_grad, value_grad = attend_back(
        starts, turned_queries, key_heads, value_heads, mixed_grad, row_totals
    )
    queries_low, query_gain_grad = query_pull(query_rot_grad)
    queries_low = queries_low.astype(low).reshape(QH * HD, mine)
    pair_grad = jnp.concatenate([key_rot_grad, value_grad], 0)
    blocks = [
        jnp.concatenate(
            [
                pair_grad[:, :, j * chunk : (j + 1) * chunk],
                pair_grad[:, :, (2 * ring - 1 - j) * chunk : (2 * ring - j) * chunk],
            ],
            axis=2,
        )
        for j in range(ring)
    ]
    blocks = by_rank(blocks, place)
    pair_grad = blocks[0]
    for k in range(1, ring):
        pair_grad += lax.ppermute(
            blocks[k].astype(low), "mp", [(i, i ^ k) for i in ranks]
        ).astype(full)
    keys_grad, key_gain_grad = key_pull(pair_grad[:KVH])
    pair_low = jnp.concatenate(
        [keys_grad.astype(low), pair_grad[KVH:].astype(low)], 0
    ).reshape(2 * KVH * HD, mine)

    query_weight_grad = dot(normed, queries_low, 0, 1).astype(low)
    query_weight_grad = lax.psum_scatter(
        query_weight_grad, "dp", scatter_dimension=0, tiled=True
    )
    query_weight_grad = dot(query_weight_grad, select_near, 1, 1).astype(low)
    pieces = [query_weight_grad[:, k * slots : (k + 1) * slots] for k in ranks]
    query_weight_grad = sum(piece.astype(full) for piece in swap(pieces, "mp")).astype(low)
    query_weight_grad = lax.all_gather(query_weight_grad, "dp", axis=0, tiled=True).astype(full)

    pair_weight_grad = dot(normed, pair_low, 0, 1).astype(low)
    pair_weight_grad = lax.psum_scatter(pair_weight_grad, "dp", scatter_dimension=0, tiled=True)
    pair_weight_grad = sum(
        piece.astype(full) for piece in swap([pair_weight_grad] * parts, "mp")
    ).astype(low)
    pair_weight_grad = lax.all_gather(pair_weight_grad, "dp", axis=0, tiled=True).astype(full)

    normed_grad = (
        dot(queries_low, query_all, 0, 1)
        + dot(pair_low[: KVH * HD], key_weight, 0, 1)
        + dot(pair_low[KVH * HD :], value_weight, 0, 1)
    )
    input_part, attention_gain_grad = norm_backward(
        inputs, first_rms, attention_gain_all, normed_grad
    )
    input_gradient = to_features(middle_grad + input_part, full)

    small = jnp.concatenate(
        [attention_gain_grad, feedforward_gain_grad, query_gain_grad, key_gain_grad]
    )
    small = lax.psum(small, ("dp", "mp"))
    return (
        output,
        input_gradient,
        lax.dynamic_slice_in_dim(small[:D], rank * share, share, 0),
        query_weight_grad,
        pair_weight_grad[:, : KVH * HD],
        pair_weight_grad[:, KVH * HD :],
        small[2 * D : 2 * D + HD],
        small[2 * D + HD :],
        output_weight_grad,
        lax.dynamic_slice_in_dim(small[D : 2 * D], rank * share, share, 0),
        gate_weight_grad,
        up_weight_grad,
        down_grad,
    )


def solution(mesh):
    in_specs = (
        P("dp", "mp"),
        P("dp"),
        P(),
        P("mp"),
        P(None, "mp"),
        P(),
        P(),
        P(),
        P(),
        P(None, "mp"),
        P("mp"),
        P(None, "mp"),
        P(None, "mp"),
        P("mp", None),
        P("dp", "mp"),
    )
    out_specs = (
        P("dp", "mp"),
        P("dp", "mp"),
        P("mp"),
        P(None, "mp"),
        P(),
        P(),
        P(),
        P(),
        P(None, "mp"),
        P("mp"),
        P(None, "mp"),
        P(None, "mp"),
        P("mp", None),
    )
    return jax.shard_map(
        on_device, mesh=mesh, in_specs=in_specs, out_specs=out_specs, check_vma=False
    )
```

```python
import functools
import math

import jax
import jax.numpy as jnp
from jax import lax
from jax.experimental.layout import Layout, with_layout_constraint
from jax.experimental import pallas as pl
from jax.experimental.pallas import tpu as pltpu
from jax.sharding import PartitionSpec as P

D = 2048
QH = 20
KVH = 5
QPG = QH // KVH
HD = 64
LEN = 1024
HALF = LEN // 2

epsilon = 1e-05
rope_base = 10000.0
masked_score = -1e30
low = jnp.bfloat16
full = jnp.float32


def dot(left, right, left_axis, right_axis):
    return lax.dot_general(
        left, right, (((left_axis,), (right_axis,)), ((), ())), preferred_element_type=full
    )


def swap(pieces, axis):
    n = len(pieces)
    return [pieces[0]] + [
        lax.ppermute(pieces[k], axis, [(i, i ^ k) for i in range(n)]) for k in range(1, n)
    ]


def by_rank(blocks, rank):
    bit = 1
    while bit < len(blocks):
        flag = (rank & bit) != 0
        blocks = [jnp.where(flag, blocks[j ^ bit], blocks[j]) for j in range(len(blocks))]
        bit *= 2
    return blocks


def exchange(array, axis, mask, n):
    return lax.ppermute(array, axis, [(i, i ^ mask) for i in range(n)])


def by_rows(array):
    return with_layout_constraint(array, Layout(tuple(range(array.ndim))))


def added(*terms):
    return sum(term.astype(full) for term in terms).astype(low)


class Order:
    def __init__(self, token):
        self.token = token

    def __call__(self, *arrays):
        self.token, *arrays = lax.optimization_barrier((self.token, *arrays))
        return arrays


class RelayGather:
    def __init__(self, piece, axis, n):
        self.axis, self.n, self.step, self.own = axis, n, 1, piece
        self.ups, self.downs = [], []
        self.send(piece, piece)

    def send(self, up, down):
        n, step = self.n, self.step
        right = [(i, i + 1) for i in range(step - 1, n - 1)]
        left = [(i, i - 1) for i in range(n - step, 0, -1)]
        self.flying = [lax.ppermute(up, self.axis, right), lax.ppermute(down, self.axis, left)]

    def take(self, up, down):
        self.ups.append(up)
        self.downs.append(down)
        self.step += 1
        if self.step < self.n:
            self.send(up, down)

    def finish(self, order):
        while self.step < self.n:
            self.take(*order(*self.flying))
        n = self.n
        return [self.own] + [self.ups[k - 1] + self.downs[n - k - 1] for k in range(1, n)]


CUBE = 8


def at_index(array, index):
    return lax.dynamic_index_in_dim(array, index, 0, keepdims=False)


class Spread:
    def __init__(self, piece, axis, n, group):
        self.axis, self.n, self.chip, self.piece = axis, n, group // 2, piece
        if n == CUBE:
            self.flying = [self.move(piece, 2), self.move(piece, 4)]
        else:
            self.flying = [lax.all_gather(piece, axis, axis=0, tiled=True)]
        self.buffer = []

    def move(self, array, mask):
        return exchange(array, self.axis, mask, self.n)

    def second(self, *got):
        self.flying = got
        if self.n == CUBE:
            near, far = got
            half = self.piece.shape[0] // 2
            self.flying = [self.move(near[:half], 4), self.move(far[half:], 2)]
            mine = jnp.zeros((4, *self.piece.shape), self.piece.dtype)
            for k, block in enumerate((self.piece, near, far)):
                mine = lax.dynamic_update_slice(mine, block[None], (self.chip ^ k, 0, 0))
            self.buffer = [mine]

    def third(self, *got):
        if self.n != CUBE:
            self.parts, self.flying = list(got), []
            return
        rows = self.piece.shape[0]
        (mine,) = self.buffer
        for k, block in enumerate(got):
            mine = lax.dynamic_update_slice(
                mine, block[None], (self.chip ^ 3, k * (rows // 2), 0)
            )
        mine = mine.reshape(4 * rows, -1)
        self.parts = [mine]
        self.flying = [self.move(mine, 1)]

    def last(self, *got):
        self.parts += got


class Collect:
    def __init__(self, other, axis, n, group):
        self.axis, self.n, self.chip = axis, n, group // 2
        if n == CUBE:
            self.flying = [self.move(other, 1)]
        else:
            self.flying = [lax.psum_scatter(other, axis, scatter_dimension=0, tiled=True)]

    def move(self, array, mask):
        return exchange(array, self.axis, mask, self.n)

    def second(self, mine, *got, launch=True):
        self.flying = got
        if self.n != CUBE:
            return
        mine = mine.reshape(4, mine.shape[0] // 4, -1)
        got = got[0].reshape(mine.shape)
        half = self.half = mine.shape[1] // 2
        self.sums = added(mine, got)
        block = lambda k: at_index(self.sums, self.chip ^ k)
        self.flying = [
            jnp.concatenate([block(3)[:half], block(1)[:half]], 0),
            jnp.concatenate([block(3)[half:], block(2)[half:]], 0),
        ]
        if launch:
            self.launch(*self.flying)

    def launch(self, *ready):
        self.flying = ready
        if self.n == CUBE:
            self.flying = [self.move(ready[0], 2), self.move(ready[1], 4)]

    def third(self, *got):
        if self.n != CUBE:
            self.flying = got
            return
        half = self.half
        block = lambda k: at_index(self.sums, self.chip ^ k)
        self.direct = [got[0][half:], got[1][half:]]
        self.flying = [
            self.move(added(block(2)[:half], got[0][:half]), 4),
            self.move(added(block(1)[half:], got[1][:half]), 2),
        ]

    def last(self, *got):
        if self.n != CUBE:
            return got[0]
        half = self.half
        own = at_index(self.sums, self.chip)
        return jnp.concatenate(
            [
                added(own[:half], self.direct[0], got[0]),
                added(own[half:], self.direct[1], got[1]),
            ],
            0,
        )


EXTRA = 128


def order_split(order, first, *lists):
    first = list(first)
    got = order(*first, *[array for arrays in lists for array in arrays])
    result, at = list(got[: len(first)]), len(first)
    for arrays in lists:
        result.append(list(got[at : at + len(arrays)]))
        at += len(arrays)
    return result


def rotary_tables(positions):
    half = HD // 2
    inverse = jnp.exp(-math.log(rope_base) * (2.0 * jnp.arange(half, dtype=full)) / HD)
    angles = inverse[:, None] * positions.astype(full)[None, :]
    cosine, sine = jnp.cos(angles), jnp.sin(angles)
    return jnp.concatenate([cosine, cosine], 0), jnp.concatenate([sine, sine], 0)


def turn(raw, gain, cosine, sine):
    half = HD // 2
    rms = lax.rsqrt(jnp.mean(raw * raw, axis=1, keepdims=True) + epsilon)
    normed = raw * rms * gain[None, :, None]
    turned = jnp.concatenate([-normed[:, half:], normed[:, :half]], axis=1)
    return normed * cosine[None] + turned * sine[None]


def mm(left, right):
    return jnp.dot(left, right, preferred_element_type=full)


def scores_of(key, query, start, first):
    scores = mm(key, query)
    if first is None:
        return scores
    rows = lax.broadcasted_iota(jnp.int32, scores.shape, 0)
    cols = lax.broadcasted_iota(jnp.int32, scores.shape, 1)
    return jnp.where(rows - cols <= start - first, scores, masked_score)


PARTS = (((0, 0),), ((0, None), (HALF, HALF)))


def attend_kernel(starts, q_ref, k_ref, v_ref, o_ref, sums_ref):
    chunk = q_ref.shape[2] // 2
    scale = 1.0 / math.sqrt(HD)
    key = k_ref[0].astype(full).T.astype(low)
    for part, pieces in enumerate(PARTS):
        span = pl.ds(part * chunk, chunk)
        for head in range(QPG):
            query = q_ref[head, :, span] * jnp.asarray(scale, low)
            scores = [
                scores_of(key[at : at + HALF], query, starts[part], first) for at, first in pieces
            ]
            peak = functools.reduce(
                jnp.maximum, [jnp.max(s, axis=0, keepdims=True) for s in scores]
            )
            total = jnp.zeros_like(peak)
            result = jnp.zeros((HD, chunk), full)
            for (at, _), s in zip(pieces, scores):
                weights = jnp.exp(s - peak)
                total += jnp.sum(weights, axis=0, keepdims=True)
                result += mm(v_ref[0, :, at : at + HALF], weights.astype(low))
            o_ref[head, :, span] = (result / total).astype(low)
            sums_ref[0, head : head + 1, span] = peak + jnp.log(total)


def attend_back_kernel(
    starts, q_ref, k_ref, v_ref, g_ref, sums_ref, dq_ref, dk_ref, dv_ref, dk_acc, dv_acc
):
    chunk = q_ref.shape[2] // 2
    scale = 1.0 / math.sqrt(HD)
    key = k_ref[0].astype(full).T.astype(low)
    value = v_ref[0].astype(full).T.astype(low)
    dk_acc[...] = jnp.zeros_like(dk_acc)
    dv_acc[...] = jnp.zeros_like(dv_acc)
    for part, pieces in enumerate(PARTS):
        span = pl.ds(part * chunk, chunk)
        for head in range(QPG):
            query = q_ref[head, :, span] * jnp.asarray(scale, low)
            grad = g_ref[head, :, span]
            query_rows = query.astype(full).T.astype(low)
            grad_rows = grad.astype(full).T.astype(low)
            sums = sums_ref[0, head : head + 1, span]
            delta = jnp.zeros((1, chunk), full)
            kept = []
            for at, first in pieces:
                probs = jnp.exp(
                    scores_of(key[at : at + HALF], query, starts[part], first) - sums
                )
                product = probs * mm(value[at : at + HALF], grad)
                delta += jnp.sum(product, axis=0, keepdims=True)
                kept.append((probs, product))
            dq = jnp.zeros((HD, chunk), full)
            for (at, _), (probs, product) in zip(pieces, kept):
                score_grad = (product - probs * delta).astype(low)
                dq += mm(k_ref[0, :, at : at + HALF], score_grad)
                dk_acc[at : at + HALF, :] += mm(score_grad, query_rows)
                dv_acc[at : at + HALF, :] += mm(probs.astype(low), grad_rows)
            dq_ref[head, :, span] = dq * scale
    dk_ref[0] = dk_acc[...].T
    dv_ref[0] = dv_acc[...].T


def attention_specs(tokens):
    heads = pl.BlockSpec((QPG, HD, tokens), lambda g, s: (g, 0, 0))
    keys = pl.BlockSpec((1, HD, LEN), lambda g, s: (g, 0, 0))
    sums = pl.BlockSpec((1, QPG, tokens), lambda g, s: (g, 0, 0))
    return heads, keys, sums


def attend(starts, queries, keys, values):
    tokens = queries.shape[2]
    heads, whole, sums = attention_specs(tokens)
    pairs = QH * (tokens // 2) * (LEN + HALF)
    return pl.pallas_call(
        attend_kernel,
        out_shape=(
            jax.ShapeDtypeStruct((QH, HD, tokens), low),
            jax.ShapeDtypeStruct((KVH, QPG, tokens), full),
        ),
        grid_spec=pltpu.PrefetchScalarGridSpec(
            num_scalar_prefetch=1,
            grid=(KVH,),
            in_specs=[heads, whole, whole],
            out_specs=[heads, sums],
        ),
        compiler_params=pltpu.CompilerParams(vmem_limit_bytes=40 << 20),
        cost_estimate=pl.CostEstimate(
            flops=pairs, bytes_accessed=1 << 20, transcendentals=0
        ),
    )(starts, queries, keys, values)


def attend_back(starts, queries, keys, values, grads, sums_in):
    tokens = queries.shape[2]
    heads, whole, sums = attention_specs(tokens)
    pairs = QH * (tokens // 2) * (LEN + HALF)
    return pl.pallas_call(
        attend_back_kernel,
        out_shape=(
            jax.ShapeDtypeStruct((QH, HD, tokens), full),
            jax.ShapeDtypeStruct((KVH, HD, LEN), full),
            jax.ShapeDtypeStruct((KVH, HD, LEN), full),
        ),
        grid_spec=pltpu.PrefetchScalarGridSpec(
            num_scalar_prefetch=1,
            grid=(KVH,),
            in_specs=[heads, whole, whole, heads, sums],
            out_specs=[heads, whole, whole],
            scratch_shapes=[pltpu.VMEM((LEN, HD), full), pltpu.VMEM((LEN, HD), full)],
        ),
        compiler_params=pltpu.CompilerParams(vmem_limit_bytes=40 << 20),
        cost_estimate=pl.CostEstimate(
            flops=pairs, bytes_accessed=1 << 20, transcendentals=0
        ),
    )(starts, queries, keys, values, grads, sums_in)


def widen_kernel(wide_ref, down_ref, gate_out, up_out, down_out):
    units = gate_out.shape[1]
    gate_out[...] = wide_ref[0, :, :units].astype(full)
    up_out[...] = wide_ref[0, :, units:].astype(full)
    down_out[...] = down_ref[...].astype(full)


def widen(wide, down):
    groups, rows, columns = wide.shape
    units = columns // 2
    if units % 128:
        pairs = jnp.transpose(wide, (1, 0, 2)).reshape(rows, groups, 2, units).astype(full)
        gate, up = (pairs[:, :, k].reshape(rows, -1) for k in range(2))
        return gate, up, down.astype(full)
    shape = jax.ShapeDtypeStruct((rows, groups * units), full)
    column = pl.BlockSpec((rows, units), lambda g: (0, g))
    return pl.pallas_call(
        widen_kernel,
        out_shape=(shape, shape, jax.ShapeDtypeStruct(down.shape, full)),
        grid=(groups,),
        in_specs=[
            pl.BlockSpec((1, rows, columns), lambda g: (g, 0, 0)),
            pl.BlockSpec((units, down.shape[1]), lambda g: (g, 0)),
        ],
        out_specs=[column, column, pl.BlockSpec((units, down.shape[1]), lambda g: (g, 0))],
        compiler_params=pltpu.CompilerParams(vmem_limit_bytes=32 << 20),
        cost_estimate=pl.CostEstimate(flops=0, bytes_accessed=1 << 16, transcendentals=0),
    )(wide, down)


def norm_backward(values, rms, gain, normed_grad):
    weighted = normed_grad * gain
    dotted = jnp.sum(weighted * values, axis=1, keepdims=True)
    grad = weighted * rms - values * (rms * rms * rms) * dotted / D
    return grad, jnp.sum(normed_grad * values * rms, axis=0)


def on_device(
    hidden_in,
    positions,
    head_counts,
    attention_gain,
    query_projection_weight,
    key_weight,
    value_weight,
    query_gain,
    key_gain,
    output_weight,
    feedforward_gain,
    gate_weight,
    up_weight,
    down_projection_weight,
    cotangent,
):
    groups = lax.axis_size("dp")
    parts = lax.axis_size("mp")
    group = lax.axis_index("dp")
    rank = lax.axis_index("mp")
    tokens, share = hidden_in.shape
    seqs = tokens // LEN
    ring = parts // seqs
    mine = tokens // parts
    chunk = mine // 2
    units = gate_weight.shape[1] // groups
    slots = query_projection_weight.shape[1]
    place = rank % ring
    ranks = range(parts)

    lower = jnp.arange(parts)[None, :] < jnp.arange(parts)[:, None]
    offsets = jnp.sum(jnp.where(lower, head_counts[None, :], 0), axis=1)

    def selection(order):
        within = jnp.arange(slots, dtype=jnp.int32)
        column = offsets[order][:, None] * HD + within[None, :]
        column = jnp.where(within[None, :] < head_counts[order][:, None] * HD, column, -1)
        return (
            column.reshape(-1)[:, None] == jnp.arange(QH * HD, dtype=jnp.int32)[None, :]
        ).astype(low)

    select_near = selection(rank ^ jnp.arange(parts, dtype=jnp.int32))
    select = selection(jnp.arange(parts, dtype=jnp.int32))

    def rows_of(array, other):
        base = (other // ring) * LEN
        at = other % ring
        first = lax.dynamic_slice_in_dim(array, base + at * chunk, chunk, 0)
        last = lax.dynamic_slice_in_dim(array, base + (2 * ring - 1 - at) * chunk, chunk, 0)
        return jnp.concatenate([first, last], 0)

    order = Order(head_counts)
    rows = D // groups
    heads_here = QH * HD // groups

    query_slice = lax.dynamic_slice_in_dim(query_projection_weight, group * rows, rows, 0)
    gains = jnp.stack([attention_gain, feedforward_gain])
    gains_high = gains.astype(low)
    gains_low = (gains - gains_high.astype(full)).astype(low)
    lines = -(-share // slots)
    gains = jnp.pad(
        jnp.concatenate([gains_high, gains_low], 0), ((0, 0), (0, lines * slots - share))
    )
    query_slice = jnp.concatenate([query_slice, gains.reshape(4 * lines, slots)], 0)
    query_slice = swap([query_slice] * parts, "mp")
    cosine, sine = rotary_tables(rows_of(positions, rank))
    chosen = lax.dynamic_slice_in_dim(select, group * heads_here, heads_here, 1)
    output_slice = dot(chosen, output_weight, 0, 0).astype(low)
    pack = jnp.concatenate(
        [
            lax.dynamic_slice_in_dim(gate_weight, group * units, units, 1),
            lax.dynamic_slice_in_dim(up_weight, group * units, units, 1),
            lax.dynamic_slice_in_dim(down_projection_weight, group * units, units, 0).T,
        ],
        1,
    )
    inputs = [rows_of(hidden_in, rank ^ k) for k in ranks]
    late = inputs[parts - 1]
    inputs = inputs[:1] + [exchange(inputs[k], "mp", k, parts) for k in range(1, parts - 1)]
    cotangent = [rows_of(cotangent, rank ^ k) for k in ranks]
    got = order(
        select_near, select, late, cosine, sine, output_slice, pack,
        *query_slice, *cotangent, *inputs
    )
    select_near, select, late, cosine, sine, output_slice, pack = got[:7]
    query_slice, cotangent = (got[7 + k * parts : 7 + (k + 1) * parts] for k in range(2))
    inputs = got[7 + 2 * parts :]

    inputs.append(exchange(late, "mp", parts - 1, parts))
    output_slice = swap([output_slice] * parts, "mp")
    gains = by_rank([piece[rows:].reshape(4, -1)[:, :share] for piece in query_slice], rank)
    gains = jnp.concatenate(gains, 1).astype(full)
    attention_gain_all, feedforward_gain_all = gains[0] + gains[2], gains[1] + gains[3]
    query_slice = jnp.concatenate([piece[:rows] for piece in query_slice], axis=1)
    query_slice = mm(query_slice, select_near).astype(low)
    query_all = lax.all_gather(query_slice, "dp", axis=0, tiled=True)
    got = order(*inputs, *output_slice)
    inputs, output_slice = got[:parts], got[parts:]

    inputs = jnp.concatenate(by_rank(inputs, rank), axis=1).astype(full)
    first_rms = lax.rsqrt(jnp.mean(inputs * inputs, axis=1, keepdims=True) + epsilon)
    normed = (inputs * first_rms * attention_gain_all).astype(low)
    keys = dot(key_weight, normed, 0, 1).reshape(KVH, HD, mine)
    values_mine = dot(value_weight, normed, 0, 1).astype(low).reshape(KVH, HD, mine)
    turned_keys, key_pull = jax.vjp(lambda v, g: turn(v, g, cosine, sine), keys, key_gain)
    pair_mine = jnp.concatenate([turned_keys.astype(low), values_mine], 0)
    pair_mine, normed = order(pair_mine, normed)

    near_pairs = [pair_mine] + [exchange(pair_mine, "mp", k, parts) for k in range(1, ring)]
    output_slice = jnp.concatenate(by_rank(output_slice, rank), axis=1)
    output_all = lax.all_gather(output_slice, "dp", axis=0, tiled=True)
    queries = dot(query_all, normed, 0, 1).reshape(QH, HD, mine)
    turned_queries, query_pull = jax.vjp(
        lambda v, g: turn(v, g, cosine, sine), queries, query_gain
    )
    got = order(turned_queries.astype(low), *near_pairs, *cotangent)
    turned_queries, near_pairs, cotangent = got[0], got[1 : ring + 1], got[ring + 1 :]

    cotangent = swap(cotangent, "mp")
    near_pairs = by_rank(near_pairs, place)
    pair = jnp.concatenate(
        [p[:, :, :chunk] for p in near_pairs] + [p[:, :, chunk:] for p in near_pairs[::-1]], axis=2
    )
    key_heads, value_heads = pair[:KVH], pair[KVH:]
    starts = jnp.stack([place * chunk, (2 * ring - 1 - place) * chunk]).astype(jnp.int32)
    mixed, row_totals = attend(starts, turned_queries, key_heads, value_heads)
    mixed = mixed.reshape(QH * HD, mine)
    middle = inputs + dot(mixed, output_all, 0, 0)
    second_rms = lax.rsqrt(jnp.mean(middle * middle, axis=1, keepdims=True) + epsilon)
    second_normed = (middle * second_rms * feedforward_gain_all).astype(low)
    second_normed, pack, *cotangent = order(second_normed, pack, *cotangent)

    second = Spread(second_normed, "dp", groups, group)
    weights = RelayGather(pack, "mp", parts)
    cotangent_mine = jnp.concatenate(by_rank(cotangent, rank), axis=1)
    cube = groups == CUBE
    if cube:
        flag = group % 2 != 0
        pairs = [normed[:, k * rows : (k + 1) * rows] for k in range(groups)]
        normed_own, normed_other = (
            jnp.concatenate(
                [jnp.where(flag, pairs[k ^ 1 ^ a], pairs[k ^ a]) for k in range(0, groups, 2)], 1
            )
            for a in (0, 1)
        )
    else:
        normed_own = normed_other = normed
    *got, up, down, cotangent_mine, normed_own, normed_other = order(
        *second.flying, *weights.flying, cotangent_mine, normed_own, normed_other
    )
    second.second(*got)
    weights.take(up, down)
    cotangent_mine, got, (up, down), second.buffer = order_split(
        order, [cotangent_mine], second.flying, weights.flying, second.buffer
    )
    cotangent_full = lax.all_gather(cotangent_mine, "dp", axis=0, tiled=True)
    second.third(*got)
    weights.take(up, down)
    got, (up, down) = order_split(order, [], second.flying, weights.flying)
    second.last(*got)
    weights.take(up, down)
    pack = weights.finish(order)
    wide = jnp.concatenate(
        [block[:, :units] for block in pack] + [block[:, units : 2 * units] for block in pack], 1
    )
    down_here = jnp.concatenate([block[:, 2 * units :] for block in pack], 1)
    half = parts * units

    raised = [mm(part, wide) for part in second.parts]
    hidden = [
        (v[:, :half] * jax.nn.sigmoid(v[:, :half]) * v[:, half:]).astype(low) for v in raised
    ]
    down_terms = [dot(h, down_here, 1, 1).astype(low) for h in hidden]
    down_terms, raised, hidden, (cotangent_full,) = order_split(
        order, [], down_terms, raised, hidden, [cotangent_full]
    )
    def cores(array, at):
        if not cube:
            return array
        array = array.reshape(4, 2, mine, D)
        return lax.dynamic_index_in_dim(array, at, 1, keepdims=False).reshape(4 * mine, D)

    cot = [cores(cotangent_full, at) for at in ((group % 2, 1 - group % 2) if cube else (0,))]

    def back(part, v):
        hidden_grad = mm(part, down_here)
        gate, up = v[:, :half], v[:, half:]
        sigma = jax.nn.sigmoid(gate)
        gate_grad = hidden_grad * up * sigma * (1.0 + gate * (1.0 - sigma))
        return jnp.concatenate([gate_grad.astype(low), (hidden_grad * gate * sigma).astype(low)], 1)

    grads = [back(cot[-1], raised[-1])]
    other = dot(grads[0], wide, 1, 1).astype(low)
    other, grads[0], *raised = order(other, grads[0], *raised)

    second_sum = Collect(other, "dp", groups, group)
    own = other
    if len(raised) > 1:
        grads.insert(0, back(cot[0], raised[0]))
        own = dot(grads[0], wide, 1, 1).astype(low)
    own, *grads, hidden, got = order_split(order, [own, *grads], hidden, second_sum.flying)

    second_sum.second(own, *got)
    wide_grad = sum(dot(part, grad, 0, 0) for part, grad in zip(second.parts, grads)).astype(low)
    down_grad = sum(dot(part, h, 0, 0) for part, h in zip(cot, hidden)).astype(low)
    down_sum = Collect(down_terms[-1], "dp", groups, group)
    down_grad, wide_grad, got, flying = order_split(
        order, [down_grad, wide_grad], second_sum.flying, down_sum.flying
    )

    second_sum.third(*got)

    def block_of(k):
        at = k * units
        return jnp.concatenate(
            [
                wide_grad[:, at : at + units],
                wide_grad[:, half + at : half + at + units],
                down_grad[:, at : at + units],
            ],
            1,
        )

    pack = jnp.zeros((parts, D, 3 * units), low)
    for k in ranks:
        pack = lax.dynamic_update_slice(
            pack, block_of(k)[None], ((rank - k) % parts, 0, 0)
        )
    pack = lax.psum_scatter(pack, "mp", scatter_dimension=0, tiled=False)
    down_sum.second(down_terms[0], *flying, launch=False)
    *got, flying = order_split(order, second_sum.flying, down_sum.flying)

    normed_two_grad = second_sum.last(*got).astype(full)
    down_sum.launch(*flying)
    middle_part, feedforward_gain_grad = norm_backward(
        middle, second_rms, feedforward_gain_all, normed_two_grad
    )
    middle_grad = cotangent_mine.astype(full) + middle_part
    lane = lax.broadcasted_iota(jnp.int32, (D, EXTRA), 1)
    wide_extra = jnp.where(lane == 0, feedforward_gain_grad[:, None], 0.0)
    branch_grad = middle_grad.astype(low)
    mixed_grad = dot(output_all, branch_grad, 1, 1).astype(low).reshape(QH, HD, mine)
    output_grad = mm(mixed, branch_grad).astype(low)
    query_rot_grad, key_rot_grad, value_grad = attend_back(
        starts, turned_queries, key_heads, value_heads, mixed_grad, row_totals
    )
    pair_grad = jnp.concatenate([key_rot_grad, value_grad], 0)
    blocks = [
        jnp.concatenate(
            [
                pair_grad[:, :, j * chunk : (j + 1) * chunk],
                pair_grad[:, :, (2 * ring - 1 - j) * chunk : (2 * ring - j) * chunk],
            ],
            axis=2,
        )
        for j in range(ring)
    ]
    blocks = by_rank(blocks, place)
    away = [block.astype(low) for block in blocks[1:]]
    query_rot_grad, *away, got = order_split(
        order, [query_rot_grad, *away], down_sum.flying
    )
    down_sum.third(*got)

    away = [exchange(block, "mp", k + 1, parts) for k, block in enumerate(away)]
    queries_low, query_gain_grad = query_pull(query_rot_grad)
    queries_low = queries_low.astype(low).reshape(QH * HD, mine)
    queries_low, pack, output_grad, wide_extra, *away, got = order_split(
        order, [queries_low, pack, output_grad, wide_extra, *away], down_sum.flying
    )
    down_total = down_sum.last(*got)
    output_grad = lax.psum_scatter(output_grad, "dp", scatter_dimension=0, tiled=True)
    pack = by_rows(pack)
    wide_grad = by_rows(lax.all_gather(by_rows(pack[:, : 2 * units]), "dp", axis=0, tiled=False))
    down_grad = by_rows(
        lax.all_gather(by_rows(pack[:, 2 * units :].T), "dp", axis=0, tiled=True)
    )
    pair_grad = sum([blocks[0]] + [block.astype(full) for block in away])
    keys_grad, key_gain_grad = key_pull(pair_grad[:KVH])
    pair_low = jnp.concatenate(
        [keys_grad.astype(low), pair_grad[KVH:].astype(low)], 0
    ).reshape(2 * KVH * HD, mine)
    all_low = jnp.concatenate([queries_low, pair_low], 0)
    heads_gain = jnp.stack([query_gain_grad, key_gain_grad])
    top = wide_extra[:2] + jnp.pad(heads_gain, ((0, 0), (EXTRA - HD, 0)))
    extra = jnp.concatenate([top, wide_extra[2:]], 0)
    wide_low = jnp.concatenate([all_low, jnp.zeros((EXTRA, mine), low)], 0)

    def projections(normed_part, extra_part):
        extra_part = jnp.pad(extra_part, ((0, 0), (wide_low.shape[0] - EXTRA, 0)))
        return (dot(normed_part, wide_low, 0, 1) + extra_part).astype(low)

    own = other = extra
    if cube:
        pairs = extra.reshape(4, 2, rows, EXTRA)
        own, other = (
            lax.dynamic_index_in_dim(pairs, at, 1, keepdims=False).reshape(4 * rows, EXTRA)
            for at in (group % 2, 1 - group % 2)
        )
    other = projections(normed_other, other)
    output = [(middle + down_total.astype(full)).astype(low)]
    other, own, wide_low, all_low, normed_own, *output = order(
        other, own, wide_low, all_low, normed_own, *output
    )
    output = by_rank([output[0][:, j * share : (j + 1) * share] for j in ranks], rank)

    def by_feature(array):
        return by_rank([array[:, j * share : (j + 1) * share] for j in ranks], rank)

    projection_sum = Collect(other, "dp", groups, group)
    output = swap(output, "mp")
    own = projections(normed_own, own) if cube else other
    queries_low, pair_low = all_low[: QH * HD], all_low[QH * HD :]
    normed_grad = (
        dot(queries_low, query_all, 0, 1)
        + dot(pair_low[: KVH * HD], key_weight, 0, 1)
        + dot(pair_low[KVH * HD :], value_weight, 0, 1)
    )
    input_part, _ = norm_backward(
        inputs, first_rms, attention_gain_all, normed_grad
    )
    input_gradient = (middle_grad + input_part).astype(low)
    input_gradient, own, got, output = order_split(
        order, [input_gradient, own], projection_sum.flying, output
    )
    projection_sum.second(own, *got)

    def by_tokens(got, kind):
        got = by_rank(got, rank)
        rows = []
        for seq in range(seqs):
            near = got[seq * ring : (seq + 1) * ring]
            rows += [block[:chunk] for block in near]
            rows += [block[chunk:] for block in near[::-1]]
        return jnp.concatenate(rows, 0).astype(kind)

    output_grad = swap(by_feature(output_grad), "mp")
    output_grad, got = order_split(order, [], output_grad, projection_sum.flying)
    output_grad = lax.all_gather(added(*output_grad), "dp", axis=0, tiled=True)
    projection_sum.third(*got)

    got = order(*projection_sum.flying, input_gradient)
    projection_total, input_gradient = projection_sum.last(*got[:-1]), got[-1]

    query_total, pair_total, extra = jnp.split(
        projection_total, [QH * HD, (QH + 2 * KVH) * HD], axis=1
    )
    here = lambda weight: lax.dynamic_slice_in_dim(weight, group * rows, rows, 0).astype(full)
    product = jnp.sum(here(query_all) * query_total.astype(full), axis=1)
    product += jnp.sum(here(key_weight) * pair_total[:, : KVH * HD].astype(full), axis=1)
    product += jnp.sum(here(value_weight) * pair_total[:, KVH * HD :].astype(full), axis=1)
    product = product / lax.dynamic_slice_in_dim(attention_gain_all, group * rows, rows, 0)
    column = lax.broadcasted_iota(jnp.int32, extra.shape, 1)
    extra = jnp.where(column == 2, product[:, None].astype(low), extra)
    query_part = dot(query_total, select_near, 1, 1).astype(low)
    projection = swap(
        [
            jnp.concatenate([query_part[:, k * slots : (k + 1) * slots], pair_total, extra], 1)
            for k in ranks
        ],
        "mp",
    )
    *projection, wide_grad, down_grad, input_gradient, output_grad = order(
        *projection, wide_grad, down_grad, input_gradient, output_grad
    )

    projection = lax.all_gather(added(*projection), "dp", axis=0, tiled=True)
    output_weight_grad = mm(select, output_grad)
    input_gradient = swap(by_feature(input_gradient), "mp")
    gate_weight_grad, up_weight_grad, down_weight_grad = widen(wide_grad, down_grad)
    output = by_tokens(output, low)
    got = order(
        projection, gate_weight_grad, up_weight_grad, down_weight_grad, output,
        output_weight_grad, *input_gradient
    )
    projection, gate_weight_grad, up_weight_grad, down_weight_grad, output = got[:5]
    output_weight_grad = got[5]
    input_gradient = by_tokens(got[6:], full)

    widths = [slots, KVH * HD, KVH * HD, EXTRA]
    cuts = [sum(widths[: k + 1]) for k in range(3)]
    query_weight_grad, key_weight_grad, value_weight_grad, extra = jnp.split(
        projection, cuts, axis=1
    )
    extra = extra.astype(full)
    own_share = lax.dynamic_slice_in_dim(extra, rank * share, share, 0)
    return (
        output,
        input_gradient,
        own_share[:, 2],
        query_weight_grad.astype(full),
        key_weight_grad.astype(full),
        value_weight_grad.astype(full),
        extra[0, EXTRA - HD :],
        extra[1, EXTRA - HD :],
        output_weight_grad,
        own_share[:, 0],
        gate_weight_grad,
        up_weight_grad,
        down_weight_grad,
    )


def solution(mesh):
    in_specs = (
        P("dp", "mp"),
        P("dp"),
        P(),
        P("mp"),
        P(None, "mp"),
        P(),
        P(),
        P(),
        P(),
        P(None, "mp"),
        P("mp"),
        P(None, "mp"),
        P(None, "mp"),
        P("mp", None),
        P("dp", "mp"),
    )
    out_specs = (
        P("dp", "mp"),
        P("dp", "mp"),
        P("mp"),
        P(None, "mp"),
        P(),
        P(),
        P(),
        P(),
        P(None, "mp"),
        P("mp"),
        P(None, "mp"),
        P(None, "mp"),
        P("mp", None),
    )
    return jax.shard_map(
        on_device, mesh=mesh, in_specs=in_specs, out_specs=out_specs, check_vma=False
    )
```

```python
import functools
import math

import jax
import jax.numpy as jnp
from jax import lax
from jax.experimental.layout import Layout, with_layout_constraint
from jax.experimental import pallas as pl
from jax.experimental.pallas import tpu as pltpu
from jax.sharding import PartitionSpec as P

D = 2048
QH = 20
KVH = 5
QPG = QH // KVH
HD = 64
LEN = 1024
HALF = LEN // 2

epsilon = 1e-05
rope_base = 10000.0
masked_score = -1e30
low = jnp.bfloat16
full = jnp.float32


def dot(left, right, left_axis, right_axis):
    return lax.dot_general(
        left, right, (((left_axis,), (right_axis,)), ((), ())), preferred_element_type=full
    )


def swap(pieces, axis):
    n = len(pieces)
    return [pieces[0]] + [
        lax.ppermute(pieces[k], axis, [(i, i ^ k) for i in range(n)]) for k in range(1, n)
    ]


def by_rank(blocks, rank):
    bit = 1
    while bit < len(blocks):
        flag = (rank & bit) != 0
        blocks = [jnp.where(flag, blocks[j ^ bit], blocks[j]) for j in range(len(blocks))]
        bit *= 2
    return blocks


def exchange(array, axis, mask, n):
    return lax.ppermute(array, axis, [(i, i ^ mask) for i in range(n)])


def by_rows(array):
    return with_layout_constraint(array, Layout(tuple(range(array.ndim))))


def added(*terms):
    return sum(term.astype(full) for term in terms).astype(low)


class Order:
    def __init__(self, token):
        self.token = token

    def __call__(self, *arrays):
        self.token, *arrays = lax.optimization_barrier((self.token, *arrays))
        return arrays


class RelayGather:
    def __init__(self, piece, axis, n):
        self.axis, self.n, self.step, self.own = axis, n, 1, piece
        self.ups, self.downs = [], []
        self.send(piece, piece)

    def send(self, up, down):
        n, step = self.n, self.step
        right = [(i, i + 1) for i in range(step - 1, n - 1)]
        left = [(i, i - 1) for i in range(n - step, 0, -1)]
        self.flying = [lax.ppermute(up, self.axis, right), lax.ppermute(down, self.axis, left)]

    def take(self, up, down):
        self.ups.append(up)
        self.downs.append(down)
        self.step += 1
        if self.step < self.n:
            self.send(up, down)

    def finish(self, order):
        while self.step < self.n:
            self.take(*order(*self.flying))
        n = self.n
        return [self.own] + [self.ups[k - 1] + self.downs[n - k - 1] for k in range(1, n)]


CUBE = 8


def at_index(array, index):
    return lax.dynamic_index_in_dim(array, index, 0, keepdims=False)


class Spread:
    def __init__(self, piece, axis, n, group):
        self.axis, self.n, self.chip, self.piece = axis, n, group // 2, piece
        if n == CUBE:
            self.flying = [self.move(piece, 2), self.move(piece, 4)]
        else:
            self.flying = [lax.all_gather(piece, axis, axis=0, tiled=True)]
        self.buffer = []

    def move(self, array, mask):
        return exchange(array, self.axis, mask, self.n)

    def second(self, *got):
        self.flying = got
        if self.n == CUBE:
            near, far = got
            half = self.piece.shape[0] // 2
            self.flying = [self.move(near[:half], 4), self.move(far[half:], 2)]
            mine = jnp.zeros((4, *self.piece.shape), self.piece.dtype)
            for k, block in enumerate((self.piece, near, far)):
                mine = lax.dynamic_update_slice(mine, block[None], (self.chip ^ k, 0, 0))
            self.buffer = [mine]

    def third(self, *got):
        if self.n != CUBE:
            self.parts, self.flying = list(got), []
            return
        rows = self.piece.shape[0]
        (mine,) = self.buffer
        for k, block in enumerate(got):
            mine = lax.dynamic_update_slice(
                mine, block[None], (self.chip ^ 3, k * (rows // 2), 0)
            )
        mine = mine.reshape(4 * rows, -1)
        self.parts = [mine]
        self.flying = [self.move(mine, 1)]

    def last(self, *got):
        self.parts += got


TOGETHER = (((3, 0), (1, 0)), ((3, 1), (2, 1)), ((0, 0), (0, 1), (2, 0), (1, 1)))
APART = (((3, 0),), ((3, 1),), ((1, 0),), ((2, 1),), ((0, 0), (0, 1), (2, 0), (1, 1)))


def chip_sums(mine, got, chip, plan):
    half, columns = mine.shape[0] // 8, mine.shape[1]
    flat = [place for places in plan for place in places]
    index = jnp.stack([(chip ^ block) * 2 + part for block, part in flat]).astype(jnp.int32)
    firsts = [sum(len(places) for places in plan[:k]) for k in range(len(plan))]

    def kernel(index_ref, mine_ref, got_ref, *outs):
        step = pl.program_id(0)
        total = (mine_ref[...].astype(full) + got_ref[...].astype(full)).astype(low)
        for first, places, out in zip(firsts, plan, outs):

            @pl.when((step >= first) & (step < first + len(places)))
            def _():
                out[...] = total

    source = pl.BlockSpec((half, columns), lambda g, index: (index[g], 0))

    def target(first, count):
        return pl.BlockSpec(
            (half, columns), lambda g, index: (jnp.clip(g - first, 0, count - 1), 0)
        )

    return pl.pallas_call(
        kernel,
        out_shape=[
            jax.ShapeDtypeStruct((len(places) * half, columns), low) for places in plan
        ],
        grid_spec=pltpu.PrefetchScalarGridSpec(
            num_scalar_prefetch=1,
            grid=(len(flat),),
            in_specs=[source, source],
            out_specs=[target(f, len(places)) for f, places in zip(firsts, plan)],
        ),
        compiler_params=pltpu.CompilerParams(vmem_limit_bytes=40 << 20),
        cost_estimate=pl.CostEstimate(flops=0, bytes_accessed=1 << 16, transcendentals=0),
    )(index, mine, got)


class Collect:
    def __init__(self, other, axis, n, group):
        self.axis, self.n, self.chip = axis, n, group // 2
        if n == CUBE:
            self.flying = [self.move(other, 1)]
        else:
            self.flying = [lax.psum_scatter(other, axis, scatter_dimension=0, tiled=True)]

    def move(self, array, mask):
        return exchange(array, self.axis, mask, self.n)

    def second(self, mine, *got, apart=False):
        self.flying, self.held = got, []
        if self.n != CUBE:
            return
        self.half = mine.shape[0] // 8
        *sent, self.keep = chip_sums(mine, got[0], self.chip, APART if apart else TOGETHER)
        self.apart = apart
        if apart:
            self.flying, self.held = sent[:2], sent[2:]
        else:
            self.launch(*sent)

    def launch(self, *ready):
        self.flying = ready
        if self.n == CUBE:
            self.flying = [self.move(ready[0], 2), self.move(ready[1], 4)]

    def third(self, *got):
        self.flying = got
        if self.n != CUBE:
            return
        half = self.half
        if not self.apart:
            self.direct = [got[0][half:], got[1][half:]]
        self.flying = [
            self.move(added(self.keep[2 * half : 3 * half], got[0][:half]), 4),
            self.move(added(self.keep[3 * half :], got[1][:half]), 2),
        ]

    def fourth(self, *got):
        self.flying = got
        if self.n == CUBE:
            self.relayed = got
            self.flying = [self.move(self.held[0], 2), self.move(self.held[1], 4)]

    def last(self, *got):
        if self.n != CUBE:
            return got[0]
        half = self.half
        direct, got = (got, self.relayed) if self.apart else (self.direct, got)
        return jnp.concatenate(
            [
                added(self.keep[:half], direct[0], got[0]),
                added(self.keep[half : 2 * half], direct[1], got[1]),
            ],
            0,
        )


EXTRA = 128


def order_split(order, first, *lists):
    first = list(first)
    got = order(*first, *[array for arrays in lists for array in arrays])
    result, at = list(got[: len(first)]), len(first)
    for arrays in lists:
        result.append(list(got[at : at + len(arrays)]))
        at += len(arrays)
    return result


def rotary_tables(positions):
    half = HD // 2
    inverse = jnp.exp(-math.log(rope_base) * (2.0 * jnp.arange(half, dtype=full)) / HD)
    angles = inverse[:, None] * positions.astype(full)[None, :]
    cosine, sine = jnp.cos(angles), jnp.sin(angles)
    return jnp.concatenate([cosine, cosine], 0), jnp.concatenate([sine, sine], 0)


def turn(raw, gain, cosine, sine):
    half = HD // 2
    rms = lax.rsqrt(jnp.mean(raw * raw, axis=1, keepdims=True) + epsilon)
    normed = raw * rms * gain[None, :, None]
    turned = jnp.concatenate([-normed[:, half:], normed[:, :half]], axis=1)
    return normed * cosine[None] + turned * sine[None]


def mm(left, right):
    return jnp.dot(left, right, preferred_element_type=full)


def scores_of(key, query, start, first):
    scores = mm(key, query)
    if first is None:
        return scores
    rows = lax.broadcasted_iota(jnp.int32, scores.shape, 0)
    cols = lax.broadcasted_iota(jnp.int32, scores.shape, 1)
    return jnp.where(rows - cols <= start - first, scores, masked_score)


PARTS = (((0, 0),), ((0, None), (HALF, HALF)))


def attend_kernel(starts, q_ref, k_ref, v_ref, o_ref, sums_ref):
    chunk = q_ref.shape[2] // 2
    scale = 1.0 / math.sqrt(HD)
    key = k_ref[0].astype(full).T.astype(low)
    for part, pieces in enumerate(PARTS):
        span = pl.ds(part * chunk, chunk)
        for head in range(QPG):
            query = q_ref[head, :, span] * jnp.asarray(scale, low)
            scores = [
                scores_of(key[at : at + HALF], query, starts[part], first) for at, first in pieces
            ]
            peak = functools.reduce(
                jnp.maximum, [jnp.max(s, axis=0, keepdims=True) for s in scores]
            )
            total = jnp.zeros_like(peak)
            result = jnp.zeros((HD, chunk), full)
            for (at, _), s in zip(pieces, scores):
                weights = jnp.exp(s - peak)
                total += jnp.sum(weights, axis=0, keepdims=True)
                result += mm(v_ref[0, :, at : at + HALF], weights.astype(low))
            o_ref[head, :, span] = (result / total).astype(low)
            sums_ref[0, head : head + 1, span] = peak + jnp.log(total)


def attend_back_kernel(
    starts, q_ref, k_ref, v_ref, g_ref, sums_ref, dq_ref, dk_ref, dv_ref, dk_acc, dv_acc
):
    chunk = q_ref.shape[2] // 2
    scale = 1.0 / math.sqrt(HD)
    key = k_ref[0].astype(full).T.astype(low)
    value = v_ref[0].astype(full).T.astype(low)
    dk_acc[...] = jnp.zeros_like(dk_acc)
    dv_acc[...] = jnp.zeros_like(dv_acc)
    for part, pieces in enumerate(PARTS):
        span = pl.ds(part * chunk, chunk)
        for head in range(QPG):
            query = q_ref[head, :, span] * jnp.asarray(scale, low)
            grad = g_ref[head, :, span]
            query_rows = query.astype(full).T.astype(low)
            grad_rows = grad.astype(full).T.astype(low)
            sums = sums_ref[0, head : head + 1, span]
            delta = jnp.zeros((1, chunk), full)
            kept = []
            for at, first in pieces:
                probs = jnp.exp(
                    scores_of(key[at : at + HALF], query, starts[part], first) - sums
                )
                product = probs * mm(value[at : at + HALF], grad)
                delta += jnp.sum(product, axis=0, keepdims=True)
                kept.append((probs, product))
            dq = jnp.zeros((HD, chunk), full)
            for (at, _), (probs, product) in zip(pieces, kept):
                score_grad = (product - probs * delta).astype(low)
                dq += mm(k_ref[0, :, at : at + HALF], score_grad)
                dk_acc[at : at + HALF, :] += mm(score_grad, query_rows)
                dv_acc[at : at + HALF, :] += mm(probs.astype(low), grad_rows)
            dq_ref[head, :, span] = dq * scale
    dk_ref[0] = dk_acc[...].T
    dv_ref[0] = dv_acc[...].T


def attention_specs(tokens):
    heads = pl.BlockSpec((QPG, HD, tokens), lambda g, s: (g, 0, 0))
    keys = pl.BlockSpec((1, HD, LEN), lambda g, s: (g, 0, 0))
    sums = pl.BlockSpec((1, QPG, tokens), lambda g, s: (g, 0, 0))
    return heads, keys, sums


def attend(starts, queries, keys, values):
    tokens = queries.shape[2]
    heads, whole, sums = attention_specs(tokens)
    pairs = QH * (tokens // 2) * (LEN + HALF)
    return pl.pallas_call(
        attend_kernel,
        out_shape=(
            jax.ShapeDtypeStruct((QH, HD, tokens), low),
            jax.ShapeDtypeStruct((KVH, QPG, tokens), full),
        ),
        grid_spec=pltpu.PrefetchScalarGridSpec(
            num_scalar_prefetch=1,
            grid=(KVH,),
            in_specs=[heads, whole, whole],
            out_specs=[heads, sums],
        ),
        compiler_params=pltpu.CompilerParams(vmem_limit_bytes=40 << 20),
        cost_estimate=pl.CostEstimate(
            flops=pairs, bytes_accessed=1 << 20, transcendentals=0
        ),
    )(starts, queries, keys, values)


def attend_back(starts, queries, keys, values, grads, sums_in):
    tokens = queries.shape[2]
    heads, whole, sums = attention_specs(tokens)
    pairs = QH * (tokens // 2) * (LEN + HALF)
    return pl.pallas_call(
        attend_back_kernel,
        out_shape=(
            jax.ShapeDtypeStruct((QH, HD, tokens), full),
            jax.ShapeDtypeStruct((KVH, HD, LEN), full),
            jax.ShapeDtypeStruct((KVH, HD, LEN), full),
        ),
        grid_spec=pltpu.PrefetchScalarGridSpec(
            num_scalar_prefetch=1,
            grid=(KVH,),
            in_specs=[heads, whole, whole, heads, sums],
            out_specs=[heads, whole, whole],
            scratch_shapes=[pltpu.VMEM((LEN, HD), full), pltpu.VMEM((LEN, HD), full)],
        ),
        compiler_params=pltpu.CompilerParams(vmem_limit_bytes=40 << 20),
        cost_estimate=pl.CostEstimate(
            flops=pairs, bytes_accessed=1 << 20, transcendentals=0
        ),
    )(starts, queries, keys, values, grads, sums_in)


def by_ranks(wide, down, rank, parts):
    rows, units = wide.shape[0], wide.shape[1] // (2 * parts)
    place = lambda r: (rank - r) % parts
    if units % 128:
        blocks = jnp.concatenate(
            [a.reshape(rows, -1, parts, units) for a in (wide, down)], 1
        )
        blocks = jnp.transpose(blocks, (2, 0, 1, 3)).reshape(parts, rows, 3 * units)
        return jnp.stack([blocks[place(r)] for r in range(parts)])

    def kernel(index_ref, gate_ref, up_ref, down_ref, out_ref):
        for k, ref in enumerate((gate_ref, up_ref, down_ref)):
            out_ref[0, :, k * units : (k + 1) * units] = ref[...]

    def column(first):
        return pl.BlockSpec((rows, units), lambda r, index: (0, first + index[r]))

    return pl.pallas_call(
        kernel,
        out_shape=jax.ShapeDtypeStruct((parts, rows, 3 * units), low),
        grid_spec=pltpu.PrefetchScalarGridSpec(
            num_scalar_prefetch=1,
            grid=(parts,),
            in_specs=[column(0), column(parts), column(0)],
            out_specs=pl.BlockSpec((1, rows, 3 * units), lambda r, index: (r, 0, 0)),
        ),
        compiler_params=pltpu.CompilerParams(vmem_limit_bytes=32 << 20),
        cost_estimate=pl.CostEstimate(flops=0, bytes_accessed=1 << 16, transcendentals=0),
    )(place(jnp.arange(parts, dtype=jnp.int32)), wide, wide, down)


def widen_kernel(pack_ref, gate_out, up_out, down_out):
    units = gate_out.shape[1]
    gate_out[...] = pack_ref[0, :, :units].astype(full)
    up_out[...] = pack_ref[0, :, units : 2 * units].astype(full)
    down_out[...] = pack_ref[0, :, 2 * units :].astype(full).T


def widen(pack):
    groups, rows, columns = pack.shape
    units = columns // 3
    if units % 128:
        gate, up, down = (
            jnp.transpose(pack[:, :, k * units : (k + 1) * units], (1, 0, 2))
            .reshape(rows, -1)
            .astype(full)
            for k in range(3)
        )
        return gate, up, down.T
    shape = jax.ShapeDtypeStruct((rows, groups * units), full)
    column = pl.BlockSpec((rows, units), lambda g: (0, g))
    return pl.pallas_call(
        widen_kernel,
        out_shape=(shape, shape, jax.ShapeDtypeStruct((groups * units, rows), full)),
        grid=(groups,),
        in_specs=[pl.BlockSpec((1, rows, columns), lambda g: (g, 0, 0))],
        out_specs=[column, column, pl.BlockSpec((units, rows), lambda g: (g, 0))],
        compiler_params=pltpu.CompilerParams(vmem_limit_bytes=32 << 20),
        cost_estimate=pl.CostEstimate(flops=0, bytes_accessed=1 << 16, transcendentals=0),
    )(pack)


def norm_backward(values, rms, gain, normed_grad):
    weighted = normed_grad * gain
    dotted = jnp.sum(weighted * values, axis=1, keepdims=True)
    grad = weighted * rms - values * (rms * rms * rms) * dotted / D
    return grad, jnp.sum(normed_grad * values * rms, axis=0)


def on_device(
    hidden_in,
    positions,
    head_counts,
    attention_gain,
    query_projection_weight,
    key_weight,
    value_weight,
    query_gain,
    key_gain,
    output_weight,
    feedforward_gain,
    gate_weight,
    up_weight,
    down_projection_weight,
    cotangent,
):
    groups = lax.axis_size("dp")
    parts = lax.axis_size("mp")
    group = lax.axis_index("dp")
    rank = lax.axis_index("mp")
    tokens, share = hidden_in.shape
    seqs = tokens // LEN
    ring = parts // seqs
    mine = tokens // parts
    chunk = mine // 2
    units = gate_weight.shape[1] // groups
    slots = query_projection_weight.shape[1]
    place = rank % ring
    ranks = range(parts)

    lower = jnp.arange(parts)[None, :] < jnp.arange(parts)[:, None]
    offsets = jnp.sum(jnp.where(lower, head_counts[None, :], 0), axis=1)

    def selection(order):
        within = jnp.arange(slots, dtype=jnp.int32)
        column = offsets[order][:, None] * HD + within[None, :]
        column = jnp.where(within[None, :] < head_counts[order][:, None] * HD, column, -1)
        return (
            column.reshape(-1)[:, None] == jnp.arange(QH * HD, dtype=jnp.int32)[None, :]
        ).astype(low)

    select_near = selection(rank ^ jnp.arange(parts, dtype=jnp.int32))
    select = selection(jnp.arange(parts, dtype=jnp.int32))

    def rows_of(array, other):
        base = (other // ring) * LEN
        at = other % ring
        first = lax.dynamic_slice_in_dim(array, base + at * chunk, chunk, 0)
        last = lax.dynamic_slice_in_dim(array, base + (2 * ring - 1 - at) * chunk, chunk, 0)
        return jnp.concatenate([first, last], 0)

    order = Order(head_counts)
    rows = D // groups
    heads_here = QH * HD // groups

    query_slice = lax.dynamic_slice_in_dim(query_projection_weight, group * rows, rows, 0)
    gains = jnp.stack([attention_gain, feedforward_gain])
    gains_high = gains.astype(low)
    gains_low = (gains - gains_high.astype(full)).astype(low)
    lines = -(-share // slots)
    gains = jnp.pad(
        jnp.concatenate([gains_high, gains_low], 0), ((0, 0), (0, lines * slots - share))
    )
    query_slice = jnp.concatenate([query_slice, gains.reshape(4 * lines, slots)], 0)
    query_slice = swap([query_slice] * parts, "mp")
    cosine, sine = rotary_tables(rows_of(positions, rank))
    chosen = lax.dynamic_slice_in_dim(select, group * heads_here, heads_here, 1)
    output_slice = dot(chosen, output_weight, 0, 0).astype(low)
    pack = jnp.concatenate(
        [
            lax.dynamic_slice_in_dim(gate_weight, group * units, units, 1),
            lax.dynamic_slice_in_dim(up_weight, group * units, units, 1),
            lax.dynamic_slice_in_dim(down_projection_weight, group * units, units, 0).T,
        ],
        1,
    )
    inputs = [rows_of(hidden_in, rank ^ k) for k in ranks]
    late = inputs[parts - 1]
    inputs = inputs[:1] + [exchange(inputs[k], "mp", k, parts) for k in range(1, parts - 1)]
    cotangent = [rows_of(cotangent, rank ^ k) for k in ranks]
    got = order(
        select_near, select, late, cosine, sine, output_slice, pack,
        *query_slice, *cotangent, *inputs
    )
    select_near, select, late, cosine, sine, output_slice, pack = got[:7]
    query_slice, cotangent = (got[7 + k * parts : 7 + (k + 1) * parts] for k in range(2))
    inputs = got[7 + 2 * parts :]

    inputs.append(exchange(late, "mp", parts - 1, parts))
    output_slice = swap([output_slice] * parts, "mp")
    gains = by_rank([piece[rows:].reshape(4, -1)[:, :share] for piece in query_slice], rank)
    gains = jnp.concatenate(gains, 1).astype(full)
    attention_gain_all, feedforward_gain_all = gains[0] + gains[2], gains[1] + gains[3]
    query_slice = jnp.concatenate([piece[:rows] for piece in query_slice], axis=1)
    query_slice = mm(query_slice, select_near).astype(low)
    query_all = lax.all_gather(query_slice, "dp", axis=0, tiled=True)
    got = order(*inputs, *output_slice)
    inputs, output_slice = got[:parts], got[parts:]

    inputs = jnp.concatenate(by_rank(inputs, rank), axis=1).astype(full)
    first_rms = lax.rsqrt(jnp.mean(inputs * inputs, axis=1, keepdims=True) + epsilon)
    normed = (inputs * first_rms * attention_gain_all).astype(low)
    keys = dot(key_weight, normed, 0, 1).reshape(KVH, HD, mine)
    values_mine = dot(value_weight, normed, 0, 1).astype(low).reshape(KVH, HD, mine)
    turned_keys, key_pull = jax.vjp(lambda v, g: turn(v, g, cosine, sine), keys, key_gain)
    pair_mine = jnp.concatenate([turned_keys.astype(low), values_mine], 0)
    pair_mine, normed = order(pair_mine, normed)

    near_pairs = [pair_mine] + [exchange(pair_mine, "mp", k, parts) for k in range(1, ring)]
    output_slice = jnp.concatenate(by_rank(output_slice, rank), axis=1)
    output_all = lax.all_gather(output_slice, "dp", axis=0, tiled=True)
    queries = dot(query_all, normed, 0, 1).reshape(QH, HD, mine)
    turned_queries, query_pull = jax.vjp(
        lambda v, g: turn(v, g, cosine, sine), queries, query_gain
    )
    got = order(turned_queries.astype(low), *near_pairs, *cotangent)
    turned_queries, near_pairs, cotangent = got[0], got[1 : ring + 1], got[ring + 1 :]

    cotangent = swap(cotangent, "mp")
    near_pairs = by_rank(near_pairs, place)
    pair = jnp.concatenate(
        [p[:, :, :chunk] for p in near_pairs] + [p[:, :, chunk:] for p in near_pairs[::-1]], axis=2
    )
    key_heads, value_heads = pair[:KVH], pair[KVH:]
    starts = jnp.stack([place * chunk, (2 * ring - 1 - place) * chunk]).astype(jnp.int32)
    mixed, row_totals = attend(starts, turned_queries, key_heads, value_heads)
    mixed = mixed.reshape(QH * HD, mine)
    middle = inputs + dot(mixed, output_all, 0, 0)
    second_rms = lax.rsqrt(jnp.mean(middle * middle, axis=1, keepdims=True) + epsilon)
    second_normed = (middle * second_rms * feedforward_gain_all).astype(low)
    second_normed, pack, *cotangent = order(second_normed, pack, *cotangent)

    second = Spread(second_normed, "dp", groups, group)
    weights = RelayGather(pack, "mp", parts)
    cotangent_mine = jnp.concatenate(by_rank(cotangent, rank), axis=1)
    cube = groups == CUBE
    if cube:
        flag = group % 2 != 0
        pairs = [normed[:, k * rows : (k + 1) * rows] for k in range(groups)]
        normed_own, normed_other = (
            jnp.concatenate(
                [jnp.where(flag, pairs[k ^ 1 ^ a], pairs[k ^ a]) for k in range(0, groups, 2)], 1
            )
            for a in (0, 1)
        )
        pairs = mixed.reshape(4, 2, heads_here, mine)
        mixed_own, mixed_other = (
            lax.dynamic_index_in_dim(pairs, at, 1, keepdims=False).reshape(-1, mine)
            for at in (group % 2, 1 - group % 2)
        )
    else:
        normed_own = normed_other = normed
        mixed_own = mixed_other = mixed
    *got, up, down, cotangent_mine, normed_own, normed_other, mixed_own, mixed_other = order(
        *second.flying, *weights.flying, cotangent_mine, normed_own, normed_other,
        mixed_own, mixed_other
    )
    second.second(*got)
    weights.take(up, down)
    cotangent_mine, got, (up, down), second.buffer = order_split(
        order, [cotangent_mine], second.flying, weights.flying, second.buffer
    )
    cotangent_full = lax.all_gather(cotangent_mine, "dp", axis=0, tiled=True)
    second.third(*got)
    weights.take(up, down)
    got, (up, down) = order_split(order, [], second.flying, weights.flying)
    second.last(*got)
    weights.take(up, down)
    pack = weights.finish(order)
    wide = jnp.concatenate(
        [block[:, :units] for block in pack] + [block[:, units : 2 * units] for block in pack], 1
    )
    down_here = jnp.concatenate([block[:, 2 * units :] for block in pack], 1)
    half = parts * units

    raised = [mm(part, wide) for part in second.parts]
    hidden = [
        (v[:, :half] * jax.nn.sigmoid(v[:, :half]) * v[:, half:]).astype(low) for v in raised
    ]
    down_terms = [dot(h, down_here, 1, 1).astype(low) for h in hidden]
    down_terms, raised, hidden, (cotangent_full,) = order_split(
        order, [], down_terms, raised, hidden, [cotangent_full]
    )
    def cores(array, at):
        if not cube:
            return array
        array = array.reshape(4, 2, mine, D)
        return lax.dynamic_index_in_dim(array, at, 1, keepdims=False).reshape(4 * mine, D)

    cot = [cores(cotangent_full, at) for at in ((group % 2, 1 - group % 2) if cube else (0,))]

    def back(part, v):
        hidden_grad = mm(part, down_here)
        gate, up = v[:, :half], v[:, half:]
        sigma = jax.nn.sigmoid(gate)
        gate_grad = hidden_grad * up * sigma * (1.0 + gate * (1.0 - sigma))
        return jnp.concatenate([gate_grad.astype(low), (hidden_grad * gate * sigma).astype(low)], 1)

    grads = [back(cot[-1], raised[-1])]
    other = dot(grads[0], wide, 1, 1).astype(low)
    other, grads[0], *raised = order(other, grads[0], *raised)

    second_sum = Collect(other, "dp", groups, group)
    own = other
    if len(raised) > 1:
        grads.insert(0, back(cot[0], raised[0]))
        own = dot(grads[0], wide, 1, 1).astype(low)
    own, *grads, hidden, got = order_split(order, [own, *grads], hidden, second_sum.flying)

    second_sum.second(own, *got)
    wide_grad = sum(dot(part, grad, 0, 0) for part, grad in zip(second.parts, grads)).astype(low)
    down_grad = sum(dot(part, h, 0, 0) for part, h in zip(cot, hidden)).astype(low)
    down_sum = Collect(down_terms[-1], "dp", groups, group)
    down_grad, wide_grad, got, flying = order_split(
        order, [down_grad, wide_grad], second_sum.flying, down_sum.flying
    )

    second_sum.third(*got)

    pack = by_ranks(wide_grad, down_grad, rank, parts)
    pack = lax.psum_scatter(pack, "mp", scatter_dimension=0, tiled=False)
    down_sum.second(down_terms[0], *flying, apart=True)
    *got, flying = order_split(order, second_sum.flying, down_sum.flying)

    normed_two_grad = second_sum.last(*got).astype(full)
    down_sum.launch(*flying)
    middle_part, feedforward_gain_grad = norm_backward(
        middle, second_rms, feedforward_gain_all, normed_two_grad
    )
    middle_grad = cotangent_mine.astype(full) + middle_part
    lane = lax.broadcasted_iota(jnp.int32, (D, EXTRA), 1)
    wide_extra = jnp.where(lane == 0, feedforward_gain_grad[:, None], 0.0)
    branch_grad = middle_grad.astype(low)
    mixed_grad = dot(output_all, branch_grad, 1, 1).astype(low).reshape(QH, HD, mine)
    output_other = mm(mixed_other, branch_grad).astype(low)
    output_own = mm(mixed_own, branch_grad).astype(low) if cube else output_other
    output_sum = Collect(output_other, "dp", groups, group)
    query_rot_grad, key_rot_grad, value_grad = attend_back(
        starts, turned_queries, key_heads, value_heads, mixed_grad, row_totals
    )
    pair_grad = jnp.concatenate([key_rot_grad, value_grad], 0)
    blocks = [
        jnp.concatenate(
            [
                pair_grad[:, :, j * chunk : (j + 1) * chunk],
                pair_grad[:, :, (2 * ring - 1 - j) * chunk : (2 * ring - j) * chunk],
            ],
            axis=2,
        )
        for j in range(ring)
    ]
    blocks = by_rank(blocks, place)
    away = [block.astype(low) for block in blocks[1:]]
    query_rot_grad, output_own, *away, got, flying = order_split(
        order, [query_rot_grad, output_own, *away], down_sum.flying, output_sum.flying
    )
    down_sum.third(*got)
    output_sum.second(output_own, *flying)

    away = [exchange(block, "mp", k + 1, parts) for k, block in enumerate(away)]
    queries_low, query_gain_grad = query_pull(query_rot_grad)
    queries_low = queries_low.astype(low).reshape(QH * HD, mine)
    queries_low, pack, wide_extra, *away, out_relayed, got = order_split(
        order, [queries_low, pack, wide_extra, *away], down_sum.flying, output_sum.flying
    )
    output_sum.third(*got)
    pack = by_rows(lax.all_gather(by_rows(pack), "dp", axis=0, tiled=False))
    pair_grad = sum([blocks[0]] + [block.astype(full) for block in away])
    keys_grad, key_gain_grad = key_pull(pair_grad[:KVH])
    pair_low = jnp.concatenate(
        [keys_grad.astype(low), pair_grad[KVH:].astype(low)], 0
    ).reshape(2 * KVH * HD, mine)
    all_low = jnp.concatenate([queries_low, pair_low], 0)
    heads_gain = jnp.stack([query_gain_grad, key_gain_grad])
    top = wide_extra[:2] + jnp.pad(heads_gain, ((0, 0), (EXTRA - HD, 0)))
    extra = jnp.concatenate([top, wide_extra[2:]], 0)
    wide_low = jnp.concatenate([all_low, jnp.zeros((EXTRA, mine), low)], 0)

    def projections(normed_part, extra_part):
        extra_part = jnp.pad(extra_part, ((0, 0), (wide_low.shape[0] - EXTRA, 0)))
        return (dot(normed_part, wide_low, 0, 1) + extra_part).astype(low)

    own = other = extra
    if cube:
        pairs = extra.reshape(4, 2, rows, EXTRA)
        own, other = (
            lax.dynamic_index_in_dim(pairs, at, 1, keepdims=False).reshape(4 * rows, EXTRA)
            for at in (group % 2, 1 - group % 2)
        )
    other = projections(normed_other, other)
    other, own, wide_low, all_low, normed_own = order(other, own, wide_low, all_low, normed_own)

    def by_feature(array):
        return by_rank([array[:, j * share : (j + 1) * share] for j in ranks], rank)

    projection_sum = Collect(other, "dp", groups, group)
    own = projections(normed_own, own) if cube else other
    queries_low, pair_low = all_low[: QH * HD], all_low[QH * HD :]
    normed_grad = (
        dot(queries_low, query_all, 0, 1)
        + dot(pair_low[: KVH * HD], key_weight, 0, 1)
        + dot(pair_low[KVH * HD :], value_weight, 0, 1)
    )
    input_part, _ = norm_backward(
        inputs, first_rms, attention_gain_all, normed_grad
    )
    input_gradient = (middle_grad + input_part).astype(low)
    input_gradient, own, got, flying = order_split(
        order, [input_gradient, own], projection_sum.flying, output_sum.flying
    )
    projection_sum.second(own, *got)
    output_grad = output_sum.last(*flying)

    def by_tokens(got, kind):
        got = by_rank(got, rank)
        rows = []
        for seq in range(seqs):
            near = got[seq * ring : (seq + 1) * ring]
            rows += [block[:chunk] for block in near]
            rows += [block[chunk:] for block in near[::-1]]
        return jnp.concatenate(rows, 0).astype(kind)

    input_gradient = swap(by_feature(input_gradient), "mp")
    input_gradient, got, out_relayed = order_split(
        order, [], input_gradient, projection_sum.flying, out_relayed
    )
    projection_sum.third(*got)

    output_grad = swap(by_feature(output_grad), "mp")
    output_grad, got, out_relayed = order_split(
        order, [], output_grad, projection_sum.flying, out_relayed
    )
    output_grad = jnp.pad(added(*output_grad), ((0, rows - heads_here), (0, 0)))
    projection_total = projection_sum.last(*got)
    down_sum.fourth(*out_relayed)

    query_total, pair_total, extra = jnp.split(
        projection_total, [QH * HD, (QH + 2 * KVH) * HD], axis=1
    )
    here = lambda weight: lax.dynamic_slice_in_dim(weight, group * rows, rows, 0).astype(full)
    product = jnp.sum(here(query_all) * query_total.astype(full), axis=1)
    product += jnp.sum(here(key_weight) * pair_total[:, : KVH * HD].astype(full), axis=1)
    product += jnp.sum(here(value_weight) * pair_total[:, KVH * HD :].astype(full), axis=1)
    product = product / lax.dynamic_slice_in_dim(attention_gain_all, group * rows, rows, 0)
    column = lax.broadcasted_iota(jnp.int32, extra.shape, 1)
    extra = jnp.where(column == 2, product[:, None].astype(low), extra)
    query_part = dot(query_total, select_near, 1, 1).astype(low)
    projection = swap(
        [
            jnp.concatenate([query_part[:, k * slots : (k + 1) * slots], pair_total, extra], 1)
            for k in ranks
        ],
        "mp",
    )
    pack, projection, flying = order_split(order, [pack], projection, down_sum.flying)

    projection = jnp.concatenate([added(*projection), output_grad], 1)
    projection = lax.all_gather(projection, "dp", axis=0, tiled=True)
    output = (middle + down_sum.last(*flying).astype(full)).astype(low)
    output = swap(by_feature(output), "mp")
    gate_weight_grad, up_weight_grad, down_weight_grad = widen(pack)
    input_gradient = by_tokens(input_gradient, full)
    got = order(
        projection, gate_weight_grad, up_weight_grad, down_weight_grad, input_gradient, *output
    )
    projection, gate_weight_grad, up_weight_grad, down_weight_grad, input_gradient = got[:5]
    output = by_tokens(got[5:], low)

    widths = [slots, KVH * HD, KVH * HD, EXTRA]
    cuts = [sum(widths[: k + 1]) for k in range(4)]
    query_weight_grad, key_weight_grad, value_weight_grad, extra, output_grad = jnp.split(
        projection, cuts, axis=1
    )
    output_grad = output_grad.reshape(groups, rows, -1)[:, :heads_here].reshape(QH * HD, -1)
    output_weight_grad = mm(select, output_grad)
    extra = extra.astype(full)
    own_share = lax.dynamic_slice_in_dim(extra, rank * share, share, 0)
    return (
        output,
        input_gradient,
        own_share[:, 2],
        query_weight_grad.astype(full),
        key_weight_grad.astype(full),
        value_weight_grad.astype(full),
        extra[0, EXTRA - HD :],
        extra[1, EXTRA - HD :],
        output_weight_grad,
        own_share[:, 0],
        gate_weight_grad,
        up_weight_grad,
        down_weight_grad,
    )


def solution(mesh):
    in_specs = (
        P("dp", "mp"),
        P("dp"),
        P(),
        P("mp"),
        P(None, "mp"),
        P(),
        P(),
        P(),
        P(),
        P(None, "mp"),
        P("mp"),
        P(None, "mp"),
        P(None, "mp"),
        P("mp", None),
        P("dp", "mp"),
    )
    out_specs = (
        P("dp", "mp"),
        P("dp", "mp"),
        P("mp"),
        P(None, "mp"),
        P(),
        P(),
        P(),
        P(),
        P(None, "mp"),
        P("mp"),
        P(None, "mp"),
        P(None, "mp"),
        P("mp", None),
    )
    return jax.shard_map(
        on_device, mesh=mesh, in_specs=in_specs, out_specs=out_specs, check_vma=False
    )
```

```python
import functools
import math

import jax
import jax.numpy as jnp
from jax import lax
from jax.experimental.layout import Layout, with_layout_constraint
from jax.experimental import pallas as pl
from jax.experimental.pallas import tpu as pltpu
from jax.sharding import PartitionSpec as P

D = 2048
QH = 20
KVH = 5
QPG = QH // KVH
HD = 64
LEN = 1024

epsilon = 1e-05
rope_base = 10000.0
masked_score = -1e30
low = jnp.bfloat16
full = jnp.float32


def dot(left, right, left_axis, right_axis):
    return lax.dot_general(
        left, right, (((left_axis,), (right_axis,)), ((), ())), preferred_element_type=full
    )


def swap(pieces, axis):
    n = len(pieces)
    return [pieces[0]] + [
        lax.ppermute(pieces[k], axis, [(i, i ^ k) for i in range(n)]) for k in range(1, n)
    ]


def by_rank(blocks, rank):
    bit = 1
    while bit < len(blocks):
        flag = (rank & bit) != 0
        blocks = [jnp.where(flag, blocks[j ^ bit], blocks[j]) for j in range(len(blocks))]
        bit *= 2
    return blocks


def exchange(array, axis, mask, n):
    return lax.ppermute(array, axis, [(i, i ^ mask) for i in range(n)])


def by_rows(array):
    return with_layout_constraint(array, Layout(tuple(range(array.ndim))))


def added(*terms):
    return sum(term.astype(full) for term in terms).astype(low)


class Order:
    def __init__(self, token):
        self.token = token

    def __call__(self, *arrays):
        self.token, *arrays = lax.optimization_barrier((self.token, *arrays))
        return arrays


class RelayGather:
    def __init__(self, piece, axis, n):
        self.axis, self.n, self.step, self.own = axis, n, 1, piece
        self.ups, self.downs = [], []
        self.send(piece, piece)

    def send(self, up, down):
        n, step = self.n, self.step
        right = [(i, i + 1) for i in range(step - 1, n - 1)]
        left = [(i, i - 1) for i in range(n - step, 0, -1)]
        self.flying = [lax.ppermute(up, self.axis, right), lax.ppermute(down, self.axis, left)]

    def take(self, up, down):
        self.ups.append(up)
        self.downs.append(down)
        self.step += 1
        if self.step < self.n:
            self.send(up, down)

    def finish(self, order):
        while self.step < self.n:
            self.take(*order(*self.flying))
        n = self.n
        return [self.own] + [self.ups[k - 1] + self.downs[n - k - 1] for k in range(1, n)]


CUBE = 8


def at_index(array, index):
    return lax.dynamic_index_in_dim(array, index, 0, keepdims=False)


class Spread:
    def __init__(self, piece, axis, n, group):
        self.axis, self.n, self.chip, self.piece = axis, n, group // 2, piece
        if n == CUBE:
            self.flying = [self.move(piece, 2), self.move(piece, 4)]
        else:
            self.flying = [lax.all_gather(piece, axis, axis=0, tiled=True)]
        self.buffer = []

    def move(self, array, mask):
        return exchange(array, self.axis, mask, self.n)

    def second(self, *got):
        self.flying = got
        if self.n == CUBE:
            near, far = got
            half = self.piece.shape[0] // 2
            self.flying = [self.move(near[:half], 4), self.move(far[half:], 2)]
            mine = jnp.zeros((4, *self.piece.shape), self.piece.dtype)
            for k, block in enumerate((self.piece, near, far)):
                mine = lax.dynamic_update_slice(mine, block[None], (self.chip ^ k, 0, 0))
            self.buffer = [mine]

    def third(self, *got):
        if self.n != CUBE:
            self.parts, self.flying = list(got), []
            return
        rows = self.piece.shape[0]
        (mine,) = self.buffer
        for k, block in enumerate(got):
            mine = lax.dynamic_update_slice(
                mine, block[None], (self.chip ^ 3, k * (rows // 2), 0)
            )
        mine = mine.reshape(4 * rows, -1)
        self.parts = [mine]
        self.flying = [self.move(mine, 1)]

    def last(self, *got):
        self.parts += got


TOGETHER = (((3, 0), (1, 0)), ((3, 1), (2, 1)), ((0, 0), (0, 1), (2, 0), (1, 1)))
APART = (((3, 0),), ((3, 1),), ((1, 0),), ((2, 1),), ((0, 0), (0, 1), (2, 0), (1, 1)))


def chip_sums(mine, got, chip, plan):
    half, columns = mine.shape[0] // 8, mine.shape[1]
    flat = [place for places in plan for place in places]
    index = jnp.stack([(chip ^ block) * 2 + part for block, part in flat]).astype(jnp.int32)
    firsts = [sum(len(places) for places in plan[:k]) for k in range(len(plan))]

    def kernel(index_ref, mine_ref, got_ref, *outs):
        step = pl.program_id(0)
        total = (mine_ref[...].astype(full) + got_ref[...].astype(full)).astype(low)
        for first, places, out in zip(firsts, plan, outs):

            @pl.when((step >= first) & (step < first + len(places)))
            def _():
                out[...] = total

    source = pl.BlockSpec((half, columns), lambda g, index: (index[g], 0))

    def target(first, count):
        return pl.BlockSpec(
            (half, columns), lambda g, index: (jnp.clip(g - first, 0, count - 1), 0)
        )

    return pl.pallas_call(
        kernel,
        out_shape=[
            jax.ShapeDtypeStruct((len(places) * half, columns), low) for places in plan
        ],
        grid_spec=pltpu.PrefetchScalarGridSpec(
            num_scalar_prefetch=1,
            grid=(len(flat),),
            in_specs=[source, source],
            out_specs=[target(f, len(places)) for f, places in zip(firsts, plan)],
        ),
        compiler_params=pltpu.CompilerParams(vmem_limit_bytes=40 << 20),
        cost_estimate=pl.CostEstimate(flops=0, bytes_accessed=1 << 16, transcendentals=0),
    )(index, mine, got)


class Collect:
    def __init__(self, other, axis, n, group):
        self.axis, self.n, self.chip = axis, n, group // 2
        if n == CUBE:
            self.flying = [self.move(other, 1)]
        else:
            self.flying = [lax.psum_scatter(other, axis, scatter_dimension=0, tiled=True)]

    def move(self, array, mask):
        return exchange(array, self.axis, mask, self.n)

    def second(self, mine, *got, apart=False):
        self.flying, self.held = got, []
        if self.n != CUBE:
            return
        self.half = mine.shape[0] // 8
        *sent, self.keep = chip_sums(mine, got[0], self.chip, APART if apart else TOGETHER)
        self.apart = apart
        if apart:
            self.flying, self.held = sent[:2], sent[2:]
        else:
            self.launch(*sent)

    def launch(self, *ready):
        self.flying = ready
        if self.n == CUBE:
            self.flying = [self.move(ready[0], 2), self.move(ready[1], 4)]

    def third(self, *got):
        self.flying = got
        if self.n != CUBE:
            return
        half = self.half
        if not self.apart:
            self.direct = [got[0][half:], got[1][half:]]
        self.flying = [
            self.move(added(self.keep[2 * half : 3 * half], got[0][:half]), 4),
            self.move(added(self.keep[3 * half :], got[1][:half]), 2),
        ]

    def fourth(self, *got):
        self.flying = got
        if self.n == CUBE:
            self.relayed = got
            self.flying = [self.move(self.held[0], 2), self.move(self.held[1], 4)]

    def last(self, *got):
        if self.n != CUBE:
            return got[0]
        half = self.half
        direct, got = (got, self.relayed) if self.apart else (self.direct, got)
        return jnp.concatenate(
            [
                added(self.keep[:half], direct[0], got[0]),
                added(self.keep[half : 2 * half], direct[1], got[1]),
            ],
            0,
        )


EXTRA = 128


def order_split(order, first, *lists):
    first = list(first)
    got = order(*first, *[array for arrays in lists for array in arrays])
    result, at = list(got[: len(first)]), len(first)
    for arrays in lists:
        result.append(list(got[at : at + len(arrays)]))
        at += len(arrays)
    return result


def rotary_tables(positions):
    half = HD // 2
    inverse = jnp.exp(-math.log(rope_base) * (2.0 * jnp.arange(half, dtype=full)) / HD)
    angles = inverse[:, None] * positions.astype(full)[None, :]
    cosine, sine = jnp.cos(angles), jnp.sin(angles)
    return jnp.concatenate([cosine, cosine], 0), jnp.concatenate([sine, sine], 0)


def turn(raw, gain, cosine, sine):
    half = HD // 2
    rms = lax.rsqrt(jnp.mean(raw * raw, axis=1, keepdims=True) + epsilon)
    normed = raw * rms * gain[None, :, None]
    turned = jnp.concatenate([-normed[:, half:], normed[:, :half]], axis=1)
    return normed * cosine[None] + turned * sine[None]


def mm(left, right):
    return jnp.dot(left, right, preferred_element_type=full)


BLOCK = LEN // 4
PARTS = (((0, True),), ((0, False), (BLOCK, False), (2 * BLOCK, True)))


def scores_of(key, query, lead):
    scores = mm(key, query)
    if lead is None:
        return scores
    rows = lax.broadcasted_iota(jnp.int32, scores.shape, 0)
    cols = lax.broadcasted_iota(jnp.int32, scores.shape, 1)
    return jnp.where(rows - cols <= lead, scores, masked_score)


def last_piece(starts, chunk):
    early = starts[0] >= BLOCK
    at = pl.multiple_of(jnp.where(early, BLOCK, 3 * BLOCK), BLOCK)
    span = pl.multiple_of(jnp.where(early, 0, chunk), 128)
    start = jnp.where(early, starts[0], starts[1])
    flag = jnp.where(early, 1.0, 0.0).astype(full)
    return early, pl.ds(at, BLOCK), pl.ds(span, chunk), start - at, (flag, 1.0 - flag)


def rows_kept(array):
    return array.astype(full).T.astype(low)


def attend_kernel(starts, q_ref, k_ref, v_ref, o_ref, sums_ref, key_ref):
    chunk = q_ref.shape[2] // 2
    scale = jnp.asarray(1.0 / math.sqrt(HD), low)
    key_ref[...] = rows_kept(k_ref[0])
    early, keys, columns, lead, flags = last_piece(starts, chunk)
    for head in range(QPG):
        scores, peaks = [], []
        for part, pieces in enumerate(PARTS):
            query = q_ref[head, :, part * chunk : (part + 1) * chunk] * scale
            scores.append(
                [
                    scores_of(key_ref[at : at + BLOCK], query, starts[part] - at if cut else None)
                    for at, cut in pieces
                ]
            )
            peaks.append(
                functools.reduce(
                    jnp.maximum, [jnp.max(s, axis=0, keepdims=True) for s in scores[-1]]
                )
            )
        more = scores_of(key_ref[keys], q_ref[head, :, columns] * scale, lead)
        peak = jnp.max(more, axis=0, keepdims=True)
        peaks = [
            jnp.maximum(peaks[0], jnp.where(early, peak, masked_score)),
            jnp.maximum(peaks[1], jnp.where(early, masked_score, peak)),
        ]
        more = jnp.exp(more - jnp.where(early, peaks[0], peaks[1]))
        more_total = jnp.sum(more, axis=0, keepdims=True)
        more_result = mm(v_ref[0, :, keys], more.astype(low))
        for part, pieces in enumerate(PARTS):
            total = more_total * flags[part]
            result = more_result * flags[part]
            for (at, _), s in zip(pieces, scores[part]):
                weights = jnp.exp(s - peaks[part])
                total += jnp.sum(weights, axis=0, keepdims=True)
                result += mm(v_ref[0, :, at : at + BLOCK], weights.astype(low))
            span = pl.ds(part * chunk, chunk)
            o_ref[head, :, span] = (result / total).astype(low)
            sums_ref[0, head : head + 1, span] = peaks[part] + jnp.log(total)


def attend_back_kernel(
    starts, q_ref, k_ref, v_ref, g_ref, sums_ref, dq_ref, dk_ref, dv_ref, dk_acc, dv_acc,
    key_ref, value_ref
):
    chunk = q_ref.shape[2] // 2
    scale = 1.0 / math.sqrt(HD)
    key_ref[...] = rows_kept(k_ref[0])
    value_ref[...] = rows_kept(v_ref[0])
    dk_acc[...] = jnp.zeros_like(dk_acc)
    dv_acc[...] = jnp.zeros_like(dv_acc)
    early, keys, columns, lead, flags = last_piece(starts, chunk)

    def products(at, query, grad, sums, lead):
        probs = jnp.exp(scores_of(key_ref[at], query, lead) - sums)
        return probs, probs * mm(value_ref[at], grad)

    def store(at, probs, product, delta, query_rows, grad_rows):
        score_grad = (product - probs * delta).astype(low)
        dk_acc[at, :] += mm(score_grad, query_rows)
        dv_acc[at, :] += mm(probs.astype(low), grad_rows)
        return mm(k_ref[0, :, at], score_grad)

    for head in range(QPG):
        parts = []
        for part, pieces in enumerate(PARTS):
            span = pl.ds(part * chunk, chunk)
            query = q_ref[head, :, span] * jnp.asarray(scale, low)
            grad = g_ref[head, :, span]
            sums = sums_ref[0, head : head + 1, span]
            found = [
                products(
                    pl.ds(at, BLOCK), query, grad, sums, starts[part] - at if cut else None
                )
                for at, cut in pieces
            ]
            delta = sum(jnp.sum(product, axis=0, keepdims=True) for _, product in found)
            parts.append([found, delta, rows_kept(query), rows_kept(grad)])
        probs, product = products(
            keys,
            q_ref[head, :, columns] * jnp.asarray(scale, low),
            g_ref[head, :, columns],
            sums_ref[0, head : head + 1, columns],
            lead,
        )
        more = jnp.sum(product, axis=0, keepdims=True)
        for part in range(2):
            parts[part][1] += more * flags[part]
        more = store(
            keys, probs, product, *(jnp.where(early, a, b) for a, b in zip(parts[0][1:], parts[1][1:]))
        )
        for part, pieces in enumerate(PARTS):
            found, delta, query_rows, grad_rows = parts[part]
            dq = more * flags[part]
            for (at, _), (probs, product) in zip(pieces, found):
                dq += store(pl.ds(at, BLOCK), probs, product, delta, query_rows, grad_rows)
            dq_ref[head, :, part * chunk : (part + 1) * chunk] = dq * scale
    dk_ref[0] = dk_acc[...].T
    dv_ref[0] = dv_acc[...].T


def attention_specs(tokens):
    heads = pl.BlockSpec((QPG, HD, tokens), lambda g, s: (g, 0, 0))
    keys = pl.BlockSpec((1, HD, LEN), lambda g, s: (g, 0, 0))
    sums = pl.BlockSpec((1, QPG, tokens), lambda g, s: (g, 0, 0))
    return heads, keys, sums


def attend(starts, queries, keys, values):
    tokens = queries.shape[2]
    heads, whole, sums = attention_specs(tokens)
    pairs = QH * (tokens // 2) * 5 * BLOCK
    return pl.pallas_call(
        attend_kernel,
        out_shape=(
            jax.ShapeDtypeStruct((QH, HD, tokens), low),
            jax.ShapeDtypeStruct((KVH, QPG, tokens), full),
        ),
        grid_spec=pltpu.PrefetchScalarGridSpec(
            num_scalar_prefetch=1,
            grid=(KVH,),
            in_specs=[heads, whole, whole],
            out_specs=[heads, sums],
            scratch_shapes=[pltpu.VMEM((LEN, HD), low)],
        ),
        compiler_params=pltpu.CompilerParams(vmem_limit_bytes=40 << 20),
        cost_estimate=pl.CostEstimate(
            flops=pairs, bytes_accessed=1 << 20, transcendentals=0
        ),
    )(starts, queries, keys, values)


def attend_back(starts, queries, keys, values, grads, sums_in):
    tokens = queries.shape[2]
    heads, whole, sums = attention_specs(tokens)
    pairs = QH * (tokens // 2) * 5 * BLOCK
    return pl.pallas_call(
        attend_back_kernel,
        out_shape=(
            jax.ShapeDtypeStruct((QH, HD, tokens), full),
            jax.ShapeDtypeStruct((KVH, HD, LEN), full),
            jax.ShapeDtypeStruct((KVH, HD, LEN), full),
        ),
        grid_spec=pltpu.PrefetchScalarGridSpec(
            num_scalar_prefetch=1,
            grid=(KVH,),
            in_specs=[heads, whole, whole, heads, sums],
            out_specs=[heads, whole, whole],
            scratch_shapes=[pltpu.VMEM((LEN, HD), kind) for kind in (full, full, low, low)],
        ),
        compiler_params=pltpu.CompilerParams(vmem_limit_bytes=40 << 20),
        cost_estimate=pl.CostEstimate(
            flops=pairs, bytes_accessed=1 << 20, transcendentals=0
        ),
    )(starts, queries, keys, values, grads, sums_in)


def by_ranks(wide, down, rank, parts):
    rows, units = wide.shape[0], wide.shape[1] // (2 * parts)
    place = lambda r: (rank - r) % parts
    if units % 128:
        blocks = jnp.concatenate(
            [a.reshape(rows, -1, parts, units) for a in (wide, down)], 1
        )
        blocks = jnp.transpose(blocks, (2, 0, 1, 3)).reshape(parts, rows, 3 * units)
        return jnp.stack([blocks[place(r)] for r in range(parts)])

    def kernel(index_ref, gate_ref, up_ref, down_ref, out_ref):
        for k, ref in enumerate((gate_ref, up_ref, down_ref)):
            out_ref[0, :, k * units : (k + 1) * units] = ref[...]

    def column(first):
        return pl.BlockSpec((rows, units), lambda r, index: (0, first + index[r]))

    return pl.pallas_call(
        kernel,
        out_shape=jax.ShapeDtypeStruct((parts, rows, 3 * units), low),
        grid_spec=pltpu.PrefetchScalarGridSpec(
            num_scalar_prefetch=1,
            grid=(parts,),
            in_specs=[column(0), column(parts), column(0)],
            out_specs=pl.BlockSpec((1, rows, 3 * units), lambda r, index: (r, 0, 0)),
        ),
        compiler_params=pltpu.CompilerParams(vmem_limit_bytes=32 << 20),
        cost_estimate=pl.CostEstimate(flops=0, bytes_accessed=1 << 16, transcendentals=0),
    )(place(jnp.arange(parts, dtype=jnp.int32)), wide, wide, down)


def widen_kernel(pack_ref, gate_out, up_out, down_out):
    units = gate_out.shape[1]
    gate_out[...] = pack_ref[0, :, :units].astype(full)
    up_out[...] = pack_ref[0, :, units : 2 * units].astype(full)
    down_out[...] = pack_ref[0, :, 2 * units :].astype(full).T


def widen(pack):
    groups, rows, columns = pack.shape
    units = columns // 3
    if units % 128:
        gate, up, down = (
            jnp.transpose(pack[:, :, k * units : (k + 1) * units], (1, 0, 2))
            .reshape(rows, -1)
            .astype(full)
            for k in range(3)
        )
        return gate, up, down.T
    shape = jax.ShapeDtypeStruct((rows, groups * units), full)
    column = pl.BlockSpec((rows, units), lambda g: (0, g))
    return pl.pallas_call(
        widen_kernel,
        out_shape=(shape, shape, jax.ShapeDtypeStruct((groups * units, rows), full)),
        grid=(groups,),
        in_specs=[pl.BlockSpec((1, rows, columns), lambda g: (g, 0, 0))],
        out_specs=[column, column, pl.BlockSpec((units, rows), lambda g: (g, 0))],
        compiler_params=pltpu.CompilerParams(vmem_limit_bytes=32 << 20),
        cost_estimate=pl.CostEstimate(flops=0, bytes_accessed=1 << 16, transcendentals=0),
    )(pack)


def split_kernel(in_ref, query_out, key_out, value_out):
    slots, width = query_out.shape[1], key_out.shape[0]
    array = in_ref[...].astype(full)
    query_out[...] = array[:, :slots]
    key_out[...] = array[:, slots : slots + width].T
    value_out[...] = array[:, slots + width : slots + 2 * width].T


def split_projections(array, slots, rows):
    width = KVH * HD
    if slots % 128 or rows % 128:
        array = array.astype(full)
        return array[:, :slots], array[:, slots:][:, :width], array[:, slots + width :][:, :width]
    turned = jax.ShapeDtypeStruct((width, array.shape[0]), full)
    column = pl.BlockSpec((width, rows), lambda g: (0, g))
    query, key, value = pl.pallas_call(
        split_kernel,
        out_shape=(jax.ShapeDtypeStruct((array.shape[0], slots), full), turned, turned),
        grid=(array.shape[0] // rows,),
        in_specs=[pl.BlockSpec((rows, array.shape[1]), lambda g: (g, 0))],
        out_specs=[pl.BlockSpec((rows, slots), lambda g: (g, 0)), column, column],
        compiler_params=pltpu.CompilerParams(vmem_limit_bytes=32 << 20),
        cost_estimate=pl.CostEstimate(flops=0, bytes_accessed=1 << 16, transcendentals=0),
    )(array)
    return query, key.T, value.T


def norm_backward(values, rms, gain, normed_grad):
    weighted = normed_grad * gain
    dotted = jnp.sum(weighted * values, axis=1, keepdims=True)
    grad = weighted * rms - values * (rms * rms * rms) * dotted / D
    return grad, jnp.sum(normed_grad * values * rms, axis=0)


def on_device(
    hidden_in,
    positions,
    head_counts,
    attention_gain,
    query_projection_weight,
    key_weight,
    value_weight,
    query_gain,
    key_gain,
    output_weight,
    feedforward_gain,
    gate_weight,
    up_weight,
    down_projection_weight,
    cotangent,
):
    groups = lax.axis_size("dp")
    parts = lax.axis_size("mp")
    group = lax.axis_index("dp")
    rank = lax.axis_index("mp")
    tokens, share = hidden_in.shape
    seqs = tokens // LEN
    ring = parts // seqs
    mine = tokens // parts
    chunk = mine // 2
    units = gate_weight.shape[1] // groups
    slots = query_projection_weight.shape[1]
    place = rank % ring
    ranks = range(parts)

    lower = jnp.arange(parts)[None, :] < jnp.arange(parts)[:, None]
    offsets = jnp.sum(jnp.where(lower, head_counts[None, :], 0), axis=1)

    def selection(order):
        within = jnp.arange(slots, dtype=jnp.int32)
        column = offsets[order][:, None] * HD + within[None, :]
        column = jnp.where(within[None, :] < head_counts[order][:, None] * HD, column, -1)
        return (
            column.reshape(-1)[:, None] == jnp.arange(QH * HD, dtype=jnp.int32)[None, :]
        ).astype(low)

    select_near = selection(rank ^ jnp.arange(parts, dtype=jnp.int32))
    select = selection(jnp.arange(parts, dtype=jnp.int32))

    def rows_of(array, other):
        base = (other // ring) * LEN
        at = other % ring
        first = lax.dynamic_slice_in_dim(array, base + at * chunk, chunk, 0)
        last = lax.dynamic_slice_in_dim(array, base + (2 * ring - 1 - at) * chunk, chunk, 0)
        return jnp.concatenate([first, last], 0)

    order = Order(head_counts)
    rows = D // groups
    heads_here = QH * HD // groups

    query_slice = lax.dynamic_slice_in_dim(query_projection_weight, group * rows, rows, 0)
    gains = jnp.stack([attention_gain, feedforward_gain])
    gains_high = gains.astype(low)
    gains_low = (gains - gains_high.astype(full)).astype(low)
    lines = -(-share // slots)
    gains = jnp.pad(
        jnp.concatenate([gains_high, gains_low], 0), ((0, 0), (0, lines * slots - share))
    )
    query_slice = jnp.concatenate([query_slice, gains.reshape(4 * lines, slots)], 0)
    query_slice = swap([query_slice] * parts, "mp")
    cosine, sine = rotary_tables(rows_of(positions, rank))
    chosen = lax.dynamic_slice_in_dim(select, group * heads_here, heads_here, 1)
    output_slice = dot(chosen, output_weight, 0, 0).astype(low)
    pack = jnp.concatenate(
        [
            lax.dynamic_slice_in_dim(gate_weight, group * units, units, 1),
            lax.dynamic_slice_in_dim(up_weight, group * units, units, 1),
            lax.dynamic_slice_in_dim(down_projection_weight, group * units, units, 0).T,
        ],
        1,
    )
    inputs = [rows_of(hidden_in, rank ^ k) for k in ranks]
    late = inputs[parts - 1]
    inputs = inputs[:1] + [exchange(inputs[k], "mp", k, parts) for k in range(1, parts - 1)]
    cotangent = [rows_of(cotangent, rank ^ k) for k in ranks]
    got = order(
        select_near, select, late, cosine, sine, output_slice, pack,
        *query_slice, *cotangent, *inputs
    )
    select_near, select, late, cosine, sine, output_slice, pack = got[:7]
    query_slice, cotangent = (got[7 + k * parts : 7 + (k + 1) * parts] for k in range(2))
    inputs = got[7 + 2 * parts :]

    inputs.append(exchange(late, "mp", parts - 1, parts))
    output_slice = swap([output_slice] * parts, "mp")
    gains = by_rank([piece[rows:].reshape(4, -1)[:, :share] for piece in query_slice], rank)
    gains = jnp.concatenate(gains, 1).astype(full)
    attention_gain_all, feedforward_gain_all = gains[0] + gains[2], gains[1] + gains[3]
    query_slice = jnp.concatenate([piece[:rows] for piece in query_slice], axis=1)
    query_slice = mm(query_slice, select_near).astype(low)
    query_all = lax.all_gather(query_slice, "dp", axis=0, tiled=True)
    got = order(*inputs, *output_slice)
    inputs, output_slice = got[:parts], got[parts:]

    inputs = jnp.concatenate(by_rank(inputs, rank), axis=1).astype(full)
    first_rms = lax.rsqrt(jnp.mean(inputs * inputs, axis=1, keepdims=True) + epsilon)
    normed = (inputs * first_rms * attention_gain_all).astype(low)
    keys = dot(key_weight, normed, 0, 1).reshape(KVH, HD, mine)
    values_mine = dot(value_weight, normed, 0, 1).astype(low).reshape(KVH, HD, mine)
    turned_keys, key_pull = jax.vjp(lambda v, g: turn(v, g, cosine, sine), keys, key_gain)
    pair_mine = jnp.concatenate([turned_keys.astype(low), values_mine], 0)
    pair_mine, normed = order(pair_mine, normed)

    near_pairs = [pair_mine] + [exchange(pair_mine, "mp", k, parts) for k in range(1, ring)]
    output_slice = jnp.concatenate(by_rank(output_slice, rank), axis=1)
    output_all = lax.all_gather(output_slice, "dp", axis=0, tiled=True)
    queries = dot(query_all, normed, 0, 1).reshape(QH, HD, mine)
    turned_queries, query_pull = jax.vjp(
        lambda v, g: turn(v, g, cosine, sine), queries, query_gain
    )
    got = order(turned_queries.astype(low), *near_pairs, *cotangent)
    turned_queries, near_pairs, cotangent = got[0], got[1 : ring + 1], got[ring + 1 :]

    cotangent = swap(cotangent, "mp")
    near_pairs = by_rank(near_pairs, place)
    pair = jnp.concatenate(
        [p[:, :, :chunk] for p in near_pairs] + [p[:, :, chunk:] for p in near_pairs[::-1]], axis=2
    )
    key_heads, value_heads = pair[:KVH], pair[KVH:]
    starts = jnp.stack([place * chunk, (2 * ring - 1 - place) * chunk]).astype(jnp.int32)
    mixed, row_totals = attend(starts, turned_queries, key_heads, value_heads)
    mixed = mixed.reshape(QH * HD, mine)
    middle = inputs + dot(mixed, output_all, 0, 0)
    second_rms = lax.rsqrt(jnp.mean(middle * middle, axis=1, keepdims=True) + epsilon)
    second_normed = (middle * second_rms * feedforward_gain_all).astype(low)
    second_normed, pack, *cotangent = order(second_normed, pack, *cotangent)

    second = Spread(second_normed, "dp", groups, group)
    weights = RelayGather(pack, "mp", parts)
    cotangent_mine = jnp.concatenate(by_rank(cotangent, rank), axis=1)
    cube = groups == CUBE
    if cube:
        flag = group % 2 != 0
        pairs = [normed[:, k * rows : (k + 1) * rows] for k in range(groups)]
        normed_own, normed_other = (
            jnp.concatenate(
                [jnp.where(flag, pairs[k ^ 1 ^ a], pairs[k ^ a]) for k in range(0, groups, 2)], 1
            )
            for a in (0, 1)
        )
        pairs = mixed.reshape(4, 2, heads_here, mine)
        mixed_own, mixed_other = (
            lax.dynamic_index_in_dim(pairs, at, 1, keepdims=False).reshape(-1, mine)
            for at in (group % 2, 1 - group % 2)
        )
    else:
        normed_own = normed_other = normed
        mixed_own = mixed_other = mixed
    *got, up, down, cotangent_mine, normed_own, normed_other, mixed_own, mixed_other = order(
        *second.flying, *weights.flying, cotangent_mine, normed_own, normed_other,
        mixed_own, mixed_other
    )
    second.second(*got)
    weights.take(up, down)
    cotangent_mine, got, (up, down), second.buffer = order_split(
        order, [cotangent_mine], second.flying, weights.flying, second.buffer
    )
    cotangent_full = lax.all_gather(cotangent_mine, "dp", axis=0, tiled=True)
    second.third(*got)
    weights.take(up, down)
    got, (up, down) = order_split(order, [], second.flying, weights.flying)
    second.last(*got)
    weights.take(up, down)
    pack = weights.finish(order)
    wide = jnp.concatenate(
        [block[:, :units] for block in pack] + [block[:, units : 2 * units] for block in pack], 1
    )
    down_here = jnp.concatenate([block[:, 2 * units :] for block in pack], 1)
    half = parts * units

    raised = [mm(part, wide) for part in second.parts]
    hidden = [
        (v[:, :half] * jax.nn.sigmoid(v[:, :half]) * v[:, half:]).astype(low) for v in raised
    ]
    down_terms = [dot(h, down_here, 1, 1).astype(low) for h in hidden]
    down_terms, raised, hidden, (cotangent_full,) = order_split(
        order, [], down_terms, raised, hidden, [cotangent_full]
    )
    def cores(array, at):
        if not cube:
            return array
        array = array.reshape(4, 2, mine, D)
        return lax.dynamic_index_in_dim(array, at, 1, keepdims=False).reshape(4 * mine, D)

    cot = [cores(cotangent_full, at) for at in ((group % 2, 1 - group % 2) if cube else (0,))]

    def back(part, v):
        hidden_grad = mm(part, down_here)
        gate, up = v[:, :half], v[:, half:]
        sigma = jax.nn.sigmoid(gate)
        gate_grad = hidden_grad * up * sigma * (1.0 + gate * (1.0 - sigma))
        return jnp.concatenate([gate_grad.astype(low), (hidden_grad * gate * sigma).astype(low)], 1)

    grads = [back(cot[-1], raised[-1])]
    other = dot(grads[0], wide, 1, 1).astype(low)
    other, grads[0], *raised = order(other, grads[0], *raised)

    second_sum = Collect(other, "dp", groups, group)
    own = other
    if len(raised) > 1:
        grads.insert(0, back(cot[0], raised[0]))
        own = dot(grads[0], wide, 1, 1).astype(low)
    own, *grads, hidden, got = order_split(order, [own, *grads], hidden, second_sum.flying)

    second_sum.second(own, *got)
    wide_grad = sum(dot(part, grad, 0, 0) for part, grad in zip(second.parts, grads)).astype(low)
    down_grad = sum(dot(part, h, 0, 0) for part, h in zip(cot, hidden)).astype(low)
    down_sum = Collect(down_terms[-1], "dp", groups, group)
    down_grad, wide_grad, got, flying = order_split(
        order, [down_grad, wide_grad], second_sum.flying, down_sum.flying
    )

    second_sum.third(*got)

    pack = by_ranks(wide_grad, down_grad, rank, parts)
    pack = lax.psum_scatter(pack, "mp", scatter_dimension=0, tiled=False)
    down_sum.second(down_terms[0], *flying, apart=True)
    *got, flying = order_split(order, second_sum.flying, down_sum.flying)

    normed_two_grad = second_sum.last(*got).astype(full)
    down_sum.launch(*flying)
    middle_part, feedforward_gain_grad = norm_backward(
        middle, second_rms, feedforward_gain_all, normed_two_grad
    )
    middle_grad = cotangent_mine.astype(full) + middle_part
    lane = lax.broadcasted_iota(jnp.int32, (D, EXTRA), 1)
    wide_extra = jnp.where(lane == 0, feedforward_gain_grad[:, None], 0.0)
    branch_grad = middle_grad.astype(low)
    mixed_grad = dot(output_all, branch_grad, 1, 1).astype(low).reshape(QH, HD, mine)
    output_other = mm(mixed_other, branch_grad).astype(low)
    output_own = mm(mixed_own, branch_grad).astype(low) if cube else output_other
    output_sum = Collect(output_other, "dp", groups, group)
    query_rot_grad, key_rot_grad, value_grad = attend_back(
        starts, turned_queries, key_heads, value_heads, mixed_grad, row_totals
    )
    pair_grad = jnp.concatenate([key_rot_grad, value_grad], 0)
    blocks = [
        jnp.concatenate(
            [
                pair_grad[:, :, j * chunk : (j + 1) * chunk],
                pair_grad[:, :, (2 * ring - 1 - j) * chunk : (2 * ring - j) * chunk],
            ],
            axis=2,
        )
        for j in range(ring)
    ]
    blocks = by_rank(blocks, place)
    away = [block.astype(low) for block in blocks[1:]]
    query_rot_grad, output_own, *away, got, flying = order_split(
        order, [query_rot_grad, output_own, *away], down_sum.flying, output_sum.flying
    )
    down_sum.third(*got)
    output_sum.second(output_own, *flying)

    away = [exchange(block, "mp", k + 1, parts) for k, block in enumerate(away)]
    queries_low, query_gain_grad = query_pull(query_rot_grad)
    queries_low = queries_low.astype(low).reshape(QH * HD, mine)
    queries_low, pack, wide_extra, *away, out_relayed, got = order_split(
        order, [queries_low, pack, wide_extra, *away], down_sum.flying, output_sum.flying
    )
    output_sum.third(*got)
    pack = by_rows(lax.all_gather(by_rows(pack), "dp", axis=0, tiled=False))
    pair_grad = sum([blocks[0]] + [block.astype(full) for block in away])
    keys_grad, key_gain_grad = key_pull(pair_grad[:KVH])
    pair_low = jnp.concatenate(
        [keys_grad.astype(low), pair_grad[KVH:].astype(low)], 0
    ).reshape(2 * KVH * HD, mine)
    all_low = jnp.concatenate([queries_low, pair_low], 0)
    heads_gain = jnp.stack([query_gain_grad, key_gain_grad])
    top = wide_extra[:2] + jnp.pad(heads_gain, ((0, 0), (EXTRA - HD, 0)))
    extra = jnp.concatenate([top, wide_extra[2:]], 0)
    wide_low = jnp.concatenate([all_low, jnp.zeros((EXTRA, mine), low)], 0)

    def projections(normed_part, extra_part):
        extra_part = jnp.pad(extra_part, ((0, 0), (wide_low.shape[0] - EXTRA, 0)))
        return (dot(normed_part, wide_low, 0, 1) + extra_part).astype(low)

    own = other = extra
    if cube:
        pairs = extra.reshape(4, 2, rows, EXTRA)
        own, other = (
            lax.dynamic_index_in_dim(pairs, at, 1, keepdims=False).reshape(4 * rows, EXTRA)
            for at in (group % 2, 1 - group % 2)
        )
    other = projections(normed_other, other)
    other, own, wide_low, all_low, normed_own = order(other, own, wide_low, all_low, normed_own)

    def by_feature(array):
        return by_rank([array[:, j * share : (j + 1) * share] for j in ranks], rank)

    projection_sum = Collect(other, "dp", groups, group)
    own = projections(normed_own, own) if cube else other
    queries_low, pair_low = all_low[: QH * HD], all_low[QH * HD :]
    normed_grad = (
        dot(queries_low, query_all, 0, 1)
        + dot(pair_low[: KVH * HD], key_weight, 0, 1)
        + dot(pair_low[KVH * HD :], value_weight, 0, 1)
    )
    input_part, _ = norm_backward(
        inputs, first_rms, attention_gain_all, normed_grad
    )
    input_gradient = (middle_grad + input_part).astype(low)
    input_gradient, own, got, flying = order_split(
        order, [input_gradient, own], projection_sum.flying, output_sum.flying
    )
    projection_sum.second(own, *got)
    output_grad = output_sum.last(*flying)

    def by_tokens(got, kind):
        got = by_rank(got, rank)
        rows = []
        for seq in range(seqs):
            near = got[seq * ring : (seq + 1) * ring]
            rows += [block[:chunk] for block in near]
            rows += [block[chunk:] for block in near[::-1]]
        return jnp.concatenate(rows, 0).astype(kind)

    input_gradient = swap(by_feature(input_gradient), "mp")
    input_gradient, got, out_relayed = order_split(
        order, [], input_gradient, projection_sum.flying, out_relayed
    )
    projection_sum.third(*got)

    output_grad = swap(by_feature(output_grad), "mp")
    output_grad, got, out_relayed = order_split(
        order, [], output_grad, projection_sum.flying, out_relayed
    )
    output_grad = lax.all_gather(added(*output_grad), "dp", axis=0, tiled=True)
    projection_total = projection_sum.last(*got)
    down_sum.fourth(*out_relayed)

    query_total, pair_total, extra = jnp.split(
        projection_total, [QH * HD, (QH + 2 * KVH) * HD], axis=1
    )
    here = lambda weight: lax.dynamic_slice_in_dim(weight, group * rows, rows, 0).astype(full)
    product = jnp.sum(here(query_all) * query_total.astype(full), axis=1)
    product += jnp.sum(here(key_weight) * pair_total[:, : KVH * HD].astype(full), axis=1)
    product += jnp.sum(here(value_weight) * pair_total[:, KVH * HD :].astype(full), axis=1)
    product = product / lax.dynamic_slice_in_dim(attention_gain_all, group * rows, rows, 0)
    column = lax.broadcasted_iota(jnp.int32, extra.shape, 1)
    extra = jnp.where(column == 2, product[:, None].astype(low), extra)
    query_part = dot(query_total, select_near, 1, 1).astype(low)
    projection = swap(
        [
            jnp.concatenate([query_part[:, k * slots : (k + 1) * slots], pair_total, extra], 1)
            for k in ranks
        ],
        "mp",
    )
    pack, projection, flying = order_split(order, [pack], projection, down_sum.flying)

    projection = lax.all_gather(added(*projection), "dp", axis=0, tiled=True)
    output_weight_grad = mm(select, output_grad)
    output = (middle + down_sum.last(*flying).astype(full)).astype(low)
    output = swap(by_feature(output), "mp")
    gate_weight_grad, up_weight_grad, down_weight_grad = widen(pack)
    input_gradient = by_tokens(input_gradient, full)
    got = order(
        gate_weight_grad, up_weight_grad, down_weight_grad, input_gradient, output_weight_grad,
        *output
    )
    gate_weight_grad, up_weight_grad, down_weight_grad, input_gradient = got[:4]
    output_weight_grad = got[4]
    output = by_tokens(got[5:], low)
    query_weight_grad, key_weight_grad, value_weight_grad = split_projections(
        projection, slots, rows
    )
    extra = projection[:, slots + 2 * KVH * HD :]
    extra = extra.astype(full)
    own_share = lax.dynamic_slice_in_dim(extra, rank * share, share, 0)
    return (
        output,
        input_gradient,
        own_share[:, 2],
        query_weight_grad.astype(full),
        key_weight_grad.astype(full),
        value_weight_grad.astype(full),
        extra[0, EXTRA - HD :],
        extra[1, EXTRA - HD :],
        output_weight_grad,
        own_share[:, 0],
        gate_weight_grad,
        up_weight_grad,
        down_weight_grad,
    )


def solution(mesh):
    in_specs = (
        P("dp", "mp"),
        P("dp"),
        P(),
        P("mp"),
        P(None, "mp"),
        P(),
        P(),
        P(),
        P(),
        P(None, "mp"),
        P("mp"),
        P(None, "mp"),
        P(None, "mp"),
        P("mp", None),
        P("dp", "mp"),
    )
    out_specs = (
        P("dp", "mp"),
        P("dp", "mp"),
        P("mp"),
        P(None, "mp"),
        P(),
        P(),
        P(),
        P(),
        P(None, "mp"),
        P("mp"),
        P(None, "mp"),
        P(None, "mp"),
        P("mp", None),
    )
    return jax.shard_map(
        on_device, mesh=mesh, in_specs=in_specs, out_specs=out_specs, check_vma=False
    )
```

```python
import functools
import math

import jax
import jax.numpy as jnp
from jax import lax
from jax.experimental.layout import Layout, with_layout_constraint
from jax.experimental import pallas as pl
from jax.experimental.pallas import tpu as pltpu
from jax.sharding import PartitionSpec as P

D = 2048
QH = 20
KVH = 5
QPG = QH // KVH
HD = 64
LEN = 1024

epsilon = 1e-05
rope_base = 10000.0
masked_score = -1e30
low = jnp.bfloat16
full = jnp.float32


def dot(left, right, left_axis, right_axis):
    return lax.dot_general(
        left, right, (((left_axis,), (right_axis,)), ((), ())), preferred_element_type=full
    )


def swap(pieces, axis):
    n = len(pieces)
    return [pieces[0]] + [
        lax.ppermute(pieces[k], axis, [(i, i ^ k) for i in range(n)]) for k in range(1, n)
    ]


def by_rank(blocks, rank):
    bit = 1
    while bit < len(blocks):
        flag = (rank & bit) != 0
        blocks = [jnp.where(flag, blocks[j ^ bit], blocks[j]) for j in range(len(blocks))]
        bit *= 2
    return blocks


def exchange(array, axis, mask, n):
    return lax.ppermute(array, axis, [(i, i ^ mask) for i in range(n)])


def by_rows(array):
    return with_layout_constraint(array, Layout(tuple(range(array.ndim))))


def added(*terms):
    return sum(term.astype(full) for term in terms).astype(low)


class Order:
    def __init__(self, token):
        self.token = token

    def __call__(self, *arrays):
        self.token, *arrays = lax.optimization_barrier((self.token, *arrays))
        return arrays


class RelayGather:
    def __init__(self, piece, axis, n):
        self.axis, self.n, self.step, self.own = axis, n, 1, piece
        self.ups, self.downs = [], []
        self.send(piece, piece)

    def send(self, up, down):
        n, step = self.n, self.step
        right = [(i, i + 1) for i in range(step - 1, n - 1)]
        left = [(i, i - 1) for i in range(n - step, 0, -1)]
        self.flying = [lax.ppermute(up, self.axis, right), lax.ppermute(down, self.axis, left)]

    def take(self, up, down):
        self.ups.append(up)
        self.downs.append(down)
        self.step += 1
        if self.step < self.n:
            self.send(up, down)

    def finish(self, order):
        while self.step < self.n:
            self.take(*order(*self.flying))
        n = self.n
        return [self.own] + [self.ups[k - 1] + self.downs[n - k - 1] for k in range(1, n)]


CUBE = 8


def at_index(array, index):
    return lax.dynamic_index_in_dim(array, index, 0, keepdims=False)


class Spread:
    def __init__(self, piece, axis, n, group):
        self.axis, self.n, self.chip, self.piece = axis, n, group // 2, piece
        if n == CUBE:
            self.flying = [self.move(piece, 2), self.move(piece, 4)]
        else:
            self.flying = [lax.all_gather(piece, axis, axis=0, tiled=True)]
        self.buffer = []

    def move(self, array, mask):
        return exchange(array, self.axis, mask, self.n)

    def second(self, *got):
        self.flying = got
        if self.n == CUBE:
            near, far = got
            half = self.piece.shape[0] // 2
            self.flying = [self.move(near[:half], 4), self.move(far[half:], 2)]
            mine = jnp.zeros((4, *self.piece.shape), self.piece.dtype)
            for k, block in enumerate((self.piece, near, far)):
                mine = lax.dynamic_update_slice(mine, block[None], (self.chip ^ k, 0, 0))
            self.buffer = [mine]

    def third(self, *got):
        if self.n != CUBE:
            self.parts, self.flying = list(got), []
            return
        rows = self.piece.shape[0]
        (mine,) = self.buffer
        for k, block in enumerate(got):
            mine = lax.dynamic_update_slice(
                mine, block[None], (self.chip ^ 3, k * (rows // 2), 0)
            )
        mine = mine.reshape(4 * rows, -1)
        self.parts = [mine]
        self.flying = [self.move(mine, 1)]

    def last(self, *got):
        self.parts += got


TOGETHER = (((3, 0), (1, 0)), ((3, 1), (2, 1)), ((0, 0), (0, 1), (2, 0), (1, 1)))
APART = (((3, 0),), ((3, 1),), ((1, 0),), ((2, 1),), ((0, 0), (0, 1), (2, 0), (1, 1)))


def chip_sums(mine, got, chip, plan):
    half, columns = mine.shape[0] // 8, mine.shape[1]
    flat = [place for places in plan for place in places]
    index = jnp.stack([(chip ^ block) * 2 + part for block, part in flat]).astype(jnp.int32)
    firsts = [sum(len(places) for places in plan[:k]) for k in range(len(plan))]

    def kernel(index_ref, mine_ref, got_ref, *outs):
        step = pl.program_id(0)
        total = (mine_ref[...].astype(full) + got_ref[...].astype(full)).astype(low)
        for first, places, out in zip(firsts, plan, outs):

            @pl.when((step >= first) & (step < first + len(places)))
            def _():
                out[...] = total

    source = pl.BlockSpec((half, columns), lambda g, index: (index[g], 0))

    def target(first, count):
        return pl.BlockSpec(
            (half, columns), lambda g, index: (jnp.clip(g - first, 0, count - 1), 0)
        )

    return pl.pallas_call(
        kernel,
        out_shape=[
            jax.ShapeDtypeStruct((len(places) * half, columns), low) for places in plan
        ],
        grid_spec=pltpu.PrefetchScalarGridSpec(
            num_scalar_prefetch=1,
            grid=(len(flat),),
            in_specs=[source, source],
            out_specs=[target(f, len(places)) for f, places in zip(firsts, plan)],
        ),
        compiler_params=pltpu.CompilerParams(vmem_limit_bytes=40 << 20),
        cost_estimate=pl.CostEstimate(flops=0, bytes_accessed=1 << 16, transcendentals=0),
    )(index, mine, got)


class Collect:
    def __init__(self, other, axis, n, group):
        self.axis, self.n, self.chip = axis, n, group // 2
        if n == CUBE:
            self.flying = [self.move(other, 1)]
        else:
            self.flying = [lax.psum_scatter(other, axis, scatter_dimension=0, tiled=True)]

    def move(self, array, mask):
        return exchange(array, self.axis, mask, self.n)

    def second(self, mine, *got, apart=False):
        self.flying, self.held = got, []
        if self.n != CUBE:
            return
        self.half = mine.shape[0] // 8
        *sent, self.keep = chip_sums(mine, got[0], self.chip, APART if apart else TOGETHER)
        self.apart = apart
        if apart:
            self.flying, self.held = sent[:2], sent[2:]
        else:
            self.launch(*sent)

    def launch(self, *ready):
        self.flying = ready
        if self.n == CUBE:
            self.flying = [self.move(ready[0], 2), self.move(ready[1], 4)]

    def third(self, *got):
        self.flying = got
        if self.n != CUBE:
            return
        half = self.half
        if not self.apart:
            self.direct = [got[0][half:], got[1][half:]]
        self.flying = [
            self.move(added(self.keep[2 * half : 3 * half], got[0][:half]), 4),
            self.move(added(self.keep[3 * half :], got[1][:half]), 2),
        ]

    def fourth(self, *got):
        self.flying = got
        if self.n == CUBE:
            self.relayed = got
            self.flying = [self.move(self.held[0], 2), self.move(self.held[1], 4)]

    def last(self, *got):
        if self.n != CUBE:
            return got[0]
        half = self.half
        direct, got = (got, self.relayed) if self.apart else (self.direct, got)
        return jnp.concatenate(
            [
                added(self.keep[:half], direct[0], got[0]),
                added(self.keep[half : 2 * half], direct[1], got[1]),
            ],
            0,
        )


EXTRA = 128


def order_split(order, first, *lists):
    first = list(first)
    got = order(*first, *[array for arrays in lists for array in arrays])
    result, at = list(got[: len(first)]), len(first)
    for arrays in lists:
        result.append(list(got[at : at + len(arrays)]))
        at += len(arrays)
    return result


def rotary_tables(positions):
    half = HD // 2
    inverse = jnp.exp(-math.log(rope_base) * (2.0 * jnp.arange(half, dtype=full)) / HD)
    angles = inverse[:, None] * positions.astype(full)[None, :]
    cosine, sine = jnp.cos(angles), jnp.sin(angles)
    return jnp.concatenate([cosine, cosine], 0), jnp.concatenate([sine, sine], 0)


def turn(raw, gain, cosine, sine):
    half = HD // 2
    rms = lax.rsqrt(jnp.mean(raw * raw, axis=1, keepdims=True) + epsilon)
    normed = raw * rms * gain[None, :, None]
    turned = jnp.concatenate([-normed[:, half:], normed[:, :half]], axis=1)
    return normed * cosine[None] + turned * sine[None]


def mm(left, right):
    return jnp.dot(left, right, preferred_element_type=full)


BLOCK = LEN // 4
PARTS = (((0, True),), ((0, False), (BLOCK, False), (2 * BLOCK, True)))


def scores_of(key, query, lead):
    scores = mm(key, query)
    if lead is None:
        return scores
    rows = lax.broadcasted_iota(jnp.int32, scores.shape, 0)
    cols = lax.broadcasted_iota(jnp.int32, scores.shape, 1)
    return jnp.where(rows - cols <= lead, scores, masked_score)


def last_piece(starts, chunk):
    early = starts[0] >= BLOCK
    at = pl.multiple_of(jnp.where(early, BLOCK, 3 * BLOCK), BLOCK)
    span = pl.multiple_of(jnp.where(early, 0, chunk), 128)
    start = jnp.where(early, starts[0], starts[1])
    flag = jnp.where(early, 1.0, 0.0).astype(full)
    return early, pl.ds(at, BLOCK), pl.ds(span, chunk), start - at, (flag, 1.0 - flag)


def rows_kept(array):
    return array.astype(full).T.astype(low)


def attend_kernel(starts, q_ref, k_ref, v_ref, o_ref, sums_ref, key_ref):
    chunk = q_ref.shape[2] // 2
    scale = jnp.asarray(1.0 / math.sqrt(HD), low)
    key_ref[...] = rows_kept(k_ref[0])
    early, keys, columns, lead, flags = last_piece(starts, chunk)
    for head in range(QPG):
        scores, peaks = [], []
        for part, pieces in enumerate(PARTS):
            query = q_ref[head, :, part * chunk : (part + 1) * chunk] * scale
            scores.append(
                [
                    scores_of(key_ref[at : at + BLOCK], query, starts[part] - at if cut else None)
                    for at, cut in pieces
                ]
            )
            peaks.append(
                functools.reduce(
                    jnp.maximum, [jnp.max(s, axis=0, keepdims=True) for s in scores[-1]]
                )
            )
        more = scores_of(key_ref[keys], q_ref[head, :, columns] * scale, lead)
        peak = jnp.max(more, axis=0, keepdims=True)
        peaks = [
            jnp.maximum(peaks[0], jnp.where(early, peak, masked_score)),
            jnp.maximum(peaks[1], jnp.where(early, masked_score, peak)),
        ]
        more = jnp.exp(more - jnp.where(early, peaks[0], peaks[1]))
        more_total = jnp.sum(more, axis=0, keepdims=True)
        more_result = mm(v_ref[0, :, keys], more.astype(low))
        for part, pieces in enumerate(PARTS):
            total = more_total * flags[part]
            result = more_result * flags[part]
            for (at, _), s in zip(pieces, scores[part]):
                weights = jnp.exp(s - peaks[part])
                total += jnp.sum(weights, axis=0, keepdims=True)
                result += mm(v_ref[0, :, at : at + BLOCK], weights.astype(low))
            span = pl.ds(part * chunk, chunk)
            o_ref[head, :, span] = (result / total).astype(low)
            sums_ref[0, head : head + 1, span] = peaks[part] + jnp.log(total)


def attend_back_kernel(
    starts, q_ref, k_ref, v_ref, g_ref, sums_ref, dq_ref, dk_ref, dv_ref, dk_acc, dv_acc,
    key_ref, value_ref
):
    chunk = q_ref.shape[2] // 2
    scale = 1.0 / math.sqrt(HD)
    key_ref[...] = rows_kept(k_ref[0])
    value_ref[...] = rows_kept(v_ref[0])
    dk_acc[...] = jnp.zeros_like(dk_acc)
    dv_acc[...] = jnp.zeros_like(dv_acc)
    early, keys, columns, lead, flags = last_piece(starts, chunk)

    def products(at, query, grad, sums, lead):
        probs = jnp.exp(scores_of(key_ref[at], query, lead) - sums)
        return probs, probs * mm(value_ref[at], grad)

    def store(at, probs, product, delta, query_rows, grad_rows):
        score_grad = (product - probs * delta).astype(low)
        dk_acc[at, :] += mm(score_grad, query_rows)
        dv_acc[at, :] += mm(probs.astype(low), grad_rows)
        return mm(k_ref[0, :, at], score_grad)

    for head in range(QPG):
        parts = []
        for part, pieces in enumerate(PARTS):
            span = pl.ds(part * chunk, chunk)
            query = q_ref[head, :, span] * jnp.asarray(scale, low)
            grad = g_ref[head, :, span]
            sums = sums_ref[0, head : head + 1, span]
            found = [
                products(
                    pl.ds(at, BLOCK), query, grad, sums, starts[part] - at if cut else None
                )
                for at, cut in pieces
            ]
            delta = sum(jnp.sum(product, axis=0, keepdims=True) for _, product in found)
            parts.append([found, delta, rows_kept(query), rows_kept(grad)])
        probs, product = products(
            keys,
            q_ref[head, :, columns] * jnp.asarray(scale, low),
            g_ref[head, :, columns],
            sums_ref[0, head : head + 1, columns],
            lead,
        )
        more = jnp.sum(product, axis=0, keepdims=True)
        for part in range(2):
            parts[part][1] += more * flags[part]
        more = store(
            keys, probs, product, *(jnp.where(early, a, b) for a, b in zip(parts[0][1:], parts[1][1:]))
        )
        for part, pieces in enumerate(PARTS):
            found, delta, query_rows, grad_rows = parts[part]
            dq = more * flags[part]
            for (at, _), (probs, product) in zip(pieces, found):
                dq += store(pl.ds(at, BLOCK), probs, product, delta, query_rows, grad_rows)
            dq_ref[head, :, part * chunk : (part + 1) * chunk] = dq * scale
    dk_ref[0] = dk_acc[...].T
    dv_ref[0] = dv_acc[...].T


def attention_specs(tokens):
    heads = pl.BlockSpec((QPG, HD, tokens), lambda g, s: (g, 0, 0))
    keys = pl.BlockSpec((1, HD, LEN), lambda g, s: (g, 0, 0))
    sums = pl.BlockSpec((1, QPG, tokens), lambda g, s: (g, 0, 0))
    return heads, keys, sums


def attend(starts, queries, keys, values):
    tokens = queries.shape[2]
    heads, whole, sums = attention_specs(tokens)
    pairs = QH * (tokens // 2) * 5 * BLOCK
    return pl.pallas_call(
        attend_kernel,
        out_shape=(
            jax.ShapeDtypeStruct((QH, HD, tokens), low),
            jax.ShapeDtypeStruct((KVH, QPG, tokens), full),
        ),
        grid_spec=pltpu.PrefetchScalarGridSpec(
            num_scalar_prefetch=1,
            grid=(KVH,),
            in_specs=[heads, whole, whole],
            out_specs=[heads, sums],
            scratch_shapes=[pltpu.VMEM((LEN, HD), low)],
        ),
        compiler_params=pltpu.CompilerParams(vmem_limit_bytes=40 << 20),
        cost_estimate=pl.CostEstimate(
            flops=pairs, bytes_accessed=1 << 20, transcendentals=0
        ),
    )(starts, queries, keys, values)


def attend_back(starts, queries, keys, values, grads, sums_in):
    tokens = queries.shape[2]
    heads, whole, sums = attention_specs(tokens)
    pairs = QH * (tokens // 2) * 5 * BLOCK
    return pl.pallas_call(
        attend_back_kernel,
        out_shape=(
            jax.ShapeDtypeStruct((QH, HD, tokens), full),
            jax.ShapeDtypeStruct((KVH, HD, LEN), full),
            jax.ShapeDtypeStruct((KVH, HD, LEN), full),
        ),
        grid_spec=pltpu.PrefetchScalarGridSpec(
            num_scalar_prefetch=1,
            grid=(KVH,),
            in_specs=[heads, whole, whole, heads, sums],
            out_specs=[heads, whole, whole],
            scratch_shapes=[pltpu.VMEM((LEN, HD), kind) for kind in (full, full, low, low)],
        ),
        compiler_params=pltpu.CompilerParams(vmem_limit_bytes=40 << 20),
        cost_estimate=pl.CostEstimate(
            flops=pairs, bytes_accessed=1 << 20, transcendentals=0
        ),
    )(starts, queries, keys, values, grads, sums_in)


def gates_back(hidden_grad, raised):
    half = raised.shape[1] // 2
    gate, up = raised[:, :half], raised[:, half:]
    sigma = jax.nn.sigmoid(gate)
    gate_grad = hidden_grad * up * sigma * (1.0 + gate * (1.0 - sigma))
    return gate_grad.astype(low), (hidden_grad * gate * sigma).astype(low)


def units_back_whole(cotangent, raised, down, wide):
    grad = jnp.concatenate(gates_back(mm(cotangent, down), raised), 1)
    return grad, dot(grad, wide, 1, 1).astype(low)


def units_back_kernel(core, cot_ref, raised_ref, down_ref, wide_ref, grad_ref, out_ref):
    half = down_ref.shape[1]
    gate_grad, up_grad = gates_back(mm(cot_ref[0, 0], down_ref[...]), raised_ref[...])
    grad_ref[:, :half] = gate_grad
    grad_ref[:, half:] = up_grad
    out_ref[...] = dot(grad_ref[...], wide_ref[...], 1, 1).astype(low)


def units_back(cotangent, core, raised, down, wide):
    rows, columns = raised.shape[0] // 4, raised.shape[1]
    width = cotangent.shape[1]
    once = lambda array: pl.BlockSpec(
        array.shape, lambda g, core: (0, 0), pipeline_mode=pl.Buffered(1)
    )
    return pl.pallas_call(
        units_back_kernel,
        out_shape=(
            jax.ShapeDtypeStruct(raised.shape, low),
            jax.ShapeDtypeStruct((4 * rows, width), low),
        ),
        grid_spec=pltpu.PrefetchScalarGridSpec(
            num_scalar_prefetch=1,
            grid=(4,),
            in_specs=[
                pl.BlockSpec((1, 1, rows, width), lambda g, core: (g, core[0], 0, 0)),
                pl.BlockSpec((rows, columns), lambda g, core: (g, 0)),
                once(down),
                once(wide),
            ],
            out_specs=[
                pl.BlockSpec((rows, columns), lambda g, core: (g, 0)),
                pl.BlockSpec((rows, width), lambda g, core: (g, 0)),
            ],
        ),
        compiler_params=pltpu.CompilerParams(vmem_limit_bytes=44 << 20),
        cost_estimate=pl.CostEstimate(flops=0, bytes_accessed=1 << 16, transcendentals=0),
    )(core.astype(jnp.int32).reshape(1), cotangent.reshape(4, 2, rows, width), raised, down, wide)


def by_ranks(wide, down, rank, parts):
    rows, units = wide.shape[0], wide.shape[1] // (2 * parts)
    place = lambda r: (rank - r) % parts
    if units % 128:
        blocks = jnp.concatenate(
            [a.reshape(rows, -1, parts, units) for a in (wide, down)], 1
        )
        blocks = jnp.transpose(blocks, (2, 0, 1, 3)).reshape(parts, rows, 3 * units)
        return jnp.stack([blocks[place(r)] for r in range(parts)])

    def kernel(index_ref, gate_ref, up_ref, down_ref, out_ref):
        for k, ref in enumerate((gate_ref, up_ref, down_ref)):
            out_ref[0, :, k * units : (k + 1) * units] = ref[...]

    def column(first):
        return pl.BlockSpec((rows, units), lambda r, index: (0, first + index[r]))

    return pl.pallas_call(
        kernel,
        out_shape=jax.ShapeDtypeStruct((parts, rows, 3 * units), low),
        grid_spec=pltpu.PrefetchScalarGridSpec(
            num_scalar_prefetch=1,
            grid=(parts,),
            in_specs=[column(0), column(parts), column(0)],
            out_specs=pl.BlockSpec((1, rows, 3 * units), lambda r, index: (r, 0, 0)),
        ),
        compiler_params=pltpu.CompilerParams(vmem_limit_bytes=32 << 20),
        cost_estimate=pl.CostEstimate(flops=0, bytes_accessed=1 << 16, transcendentals=0),
    )(place(jnp.arange(parts, dtype=jnp.int32)), wide, wide, down)


def widen_kernel(pack_ref, gate_out, up_out, down_out):
    units = gate_out.shape[1]
    gate_out[...] = pack_ref[0, :, :units].astype(full)
    up_out[...] = pack_ref[0, :, units : 2 * units].astype(full)
    down_out[...] = pack_ref[0, :, 2 * units :].astype(full).T


def widen(pack):
    groups, rows, columns = pack.shape
    units = columns // 3
    if units % 128:
        gate, up, down = (
            jnp.transpose(pack[:, :, k * units : (k + 1) * units], (1, 0, 2))
            .reshape(rows, -1)
            .astype(full)
            for k in range(3)
        )
        return gate, up, down.T
    shape = jax.ShapeDtypeStruct((rows, groups * units), full)
    column = pl.BlockSpec((rows, units), lambda g: (0, g))
    return pl.pallas_call(
        widen_kernel,
        out_shape=(shape, shape, jax.ShapeDtypeStruct((groups * units, rows), full)),
        grid=(groups,),
        in_specs=[pl.BlockSpec((1, rows, columns), lambda g: (g, 0, 0))],
        out_specs=[column, column, pl.BlockSpec((units, rows), lambda g: (g, 0))],
        compiler_params=pltpu.CompilerParams(vmem_limit_bytes=32 << 20),
        cost_estimate=pl.CostEstimate(flops=0, bytes_accessed=1 << 16, transcendentals=0),
    )(pack)


def split_kernel(in_ref, query_out, key_out, value_out):
    slots, width = query_out.shape[1], key_out.shape[0]
    array = in_ref[...].astype(full)
    query_out[...] = array[:, :slots]
    key_out[...] = array[:, slots : slots + width].T
    value_out[...] = array[:, slots + width : slots + 2 * width].T


def split_projections(array, slots, rows):
    width = KVH * HD
    if slots % 128 or rows % 128:
        array = array.astype(full)
        return array[:, :slots], array[:, slots:][:, :width], array[:, slots + width :][:, :width]
    turned = jax.ShapeDtypeStruct((width, array.shape[0]), full)
    column = pl.BlockSpec((width, rows), lambda g: (0, g))
    query, key, value = pl.pallas_call(
        split_kernel,
        out_shape=(jax.ShapeDtypeStruct((array.shape[0], slots), full), turned, turned),
        grid=(array.shape[0] // rows,),
        in_specs=[pl.BlockSpec((rows, array.shape[1]), lambda g: (g, 0))],
        out_specs=[pl.BlockSpec((rows, slots), lambda g: (g, 0)), column, column],
        compiler_params=pltpu.CompilerParams(vmem_limit_bytes=32 << 20),
        cost_estimate=pl.CostEstimate(flops=0, bytes_accessed=1 << 16, transcendentals=0),
    )(array)
    return query, key.T, value.T


def norm_backward(values, rms, gain, normed_grad):
    weighted = normed_grad * gain
    dotted = jnp.sum(weighted * values, axis=1, keepdims=True)
    grad = weighted * rms - values * (rms * rms * rms) * dotted / D
    return grad, jnp.sum(normed_grad * values * rms, axis=0)


def on_device(
    hidden_in,
    positions,
    head_counts,
    attention_gain,
    query_projection_weight,
    key_weight,
    value_weight,
    query_gain,
    key_gain,
    output_weight,
    feedforward_gain,
    gate_weight,
    up_weight,
    down_projection_weight,
    cotangent,
):
    groups = lax.axis_size("dp")
    parts = lax.axis_size("mp")
    group = lax.axis_index("dp")
    rank = lax.axis_index("mp")
    tokens, share = hidden_in.shape
    seqs = tokens // LEN
    ring = parts // seqs
    mine = tokens // parts
    chunk = mine // 2
    units = gate_weight.shape[1] // groups
    slots = query_projection_weight.shape[1]
    place = rank % ring
    ranks = range(parts)

    lower = jnp.arange(parts)[None, :] < jnp.arange(parts)[:, None]
    offsets = jnp.sum(jnp.where(lower, head_counts[None, :], 0), axis=1)

    def selection(order):
        within = jnp.arange(slots, dtype=jnp.int32)
        column = offsets[order][:, None] * HD + within[None, :]
        column = jnp.where(within[None, :] < head_counts[order][:, None] * HD, column, -1)
        return (
            column.reshape(-1)[:, None] == jnp.arange(QH * HD, dtype=jnp.int32)[None, :]
        ).astype(low)

    select_near = selection(rank ^ jnp.arange(parts, dtype=jnp.int32))
    select = selection(jnp.arange(parts, dtype=jnp.int32))

    def rows_of(array, other):
        base = (other // ring) * LEN
        at = other % ring
        first = lax.dynamic_slice_in_dim(array, base + at * chunk, chunk, 0)
        last = lax.dynamic_slice_in_dim(array, base + (2 * ring - 1 - at) * chunk, chunk, 0)
        return jnp.concatenate([first, last], 0)

    order = Order(head_counts)
    rows = D // groups
    heads_here = QH * HD // groups

    query_slice = lax.dynamic_slice_in_dim(query_projection_weight, group * rows, rows, 0)
    gains = jnp.stack([attention_gain, feedforward_gain])
    gains_high = gains.astype(low)
    gains_low = (gains - gains_high.astype(full)).astype(low)
    lines = -(-share // slots)
    gains = jnp.pad(
        jnp.concatenate([gains_high, gains_low], 0), ((0, 0), (0, lines * slots - share))
    )
    query_slice = jnp.concatenate([query_slice, gains.reshape(4 * lines, slots)], 0)
    query_slice = swap([query_slice] * parts, "mp")
    cosine, sine = rotary_tables(rows_of(positions, rank))
    chosen = lax.dynamic_slice_in_dim(select, group * heads_here, heads_here, 1)
    output_slice = dot(chosen, output_weight, 0, 0).astype(low)
    pack = jnp.concatenate(
        [
            lax.dynamic_slice_in_dim(gate_weight, group * units, units, 1),
            lax.dynamic_slice_in_dim(up_weight, group * units, units, 1),
            lax.dynamic_slice_in_dim(down_projection_weight, group * units, units, 0).T,
        ],
        1,
    )
    inputs = [rows_of(hidden_in, rank ^ k) for k in ranks]
    late = inputs[parts - 1]
    inputs = inputs[:1] + [exchange(inputs[k], "mp", k, parts) for k in range(1, parts - 1)]
    cotangent = [rows_of(cotangent, rank ^ k) for k in ranks]
    got = order(
        select_near, select, late, cosine, sine, output_slice, pack,
        *query_slice, *cotangent, *inputs
    )
    select_near, select, late, cosine, sine, output_slice, pack = got[:7]
    query_slice, cotangent = (got[7 + k * parts : 7 + (k + 1) * parts] for k in range(2))
    inputs = got[7 + 2 * parts :]

    inputs.append(exchange(late, "mp", parts - 1, parts))
    output_slice = swap([output_slice] * parts, "mp")
    gains = by_rank([piece[rows:].reshape(4, -1)[:, :share] for piece in query_slice], rank)
    gains = jnp.concatenate(gains, 1).astype(full)
    attention_gain_all, feedforward_gain_all = gains[0] + gains[2], gains[1] + gains[3]
    query_slice = jnp.concatenate([piece[:rows] for piece in query_slice], axis=1)
    query_slice = mm(query_slice, select_near).astype(low)
    query_all = lax.all_gather(query_slice, "dp", axis=0, tiled=True)
    got = order(*inputs, *output_slice)
    inputs, output_slice = got[:parts], got[parts:]

    inputs = jnp.concatenate(by_rank(inputs, rank), axis=1).astype(full)
    first_rms = lax.rsqrt(jnp.mean(inputs * inputs, axis=1, keepdims=True) + epsilon)
    normed = (inputs * first_rms * attention_gain_all).astype(low)
    keys = dot(key_weight, normed, 0, 1).reshape(KVH, HD, mine)
    values_mine = dot(value_weight, normed, 0, 1).astype(low).reshape(KVH, HD, mine)
    turned_keys, key_pull = jax.vjp(lambda v, g: turn(v, g, cosine, sine), keys, key_gain)
    pair_mine = jnp.concatenate([turned_keys.astype(low), values_mine], 0)
    pair_mine, normed = order(pair_mine, normed)

    near_pairs = [pair_mine] + [exchange(pair_mine, "mp", k, parts) for k in range(1, ring)]
    output_slice = jnp.concatenate(by_rank(output_slice, rank), axis=1)
    output_all = lax.all_gather(output_slice, "dp", axis=0, tiled=True)
    queries = dot(query_all, normed, 0, 1).reshape(QH, HD, mine)
    turned_queries, query_pull = jax.vjp(
        lambda v, g: turn(v, g, cosine, sine), queries, query_gain
    )
    got = order(turned_queries.astype(low), *near_pairs, *cotangent)
    turned_queries, near_pairs, cotangent = got[0], got[1 : ring + 1], got[ring + 1 :]

    cotangent = swap(cotangent, "mp")
    near_pairs = by_rank(near_pairs, place)
    pair = jnp.concatenate(
        [p[:, :, :chunk] for p in near_pairs] + [p[:, :, chunk:] for p in near_pairs[::-1]], axis=2
    )
    key_heads, value_heads = pair[:KVH], pair[KVH:]
    starts = jnp.stack([place * chunk, (2 * ring - 1 - place) * chunk]).astype(jnp.int32)
    mixed, row_totals = attend(starts, turned_queries, key_heads, value_heads)
    mixed = mixed.reshape(QH * HD, mine)
    middle = inputs + dot(mixed, output_all, 0, 0)
    second_rms = lax.rsqrt(jnp.mean(middle * middle, axis=1, keepdims=True) + epsilon)
    second_normed = (middle * second_rms * feedforward_gain_all).astype(low)
    second_normed, pack, *cotangent = order(second_normed, pack, *cotangent)

    second = Spread(second_normed, "dp", groups, group)
    weights = RelayGather(pack, "mp", parts)
    cotangent_mine = jnp.concatenate(by_rank(cotangent, rank), axis=1)
    cube = groups == CUBE
    if cube:
        flag = group % 2 != 0
        pairs = [normed[:, k * rows : (k + 1) * rows] for k in range(groups)]
        normed_own, normed_other = (
            jnp.concatenate(
                [jnp.where(flag, pairs[k ^ 1 ^ a], pairs[k ^ a]) for k in range(0, groups, 2)], 1
            )
            for a in (0, 1)
        )
        pairs = mixed.reshape(4, 2, heads_here, mine)
        mixed_own, mixed_other = (
            lax.dynamic_index_in_dim(pairs, at, 1, keepdims=False).reshape(-1, mine)
            for at in (group % 2, 1 - group % 2)
        )
    else:
        normed_own = normed_other = normed
        mixed_own = mixed_other = mixed
    *got, up, down, cotangent_mine, normed_own, normed_other, mixed_own, mixed_other = order(
        *second.flying, *weights.flying, cotangent_mine, normed_own, normed_other,
        mixed_own, mixed_other
    )
    second.second(*got)
    weights.take(up, down)
    cotangent_mine, got, (up, down), second.buffer = order_split(
        order, [cotangent_mine], second.flying, weights.flying, second.buffer
    )
    cotangent_full = lax.all_gather(cotangent_mine, "dp", axis=0, tiled=True)
    second.third(*got)
    weights.take(up, down)
    got, (up, down) = order_split(order, [], second.flying, weights.flying)
    second.last(*got)
    weights.take(up, down)
    pack = weights.finish(order)
    wide = jnp.concatenate(
        [block[:, :units] for block in pack] + [block[:, units : 2 * units] for block in pack], 1
    )
    down_here = jnp.concatenate([block[:, 2 * units :] for block in pack], 1)
    half = parts * units

    raised = [mm(part, wide) for part in second.parts]
    hidden = [
        (v[:, :half] * jax.nn.sigmoid(v[:, :half]) * v[:, half:]).astype(low) for v in raised
    ]
    down_terms = [dot(h, down_here, 1, 1).astype(low) for h in hidden]
    down_terms, raised, hidden, (cotangent_full,) = order_split(
        order, [], down_terms, raised, hidden, [cotangent_full]
    )

    core = group % 2
    if cube:
        back = lambda at, v: units_back(cotangent_full, at, v, down_here, wide)
    else:
        back = lambda at, v: units_back_whole(cotangent_full, v, down_here, wide)
    grad, other = back(1 - core, raised[-1])
    grads = [grad]
    other, grads[0], *raised = order(other, grads[0], *raised)

    second_sum = Collect(other, "dp", groups, group)
    own = other
    if len(raised) > 1:
        grad, own = back(core, raised[0])
        grads.insert(0, grad)
    own, *grads, hidden, got = order_split(order, [own, *grads], hidden, second_sum.flying)

    second_sum.second(own, *got)
    wide_grad = sum(dot(part, grad, 0, 0) for part, grad in zip(second.parts, grads)).astype(low)
    if cube:
        shape = (4, 1, mine, half)
        first, last = (h.reshape(shape) for h in hidden)
        hidden_full = jnp.concatenate(
            [jnp.where(core == 0, first, last), jnp.where(core == 0, last, first)], 1
        ).reshape(2 * 4 * mine, half)
    else:
        hidden_full = hidden[0]
    down_grad = dot(cotangent_full, hidden_full, 0, 0).astype(low)
    down_sum = Collect(down_terms[-1], "dp", groups, group)
    down_grad, wide_grad, got, flying = order_split(
        order, [down_grad, wide_grad], second_sum.flying, down_sum.flying
    )

    second_sum.third(*got)

    pack = by_ranks(wide_grad, down_grad, rank, parts)
    pack = lax.psum_scatter(pack, "mp", scatter_dimension=0, tiled=False)
    down_sum.second(down_terms[0], *flying, apart=True)
    *got, flying = order_split(order, second_sum.flying, down_sum.flying)

    normed_two_grad = second_sum.last(*got).astype(full)
    down_sum.launch(*flying)
    middle_part, feedforward_gain_grad = norm_backward(
        middle, second_rms, feedforward_gain_all, normed_two_grad
    )
    middle_grad = cotangent_mine.astype(full) + middle_part
    lane = lax.broadcasted_iota(jnp.int32, (D, EXTRA), 1)
    wide_extra = jnp.where(lane == 0, feedforward_gain_grad[:, None], 0.0)
    branch_grad = middle_grad.astype(low)
    mixed_grad = dot(output_all, branch_grad, 1, 1).astype(low).reshape(QH, HD, mine)
    output_other = mm(mixed_other, branch_grad).astype(low)
    output_own = mm(mixed_own, branch_grad).astype(low) if cube else output_other
    output_sum = Collect(output_other, "dp", groups, group)
    query_rot_grad, key_rot_grad, value_grad = attend_back(
        starts, turned_queries, key_heads, value_heads, mixed_grad, row_totals
    )
    pair_grad = jnp.concatenate([key_rot_grad, value_grad], 0)
    blocks = [
        jnp.concatenate(
            [
                pair_grad[:, :, j * chunk : (j + 1) * chunk],
                pair_grad[:, :, (2 * ring - 1 - j) * chunk : (2 * ring - j) * chunk],
            ],
            axis=2,
        )
        for j in range(ring)
    ]
    blocks = by_rank(blocks, place)
    away = [block.astype(low) for block in blocks[1:]]
    query_rot_grad, output_own, *away, got, flying = order_split(
        order, [query_rot_grad, output_own, *away], down_sum.flying, output_sum.flying
    )
    down_sum.third(*got)
    output_sum.second(output_own, *flying)

    away = [exchange(block, "mp", k + 1, parts) for k, block in enumerate(away)]
    queries_low, query_gain_grad = query_pull(query_rot_grad)
    queries_low = queries_low.astype(low).reshape(QH * HD, mine)
    queries_low, pack, wide_extra, *away, out_relayed, got = order_split(
        order, [queries_low, pack, wide_extra, *away], down_sum.flying, output_sum.flying
    )
    output_sum.third(*got)
    pack = by_rows(lax.all_gather(by_rows(pack), "dp", axis=0, tiled=False))
    pair_grad = sum([blocks[0]] + [block.astype(full) for block in away])
    keys_grad, key_gain_grad = key_pull(pair_grad[:KVH])
    pair_low = jnp.concatenate(
        [keys_grad.astype(low), pair_grad[KVH:].astype(low)], 0
    ).reshape(2 * KVH * HD, mine)
    all_low = jnp.concatenate([queries_low, pair_low], 0)
    heads_gain = jnp.stack([query_gain_grad, key_gain_grad])
    top = wide_extra[:2] + jnp.pad(heads_gain, ((0, 0), (EXTRA - HD, 0)))
    extra = jnp.concatenate([top, wide_extra[2:]], 0)
    wide_low = jnp.concatenate([all_low, jnp.zeros((EXTRA, mine), low)], 0)

    def projections(normed_part, extra_part):
        extra_part = jnp.pad(extra_part, ((0, 0), (wide_low.shape[0] - EXTRA, 0)))
        return (dot(normed_part, wide_low, 0, 1) + extra_part).astype(low)

    own = other = extra
    if cube:
        pairs = extra.reshape(4, 2, rows, EXTRA)
        own, other = (
            lax.dynamic_index_in_dim(pairs, at, 1, keepdims=False).reshape(4 * rows, EXTRA)
            for at in (group % 2, 1 - group % 2)
        )
    other = projections(normed_other, other)
    other, own, wide_low, all_low, normed_own = order(other, own, wide_low, all_low, normed_own)

    def by_feature(array):
        return by_rank([array[:, j * share : (j + 1) * share] for j in ranks], rank)

    projection_sum = Collect(other, "dp", groups, group)
    own = projections(normed_own, own) if cube else other
    queries_low, pair_low = all_low[: QH * HD], all_low[QH * HD :]
    normed_grad = (
        dot(queries_low, query_all, 0, 1)
        + dot(pair_low[: KVH * HD], key_weight, 0, 1)
        + dot(pair_low[KVH * HD :], value_weight, 0, 1)
    )
    input_part, _ = norm_backward(
        inputs, first_rms, attention_gain_all, normed_grad
    )
    input_gradient = (middle_grad + input_part).astype(low)
    input_gradient, own, got, flying = order_split(
        order, [input_gradient, own], projection_sum.flying, output_sum.flying
    )
    projection_sum.second(own, *got)
    output_grad = output_sum.last(*flying)

    def by_tokens(got, kind):
        got = by_rank(got, rank)
        rows = []
        for seq in range(seqs):
            near = got[seq * ring : (seq + 1) * ring]
            rows += [block[:chunk] for block in near]
            rows += [block[chunk:] for block in near[::-1]]
        return jnp.concatenate(rows, 0).astype(kind)

    input_gradient = swap(by_feature(input_gradient), "mp")
    input_gradient, got, out_relayed = order_split(
        order, [], input_gradient, projection_sum.flying, out_relayed
    )
    projection_sum.third(*got)

    output_grad = swap(by_feature(output_grad), "mp")
    output_grad, got, out_relayed = order_split(
        order, [], output_grad, projection_sum.flying, out_relayed
    )
    output_grad = lax.all_gather(added(*output_grad), "dp", axis=0, tiled=True)
    projection_total = projection_sum.last(*got)
    down_sum.fourth(*out_relayed)

    query_total, pair_total, extra = jnp.split(
        projection_total, [QH * HD, (QH + 2 * KVH) * HD], axis=1
    )
    here = lambda weight: lax.dynamic_slice_in_dim(weight, group * rows, rows, 0).astype(full)
    product = jnp.sum(here(query_all) * query_total.astype(full), axis=1)
    product += jnp.sum(here(key_weight) * pair_total[:, : KVH * HD].astype(full), axis=1)
    product += jnp.sum(here(value_weight) * pair_total[:, KVH * HD :].astype(full), axis=1)
    product = product / lax.dynamic_slice_in_dim(attention_gain_all, group * rows, rows, 0)
    column = lax.broadcasted_iota(jnp.int32, extra.shape, 1)
    extra = jnp.where(column == 2, product[:, None].astype(low), extra)
    query_part = dot(query_total, select_near, 1, 1).astype(low)
    projection = swap(
        [
            jnp.concatenate([query_part[:, k * slots : (k + 1) * slots], pair_total, extra], 1)
            for k in ranks
        ],
        "mp",
    )
    pack, projection, flying = order_split(order, [pack], projection, down_sum.flying)

    projection = lax.all_gather(added(*projection), "dp", axis=0, tiled=True)
    output_weight_grad = mm(select, output_grad)
    output = (middle + down_sum.last(*flying).astype(full)).astype(low)
    output = swap(by_feature(output), "mp")
    gate_weight_grad, up_weight_grad, down_weight_grad = widen(pack)
    input_gradient = by_tokens(input_gradient, full)
    got = order(
        gate_weight_grad, up_weight_grad, down_weight_grad, input_gradient, output_weight_grad,
        *output
    )
    gate_weight_grad, up_weight_grad, down_weight_grad, input_gradient = got[:4]
    output_weight_grad = got[4]
    output = by_tokens(got[5:], low)
    query_weight_grad, key_weight_grad, value_weight_grad = split_projections(
        projection, slots, rows
    )
    extra = projection[:, slots + 2 * KVH * HD :]
    extra = extra.astype(full)
    own_share = lax.dynamic_slice_in_dim(extra, rank * share, share, 0)
    return (
        output,
        input_gradient,
        own_share[:, 2],
        query_weight_grad.astype(full),
        key_weight_grad.astype(full),
        value_weight_grad.astype(full),
        extra[0, EXTRA - HD :],
        extra[1, EXTRA - HD :],
        output_weight_grad,
        own_share[:, 0],
        gate_weight_grad,
        up_weight_grad,
        down_weight_grad,
    )


def solution(mesh):
    in_specs = (
        P("dp", "mp"),
        P("dp"),
        P(),
        P("mp"),
        P(None, "mp"),
        P(),
        P(),
        P(),
        P(),
        P(None, "mp"),
        P("mp"),
        P(None, "mp"),
        P(None, "mp"),
        P("mp", None),
        P("dp", "mp"),
    )
    out_specs = (
        P("dp", "mp"),
        P("dp", "mp"),
        P("mp"),
        P(None, "mp"),
        P(),
        P(),
        P(),
        P(),
        P(None, "mp"),
        P("mp"),
        P(None, "mp"),
        P(None, "mp"),
        P("mp", None),
    )
    return jax.shard_map(
        on_device, mesh=mesh, in_specs=in_specs, out_specs=out_specs, check_vma=False
    )
```

```python
import functools
import math

import jax
import jax.numpy as jnp
from jax import lax
from jax.experimental.layout import Layout, with_layout_constraint
from jax.experimental import pallas as pl
from jax.experimental.pallas import tpu as pltpu
from jax.sharding import PartitionSpec as P

D = 2048
QH = 20
KVH = 5
QPG = QH // KVH
HD = 64
LEN = 1024

epsilon = 1e-05
rope_base = 10000.0
masked_score = -1e30
low = jnp.bfloat16
full = jnp.float32


def dot(left, right, left_axis, right_axis):
    return lax.dot_general(
        left, right, (((left_axis,), (right_axis,)), ((), ())), preferred_element_type=full
    )


def swap(pieces, axis):
    n = len(pieces)
    return [pieces[0]] + [
        lax.ppermute(pieces[k], axis, [(i, i ^ k) for i in range(n)]) for k in range(1, n)
    ]


def by_rank(blocks, rank):
    bit = 1
    while bit < len(blocks):
        flag = (rank & bit) != 0
        blocks = [jnp.where(flag, blocks[j ^ bit], blocks[j]) for j in range(len(blocks))]
        bit *= 2
    return blocks


def exchange(array, axis, mask, n):
    return lax.ppermute(array, axis, [(i, i ^ mask) for i in range(n)])


def by_rows(array):
    return with_layout_constraint(array, Layout(tuple(range(array.ndim))))


def added(*terms):
    return sum(term.astype(full) for term in terms).astype(low)


class Order:
    def __init__(self, token):
        self.token = token

    def __call__(self, *arrays):
        self.token, *arrays = lax.optimization_barrier((self.token, *arrays))
        return arrays


class RelayGather:
    def __init__(self, piece, axis, n):
        self.axis, self.n, self.step, self.own = axis, n, 1, piece
        self.ups, self.downs = [], []
        self.send(piece, piece)

    def send(self, up, down):
        n, step = self.n, self.step
        right = [(i, i + 1) for i in range(step - 1, n - 1)]
        left = [(i, i - 1) for i in range(n - step, 0, -1)]
        self.flying = [lax.ppermute(up, self.axis, right), lax.ppermute(down, self.axis, left)]

    def take(self, up, down):
        self.ups.append(up)
        self.downs.append(down)
        self.step += 1
        if self.step < self.n:
            self.send(up, down)

    def finish(self, order):
        while self.step < self.n:
            self.take(*order(*self.flying))
        n = self.n
        return [self.own] + [self.ups[k - 1] + self.downs[n - k - 1] for k in range(1, n)]


CUBE = 8


def at_index(array, index):
    return lax.dynamic_index_in_dim(array, index, 0, keepdims=False)


class Spread:
    def __init__(self, piece, axis, n, group):
        self.axis, self.n, self.chip, self.piece = axis, n, group // 2, piece
        if n == CUBE:
            self.flying = [self.move(piece, 2), self.move(piece, 4)]
        else:
            self.flying = [lax.all_gather(piece, axis, axis=0, tiled=True)]
        self.buffer = []

    def move(self, array, mask):
        return exchange(array, self.axis, mask, self.n)

    def second(self, *got):
        self.flying = got
        if self.n == CUBE:
            near, far = got
            half = self.piece.shape[0] // 2
            self.flying = [self.move(near[:half], 4), self.move(far[half:], 2)]
            mine = jnp.zeros((4, *self.piece.shape), self.piece.dtype)
            for k, block in enumerate((self.piece, near, far)):
                mine = lax.dynamic_update_slice(mine, block[None], (self.chip ^ k, 0, 0))
            self.buffer = [mine]

    def third(self, *got):
        if self.n != CUBE:
            self.parts, self.flying = list(got), []
            return
        rows = self.piece.shape[0]
        (mine,) = self.buffer
        for k, block in enumerate(got):
            mine = lax.dynamic_update_slice(
                mine, block[None], (self.chip ^ 3, k * (rows // 2), 0)
            )
        mine = mine.reshape(4 * rows, -1)
        self.parts = [mine]
        self.flying = [self.move(mine, 1)]

    def last(self, *got):
        self.parts += got


TOGETHER = (((3, 0), (1, 0)), ((3, 1), (2, 1)), ((0, 0), (0, 1), (2, 0), (1, 1)))
APART = (((3, 0),), ((3, 1),), ((1, 0),), ((2, 1),), ((0, 0), (0, 1), (2, 0), (1, 1)))


def chip_sums(mine, got, chip, plan):
    half, columns = mine.shape[0] // 8, mine.shape[1]
    flat = [place for places in plan for place in places]
    index = jnp.stack([(chip ^ block) * 2 + part for block, part in flat]).astype(jnp.int32)
    firsts = [sum(len(places) for places in plan[:k]) for k in range(len(plan))]

    def kernel(index_ref, mine_ref, got_ref, *outs):
        step = pl.program_id(0)
        total = (mine_ref[...].astype(full) + got_ref[...].astype(full)).astype(low)
        for first, places, out in zip(firsts, plan, outs):

            @pl.when((step >= first) & (step < first + len(places)))
            def _():
                out[...] = total

    source = pl.BlockSpec((half, columns), lambda g, index: (index[g], 0))

    def target(first, count):
        return pl.BlockSpec(
            (half, columns), lambda g, index: (jnp.clip(g - first, 0, count - 1), 0)
        )

    return pl.pallas_call(
        kernel,
        out_shape=[
            jax.ShapeDtypeStruct((len(places) * half, columns), low) for places in plan
        ],
        grid_spec=pltpu.PrefetchScalarGridSpec(
            num_scalar_prefetch=1,
            grid=(len(flat),),
            in_specs=[source, source],
            out_specs=[target(f, len(places)) for f, places in zip(firsts, plan)],
        ),
        compiler_params=pltpu.CompilerParams(vmem_limit_bytes=40 << 20),
        cost_estimate=pl.CostEstimate(flops=0, bytes_accessed=1 << 16, transcendentals=0),
    )(index, mine, got)


class Collect:
    def __init__(self, other, axis, n, group):
        self.axis, self.n, self.chip = axis, n, group // 2
        if n == CUBE:
            self.flying = [self.move(other, 1)]
        else:
            self.flying = [lax.psum_scatter(other, axis, scatter_dimension=0, tiled=True)]

    def move(self, array, mask):
        return exchange(array, self.axis, mask, self.n)

    def second(self, mine, *got, apart=False):
        self.flying, self.held = got, []
        if self.n != CUBE:
            return
        self.half = mine.shape[0] // 8
        *sent, self.keep = chip_sums(mine, got[0], self.chip, APART if apart else TOGETHER)
        self.apart = apart
        if apart:
            self.flying, self.held = sent[:2], sent[2:]
        else:
            self.launch(*sent)

    def launch(self, *ready):
        self.flying = ready
        if self.n == CUBE:
            self.flying = [self.move(ready[0], 2), self.move(ready[1], 4)]

    def third(self, *got):
        self.flying = got
        if self.n != CUBE:
            return
        half = self.half
        if not self.apart:
            self.direct = [got[0][half:], got[1][half:]]
        self.flying = [
            self.move(added(self.keep[2 * half : 3 * half], got[0][:half]), 4),
            self.move(added(self.keep[3 * half :], got[1][:half]), 2),
        ]

    def fourth(self, *got):
        self.flying = got
        if self.n == CUBE:
            self.relayed = got
            self.flying = [self.move(self.held[0], 2), self.move(self.held[1], 4)]

    def last(self, *got):
        if self.n != CUBE:
            return got[0]
        half = self.half
        direct, got = (got, self.relayed) if self.apart else (self.direct, got)
        return jnp.concatenate(
            [
                added(self.keep[:half], direct[0], got[0]),
                added(self.keep[half : 2 * half], direct[1], got[1]),
            ],
            0,
        )


EXTRA = 128


def order_split(order, first, *lists):
    first = list(first)
    got = order(*first, *[array for arrays in lists for array in arrays])
    result, at = list(got[: len(first)]), len(first)
    for arrays in lists:
        result.append(list(got[at : at + len(arrays)]))
        at += len(arrays)
    return result


def rotary_tables(positions):
    half = HD // 2
    inverse = jnp.exp(-math.log(rope_base) * (2.0 * jnp.arange(half, dtype=full)) / HD)
    angles = inverse[:, None] * positions.astype(full)[None, :]
    cosine, sine = jnp.cos(angles), jnp.sin(angles)
    return jnp.concatenate([cosine, cosine], 0), jnp.concatenate([sine, sine], 0)


def turn(raw, gain, cosine, sine):
    half = HD // 2
    rms = lax.rsqrt(jnp.mean(raw * raw, axis=1, keepdims=True) + epsilon)
    normed = raw * rms * gain[None, :, None]
    turned = jnp.concatenate([-normed[:, half:], normed[:, :half]], axis=1)
    return normed * cosine[None] + turned * sine[None]


def mm(left, right):
    return jnp.dot(left, right, preferred_element_type=full)


BLOCK = LEN // 4
PARTS = (((0, True),), ((0, False), (BLOCK, False), (2 * BLOCK, True)))


def scores_of(key, query, lead):
    scores = mm(key, query)
    if lead is None:
        return scores
    rows = lax.broadcasted_iota(jnp.int32, scores.shape, 0)
    cols = lax.broadcasted_iota(jnp.int32, scores.shape, 1)
    return jnp.where(rows - cols <= lead, scores, masked_score)


def last_piece(starts, chunk):
    early = starts[0] >= BLOCK
    at = pl.multiple_of(jnp.where(early, BLOCK, 3 * BLOCK), BLOCK)
    span = pl.multiple_of(jnp.where(early, 0, chunk), 128)
    start = jnp.where(early, starts[0], starts[1])
    flag = jnp.where(early, 1.0, 0.0).astype(full)
    return early, pl.ds(at, BLOCK), pl.ds(span, chunk), start - at, (flag, 1.0 - flag)


def rows_kept(array):
    return array.astype(full).T.astype(low)


def attend_kernel(starts, q_ref, k_ref, v_ref, o_ref, sums_ref, key_ref):
    chunk = q_ref.shape[2] // 2
    scale = jnp.asarray(1.0 / math.sqrt(HD), low)
    key_ref[...] = rows_kept(k_ref[0])
    early, keys, columns, lead, flags = last_piece(starts, chunk)
    for head in range(QPG):
        scores, peaks = [], []
        for part, pieces in enumerate(PARTS):
            query = q_ref[head, :, part * chunk : (part + 1) * chunk] * scale
            scores.append(
                [
                    scores_of(key_ref[at : at + BLOCK], query, starts[part] - at if cut else None)
                    for at, cut in pieces
                ]
            )
            peaks.append(
                functools.reduce(
                    jnp.maximum, [jnp.max(s, axis=0, keepdims=True) for s in scores[-1]]
                )
            )
        more = scores_of(key_ref[keys], q_ref[head, :, columns] * scale, lead)
        peak = jnp.max(more, axis=0, keepdims=True)
        peaks = [
            jnp.maximum(peaks[0], jnp.where(early, peak, masked_score)),
            jnp.maximum(peaks[1], jnp.where(early, masked_score, peak)),
        ]
        more = jnp.exp(more - jnp.where(early, peaks[0], peaks[1]))
        more_total = jnp.sum(more, axis=0, keepdims=True)
        more_result = mm(v_ref[0, :, keys], more.astype(low))
        for part, pieces in enumerate(PARTS):
            total = more_total * flags[part]
            result = more_result * flags[part]
            for (at, _), s in zip(pieces, scores[part]):
                weights = jnp.exp(s - peaks[part])
                total += jnp.sum(weights, axis=0, keepdims=True)
                result += mm(v_ref[0, :, at : at + BLOCK], weights.astype(low))
            span = pl.ds(part * chunk, chunk)
            o_ref[head, :, span] = (result / total).astype(low)
            sums_ref[0, head : head + 1, span] = peaks[part] + jnp.log(total)


def attend_back_kernel(
    starts, q_ref, k_ref, v_ref, g_ref, sums_ref, dq_ref, dk_ref, dv_ref, dk_acc, dv_acc,
    key_ref, value_ref
):
    chunk = q_ref.shape[2] // 2
    scale = 1.0 / math.sqrt(HD)
    key_ref[...] = rows_kept(k_ref[0])
    value_ref[...] = rows_kept(v_ref[0])
    dk_acc[...] = jnp.zeros_like(dk_acc)
    dv_acc[...] = jnp.zeros_like(dv_acc)
    early, keys, columns, lead, flags = last_piece(starts, chunk)

    def products(at, query, grad, sums, lead):
        probs = jnp.exp(scores_of(key_ref[at], query, lead) - sums)
        return probs, probs * mm(value_ref[at], grad)

    def store(at, probs, product, delta, query_rows, grad_rows):
        score_grad = (product - probs * delta).astype(low)
        dk_acc[at, :] += mm(score_grad, query_rows)
        dv_acc[at, :] += mm(probs.astype(low), grad_rows)
        return mm(k_ref[0, :, at], score_grad)

    for head in range(QPG):
        parts = []
        for part, pieces in enumerate(PARTS):
            span = pl.ds(part * chunk, chunk)
            query = q_ref[head, :, span] * jnp.asarray(scale, low)
            grad = g_ref[head, :, span]
            sums = sums_ref[0, head : head + 1, span]
            found = [
                products(
                    pl.ds(at, BLOCK), query, grad, sums, starts[part] - at if cut else None
                )
                for at, cut in pieces
            ]
            delta = sum(jnp.sum(product, axis=0, keepdims=True) for _, product in found)
            parts.append([found, delta, rows_kept(query), rows_kept(grad)])
        probs, product = products(
            keys,
            q_ref[head, :, columns] * jnp.asarray(scale, low),
            g_ref[head, :, columns],
            sums_ref[0, head : head + 1, columns],
            lead,
        )
        more = jnp.sum(product, axis=0, keepdims=True)
        for part in range(2):
            parts[part][1] += more * flags[part]
        more = store(
            keys, probs, product, *(jnp.where(early, a, b) for a, b in zip(parts[0][1:], parts[1][1:]))
        )
        for part, pieces in enumerate(PARTS):
            found, delta, query_rows, grad_rows = parts[part]
            dq = more * flags[part]
            for (at, _), (probs, product) in zip(pieces, found):
                dq += store(pl.ds(at, BLOCK), probs, product, delta, query_rows, grad_rows)
            dq_ref[head, :, part * chunk : (part + 1) * chunk] = dq * scale
    dk_ref[0] = dk_acc[...].T
    dv_ref[0] = dv_acc[...].T


def attention_specs(tokens):
    heads = pl.BlockSpec((QPG, HD, tokens), lambda g, s: (g, 0, 0))
    keys = pl.BlockSpec((1, HD, LEN), lambda g, s: (g, 0, 0))
    sums = pl.BlockSpec((1, QPG, tokens), lambda g, s: (g, 0, 0))
    return heads, keys, sums


def attend(starts, queries, keys, values):
    tokens = queries.shape[2]
    heads, whole, sums = attention_specs(tokens)
    pairs = QH * (tokens // 2) * 5 * BLOCK
    return pl.pallas_call(
        attend_kernel,
        out_shape=(
            jax.ShapeDtypeStruct((QH, HD, tokens), low),
            jax.ShapeDtypeStruct((KVH, QPG, tokens), full),
        ),
        grid_spec=pltpu.PrefetchScalarGridSpec(
            num_scalar_prefetch=1,
            grid=(KVH,),
            in_specs=[heads, whole, whole],
            out_specs=[heads, sums],
            scratch_shapes=[pltpu.VMEM((LEN, HD), low)],
        ),
        compiler_params=pltpu.CompilerParams(vmem_limit_bytes=40 << 20),
        cost_estimate=pl.CostEstimate(
            flops=pairs, bytes_accessed=1 << 20, transcendentals=0
        ),
    )(starts, queries, keys, values)


def attend_back(starts, queries, keys, values, grads, sums_in):
    tokens = queries.shape[2]
    heads, whole, sums = attention_specs(tokens)
    pairs = QH * (tokens // 2) * 5 * BLOCK
    return pl.pallas_call(
        attend_back_kernel,
        out_shape=(
            jax.ShapeDtypeStruct((QH, HD, tokens), full),
            jax.ShapeDtypeStruct((KVH, HD, LEN), full),
            jax.ShapeDtypeStruct((KVH, HD, LEN), full),
        ),
        grid_spec=pltpu.PrefetchScalarGridSpec(
            num_scalar_prefetch=1,
            grid=(KVH,),
            in_specs=[heads, whole, whole, heads, sums],
            out_specs=[heads, whole, whole],
            scratch_shapes=[pltpu.VMEM((LEN, HD), kind) for kind in (full, full, low, low)],
        ),
        compiler_params=pltpu.CompilerParams(vmem_limit_bytes=40 << 20),
        cost_estimate=pl.CostEstimate(
            flops=pairs, bytes_accessed=1 << 20, transcendentals=0
        ),
    )(starts, queries, keys, values, grads, sums_in)


def compact_kernel(*refs):
    *pieces, select_ref, out_ref = refs
    rows, slots = out_ref.shape[0], pieces[0].shape[1]
    out_ref[...] = sum(
        mm(piece[:rows, :], select_ref[k * slots : (k + 1) * slots, :])
        for k, piece in enumerate(pieces)
    ).astype(low)


def compact(pieces, select, rows):
    if pieces[0].shape[1] % 128:
        joined = jnp.concatenate([piece[:rows] for piece in pieces], axis=1)
        return mm(joined, select).astype(low)
    return pl.pallas_call(
        compact_kernel,
        out_shape=jax.ShapeDtypeStruct((rows, select.shape[1]), low),
        compiler_params=pltpu.CompilerParams(vmem_limit_bytes=32 << 20),
        cost_estimate=pl.CostEstimate(flops=0, bytes_accessed=1 << 16, transcendentals=0),
    )(*pieces, select)


def gates_back(hidden_grad, raised):
    half = raised.shape[1] // 2
    gate, up = raised[:, :half], raised[:, half:]
    sigma = jax.nn.sigmoid(gate)
    gate_grad = hidden_grad * up * sigma * (1.0 + gate * (1.0 - sigma))
    return gate_grad.astype(low), (hidden_grad * gate * sigma).astype(low)


def units_back_whole(cotangent, raised, down, wide):
    grad = jnp.concatenate(gates_back(mm(cotangent, down), raised), 1)
    return grad, dot(grad, wide, 1, 1).astype(low)


def units_back_kernel(core, cot_ref, raised_ref, down_ref, wide_ref, grad_ref, out_ref):
    half = down_ref.shape[1]
    gate_grad, up_grad = gates_back(mm(cot_ref[0, 0], down_ref[...]), raised_ref[...])
    grad_ref[:, :half] = gate_grad
    grad_ref[:, half:] = up_grad
    out_ref[...] = dot(grad_ref[...], wide_ref[...], 1, 1).astype(low)


def units_back(cotangent, core, raised, down, wide):
    rows, columns = raised.shape[0] // 4, raised.shape[1]
    width = cotangent.shape[1]
    once = lambda array: pl.BlockSpec(
        array.shape, lambda g, core: (0, 0), pipeline_mode=pl.Buffered(1)
    )
    return pl.pallas_call(
        units_back_kernel,
        out_shape=(
            jax.ShapeDtypeStruct(raised.shape, low),
            jax.ShapeDtypeStruct((4 * rows, width), low),
        ),
        grid_spec=pltpu.PrefetchScalarGridSpec(
            num_scalar_prefetch=1,
            grid=(4,),
            in_specs=[
                pl.BlockSpec((1, 1, rows, width), lambda g, core: (g, core[0], 0, 0)),
                pl.BlockSpec((rows, columns), lambda g, core: (g, 0)),
                once(down),
                once(wide),
            ],
            out_specs=[
                pl.BlockSpec((rows, columns), lambda g, core: (g, 0)),
                pl.BlockSpec((rows, width), lambda g, core: (g, 0)),
            ],
        ),
        compiler_params=pltpu.CompilerParams(vmem_limit_bytes=44 << 20),
        cost_estimate=pl.CostEstimate(flops=0, bytes_accessed=1 << 16, transcendentals=0),
    )(core.astype(jnp.int32).reshape(1), cotangent.reshape(4, 2, rows, width), raised, down, wide)


def by_ranks(wide, down, rank, parts):
    rows, units = wide.shape[0], wide.shape[1] // (2 * parts)
    place = lambda r: (rank - r) % parts
    if units % 128:
        blocks = jnp.concatenate(
            [a.reshape(rows, -1, parts, units) for a in (wide, down)], 1
        )
        blocks = jnp.transpose(blocks, (2, 0, 1, 3)).reshape(parts, rows, 3 * units)
        return jnp.stack([blocks[place(r)] for r in range(parts)])

    def kernel(index_ref, gate_ref, up_ref, down_ref, out_ref):
        for k, ref in enumerate((gate_ref, up_ref, down_ref)):
            out_ref[0, :, k * units : (k + 1) * units] = ref[...]

    def column(first):
        return pl.BlockSpec((rows, units), lambda r, index: (0, first + index[r]))

    return pl.pallas_call(
        kernel,
        out_shape=jax.ShapeDtypeStruct((parts, rows, 3 * units), low),
        grid_spec=pltpu.PrefetchScalarGridSpec(
            num_scalar_prefetch=1,
            grid=(parts,),
            in_specs=[column(0), column(parts), column(0)],
            out_specs=pl.BlockSpec((1, rows, 3 * units), lambda r, index: (r, 0, 0)),
        ),
        compiler_params=pltpu.CompilerParams(vmem_limit_bytes=32 << 20),
        cost_estimate=pl.CostEstimate(flops=0, bytes_accessed=1 << 16, transcendentals=0),
    )(place(jnp.arange(parts, dtype=jnp.int32)), wide, wide, down)


def widen_kernel(pack_ref, gate_out, up_out, down_out):
    units = gate_out.shape[1]
    gate_out[...] = pack_ref[0, :, :units].astype(full)
    up_out[...] = pack_ref[0, :, units : 2 * units].astype(full)
    down_out[...] = pack_ref[0, :, 2 * units :].astype(full).T


def widen(pack):
    groups, rows, columns = pack.shape
    units = columns // 3
    if units % 128:
        gate, up, down = (
            jnp.transpose(pack[:, :, k * units : (k + 1) * units], (1, 0, 2))
            .reshape(rows, -1)
            .astype(full)
            for k in range(3)
        )
        return gate, up, down.T
    shape = jax.ShapeDtypeStruct((rows, groups * units), full)
    column = pl.BlockSpec((rows, units), lambda g: (0, g))
    return pl.pallas_call(
        widen_kernel,
        out_shape=(shape, shape, jax.ShapeDtypeStruct((groups * units, rows), full)),
        grid=(groups,),
        in_specs=[pl.BlockSpec((1, rows, columns), lambda g: (g, 0, 0))],
        out_specs=[column, column, pl.BlockSpec((units, rows), lambda g: (g, 0))],
        compiler_params=pltpu.CompilerParams(vmem_limit_bytes=32 << 20),
        cost_estimate=pl.CostEstimate(flops=0, bytes_accessed=1 << 16, transcendentals=0),
    )(pack)


def split_kernel(in_ref, query_out, key_out, value_out):
    slots, width = query_out.shape[1], key_out.shape[0]
    array = in_ref[...].astype(full)
    query_out[...] = array[:, :slots]
    key_out[...] = array[:, slots : slots + width].T
    value_out[...] = array[:, slots + width : slots + 2 * width].T


def split_projections(array, slots, rows):
    width = KVH * HD
    if slots % 128 or rows % 128:
        array = array.astype(full)
        return array[:, :slots], array[:, slots:][:, :width], array[:, slots + width :][:, :width]
    turned = jax.ShapeDtypeStruct((width, array.shape[0]), full)
    column = pl.BlockSpec((width, rows), lambda g: (0, g))
    query, key, value = pl.pallas_call(
        split_kernel,
        out_shape=(jax.ShapeDtypeStruct((array.shape[0], slots), full), turned, turned),
        grid=(array.shape[0] // rows,),
        in_specs=[pl.BlockSpec((rows, array.shape[1]), lambda g: (g, 0))],
        out_specs=[pl.BlockSpec((rows, slots), lambda g: (g, 0)), column, column],
        compiler_params=pltpu.CompilerParams(vmem_limit_bytes=32 << 20),
        cost_estimate=pl.CostEstimate(flops=0, bytes_accessed=1 << 16, transcendentals=0),
    )(array)
    return query, key.T, value.T


def norm_backward(values, rms, gain, normed_grad):
    weighted = normed_grad * gain
    dotted = jnp.sum(weighted * values, axis=1, keepdims=True)
    grad = weighted * rms - values * (rms * rms * rms) * dotted / D
    return grad, jnp.sum(normed_grad * values * rms, axis=0)


def on_device(
    hidden_in,
    positions,
    head_counts,
    attention_gain,
    query_projection_weight,
    key_weight,
    value_weight,
    query_gain,
    key_gain,
    output_weight,
    feedforward_gain,
    gate_weight,
    up_weight,
    down_projection_weight,
    cotangent,
):
    groups = lax.axis_size("dp")
    parts = lax.axis_size("mp")
    group = lax.axis_index("dp")
    rank = lax.axis_index("mp")
    tokens, share = hidden_in.shape
    seqs = tokens // LEN
    ring = parts // seqs
    mine = tokens // parts
    chunk = mine // 2
    units = gate_weight.shape[1] // groups
    slots = query_projection_weight.shape[1]
    place = rank % ring
    ranks = range(parts)

    lower = jnp.arange(parts)[None, :] < jnp.arange(parts)[:, None]
    offsets = jnp.sum(jnp.where(lower, head_counts[None, :], 0), axis=1)

    def selection(order):
        within = jnp.arange(slots, dtype=jnp.int32)
        column = offsets[order][:, None] * HD + within[None, :]
        column = jnp.where(within[None, :] < head_counts[order][:, None] * HD, column, -1)
        return (
            column.reshape(-1)[:, None] == jnp.arange(QH * HD, dtype=jnp.int32)[None, :]
        ).astype(low)

    select_near = selection(rank ^ jnp.arange(parts, dtype=jnp.int32))
    select = selection(jnp.arange(parts, dtype=jnp.int32))

    def rows_of(array, other):
        base = (other // ring) * LEN
        at = other % ring
        first = lax.dynamic_slice_in_dim(array, base + at * chunk, chunk, 0)
        last = lax.dynamic_slice_in_dim(array, base + (2 * ring - 1 - at) * chunk, chunk, 0)
        return jnp.concatenate([first, last], 0)

    order = Order(head_counts)
    rows = D // groups
    heads_here = QH * HD // groups

    query_slice = lax.dynamic_slice_in_dim(query_projection_weight, group * rows, rows, 0)
    gains = jnp.stack([attention_gain, feedforward_gain])
    gains_high = gains.astype(low)
    gains_low = (gains - gains_high.astype(full)).astype(low)
    lines = -(-share // slots)
    gains = jnp.pad(
        jnp.concatenate([gains_high, gains_low], 0), ((0, 0), (0, lines * slots - share))
    )
    query_slice = jnp.concatenate([query_slice, gains.reshape(4 * lines, slots)], 0)
    query_slice = swap([query_slice] * parts, "mp")
    cosine, sine = rotary_tables(rows_of(positions, rank))
    chosen = lax.dynamic_slice_in_dim(select, group * heads_here, heads_here, 1)
    output_slice = dot(chosen, output_weight, 0, 0).astype(low)
    pack = jnp.concatenate(
        [
            lax.dynamic_slice_in_dim(gate_weight, group * units, units, 1),
            lax.dynamic_slice_in_dim(up_weight, group * units, units, 1),
            lax.dynamic_slice_in_dim(down_projection_weight, group * units, units, 0).T,
        ],
        1,
    )
    inputs = [rows_of(hidden_in, rank ^ k) for k in ranks]
    late = inputs[parts - 1]
    inputs = inputs[:1] + [exchange(inputs[k], "mp", k, parts) for k in range(1, parts - 1)]
    cotangent = [rows_of(cotangent, rank ^ k) for k in ranks]
    got = order(
        select_near, select, late, cosine, sine, output_slice, pack,
        *query_slice, *cotangent, *inputs
    )
    select_near, select, late, cosine, sine, output_slice, pack = got[:7]
    query_slice, cotangent = (got[7 + k * parts : 7 + (k + 1) * parts] for k in range(2))
    inputs = got[7 + 2 * parts :]

    inputs.append(exchange(late, "mp", parts - 1, parts))
    gains = by_rank([piece[rows:].reshape(4, -1)[:, :share] for piece in query_slice], rank)
    gains = jnp.concatenate(gains, 1).astype(full)
    attention_gain_all, feedforward_gain_all = gains[0] + gains[2], gains[1] + gains[3]
    query_slice = compact(query_slice, select_near, rows)
    query_all = lax.all_gather(query_slice, "dp", axis=0, tiled=True)
    *inputs, output_slice = order(*inputs, output_slice)

    output_slice = swap([output_slice] * parts, "mp")
    inputs = jnp.concatenate(by_rank(inputs, rank), axis=1).astype(full)
    first_rms = lax.rsqrt(jnp.mean(inputs * inputs, axis=1, keepdims=True) + epsilon)
    normed = (inputs * first_rms * attention_gain_all).astype(low)
    keys = dot(key_weight, normed, 0, 1).reshape(KVH, HD, mine)
    values_mine = dot(value_weight, normed, 0, 1).astype(low).reshape(KVH, HD, mine)
    turned_keys, key_pull = jax.vjp(lambda v, g: turn(v, g, cosine, sine), keys, key_gain)
    pair_mine = jnp.concatenate([turned_keys.astype(low), values_mine], 0)
    pair_mine, normed, *output_slice = order(pair_mine, normed, *output_slice)

    near_pairs = [pair_mine] + [exchange(pair_mine, "mp", k, parts) for k in range(1, ring)]
    output_slice = jnp.concatenate(by_rank(output_slice, rank), axis=1)
    output_all = lax.all_gather(output_slice, "dp", axis=0, tiled=True)
    queries = dot(query_all, normed, 0, 1).reshape(QH, HD, mine)
    turned_queries, query_pull = jax.vjp(
        lambda v, g: turn(v, g, cosine, sine), queries, query_gain
    )
    got = order(turned_queries.astype(low), *near_pairs, *cotangent)
    turned_queries, near_pairs, cotangent = got[0], got[1 : ring + 1], got[ring + 1 :]

    cotangent = swap(cotangent, "mp")
    near_pairs = by_rank(near_pairs, place)
    pair = jnp.concatenate(
        [p[:, :, :chunk] for p in near_pairs] + [p[:, :, chunk:] for p in near_pairs[::-1]], axis=2
    )
    key_heads, value_heads = pair[:KVH], pair[KVH:]
    starts = jnp.stack([place * chunk, (2 * ring - 1 - place) * chunk]).astype(jnp.int32)
    mixed, row_totals = attend(starts, turned_queries, key_heads, value_heads)
    mixed = mixed.reshape(QH * HD, mine)
    middle = inputs + dot(mixed, output_all, 0, 0)
    second_rms = lax.rsqrt(jnp.mean(middle * middle, axis=1, keepdims=True) + epsilon)
    second_normed = (middle * second_rms * feedforward_gain_all).astype(low)
    second_normed, pack, *cotangent = order(second_normed, pack, *cotangent)

    second = Spread(second_normed, "dp", groups, group)
    weights = RelayGather(pack, "mp", parts)
    cotangent_mine = jnp.concatenate(by_rank(cotangent, rank), axis=1)
    cube = groups == CUBE
    if cube:
        flag = group % 2 != 0
        pairs = [normed[:, k * rows : (k + 1) * rows] for k in range(groups)]
        normed_own, normed_other = (
            jnp.concatenate(
                [jnp.where(flag, pairs[k ^ 1 ^ a], pairs[k ^ a]) for k in range(0, groups, 2)], 1
            )
            for a in (0, 1)
        )
        pairs = mixed.reshape(4, 2, heads_here, mine)
        mixed_own, mixed_other = (
            lax.dynamic_index_in_dim(pairs, at, 1, keepdims=False).reshape(-1, mine)
            for at in (group % 2, 1 - group % 2)
        )
    else:
        normed_own = normed_other = normed
        mixed_own = mixed_other = mixed
    *got, up, down, cotangent_mine, normed_own, normed_other, mixed_own, mixed_other = order(
        *second.flying, *weights.flying, cotangent_mine, normed_own, normed_other,
        mixed_own, mixed_other
    )
    second.second(*got)
    weights.take(up, down)
    cotangent_mine, got, (up, down), second.buffer = order_split(
        order, [cotangent_mine], second.flying, weights.flying, second.buffer
    )
    cotangent_full = lax.all_gather(cotangent_mine, "dp", axis=0, tiled=True)
    second.third(*got)
    weights.take(up, down)
    got, (up, down) = order_split(order, [], second.flying, weights.flying)
    second.last(*got)
    weights.take(up, down)
    pack = weights.finish(order)
    wide = jnp.concatenate(
        [block[:, :units] for block in pack] + [block[:, units : 2 * units] for block in pack], 1
    )
    down_here = jnp.concatenate([block[:, 2 * units :] for block in pack], 1)
    half = parts * units

    raised = [mm(part, wide) for part in second.parts]
    hidden = [
        (v[:, :half] * jax.nn.sigmoid(v[:, :half]) * v[:, half:]).astype(low) for v in raised
    ]
    down_terms = [dot(h, down_here, 1, 1).astype(low) for h in hidden]
    down_terms, raised, hidden, (cotangent_full,) = order_split(
        order, [], down_terms, raised, hidden, [cotangent_full]
    )

    core = group % 2
    if cube:
        back = lambda at, v: units_back(cotangent_full, at, v, down_here, wide)
    else:
        back = lambda at, v: units_back_whole(cotangent_full, v, down_here, wide)
    grad, other = back(1 - core, raised[-1])
    grads = [grad]
    other, grads[0], *raised = order(other, grads[0], *raised)

    second_sum = Collect(other, "dp", groups, group)
    own = other
    if len(raised) > 1:
        grad, own = back(core, raised[0])
        grads.insert(0, grad)
    own, *grads, hidden, got = order_split(order, [own, *grads], hidden, second_sum.flying)

    second_sum.second(own, *got)
    wide_grad = sum(dot(part, grad, 0, 0) for part, grad in zip(second.parts, grads)).astype(low)
    if cube:
        shape = (4, 1, mine, half)
        first, last = (h.reshape(shape) for h in hidden)
        hidden_full = jnp.concatenate(
            [jnp.where(core == 0, first, last), jnp.where(core == 0, last, first)], 1
        ).reshape(2 * 4 * mine, half)
    else:
        hidden_full = hidden[0]
    down_grad = dot(cotangent_full, hidden_full, 0, 0).astype(low)
    down_sum = Collect(down_terms[-1], "dp", groups, group)
    down_grad, wide_grad, got, flying = order_split(
        order, [down_grad, wide_grad], second_sum.flying, down_sum.flying
    )

    second_sum.third(*got)

    pack = by_ranks(wide_grad, down_grad, rank, parts)
    pack = lax.psum_scatter(pack, "mp", scatter_dimension=0, tiled=False)
    down_sum.second(down_terms[0], *flying, apart=True)
    *got, flying = order_split(order, second_sum.flying, down_sum.flying)

    normed_two_grad = second_sum.last(*got).astype(full)
    down_sum.launch(*flying)
    middle_part, feedforward_gain_grad = norm_backward(
        middle, second_rms, feedforward_gain_all, normed_two_grad
    )
    middle_grad = cotangent_mine.astype(full) + middle_part
    lane = lax.broadcasted_iota(jnp.int32, (D, EXTRA), 1)
    wide_extra = jnp.where(lane == 0, feedforward_gain_grad[:, None], 0.0)
    branch_grad = middle_grad.astype(low)
    mixed_grad = dot(output_all, branch_grad, 1, 1).astype(low).reshape(QH, HD, mine)
    output_other = mm(mixed_other, branch_grad).astype(low)
    output_own = mm(mixed_own, branch_grad).astype(low) if cube else output_other
    output_sum = Collect(output_other, "dp", groups, group)
    query_rot_grad, key_rot_grad, value_grad = attend_back(
        starts, turned_queries, key_heads, value_heads, mixed_grad, row_totals
    )
    pair_grad = jnp.concatenate([key_rot_grad, value_grad], 0)
    blocks = [
        jnp.concatenate(
            [
                pair_grad[:, :, j * chunk : (j + 1) * chunk],
                pair_grad[:, :, (2 * ring - 1 - j) * chunk : (2 * ring - j) * chunk],
            ],
            axis=2,
        )
        for j in range(ring)
    ]
    blocks = by_rank(blocks, place)
    away = [block.astype(low) for block in blocks[1:]]
    query_rot_grad, output_own, *away, got, flying = order_split(
        order, [query_rot_grad, output_own, *away], down_sum.flying, output_sum.flying
    )
    down_sum.third(*got)
    output_sum.second(output_own, *flying)

    away = [exchange(block, "mp", k + 1, parts) for k, block in enumerate(away)]
    queries_low, query_gain_grad = query_pull(query_rot_grad)
    queries_low = queries_low.astype(low).reshape(QH * HD, mine)
    queries_low, pack, wide_extra, *away, out_relayed, got = order_split(
        order, [queries_low, pack, wide_extra, *away], down_sum.flying, output_sum.flying
    )
    output_sum.third(*got)
    pack = by_rows(lax.all_gather(by_rows(pack), "dp", axis=0, tiled=False))
    pair_grad = sum([blocks[0]] + [block.astype(full) for block in away])
    keys_grad, key_gain_grad = key_pull(pair_grad[:KVH])
    pair_low = jnp.concatenate(
        [keys_grad.astype(low), pair_grad[KVH:].astype(low)], 0
    ).reshape(2 * KVH * HD, mine)
    all_low = jnp.concatenate([queries_low, pair_low], 0)
    heads_gain = jnp.stack([query_gain_grad, key_gain_grad])
    top = wide_extra[:2] + jnp.pad(heads_gain, ((0, 0), (EXTRA - HD, 0)))
    extra = jnp.concatenate([top, wide_extra[2:]], 0)
    wide_low = jnp.concatenate([all_low, jnp.zeros((EXTRA, mine), low)], 0)

    def projections(normed_part, extra_part):
        extra_part = jnp.pad(extra_part, ((0, 0), (wide_low.shape[0] - EXTRA, 0)))
        return (dot(normed_part, wide_low, 0, 1) + extra_part).astype(low)

    own = other = extra
    if cube:
        pairs = extra.reshape(4, 2, rows, EXTRA)
        own, other = (
            lax.dynamic_index_in_dim(pairs, at, 1, keepdims=False).reshape(4 * rows, EXTRA)
            for at in (group % 2, 1 - group % 2)
        )
    other = projections(normed_other, other)
    other, own, wide_low, all_low, normed_own = order(other, own, wide_low, all_low, normed_own)

    def by_feature(array):
        return by_rank([array[:, j * share : (j + 1) * share] for j in ranks], rank)

    projection_sum = Collect(other, "dp", groups, group)
    own = projections(normed_own, own) if cube else other
    queries_low, pair_low = all_low[: QH * HD], all_low[QH * HD :]
    normed_grad = (
        dot(queries_low, query_all, 0, 1)
        + dot(pair_low[: KVH * HD], key_weight, 0, 1)
        + dot(pair_low[KVH * HD :], value_weight, 0, 1)
    )
    input_part, _ = norm_backward(
        inputs, first_rms, attention_gain_all, normed_grad
    )
    input_gradient = (middle_grad + input_part).astype(low)
    input_gradient, own, got, flying = order_split(
        order, [input_gradient, own], projection_sum.flying, output_sum.flying
    )
    projection_sum.second(own, *got)
    output_grad = output_sum.last(*flying)

    def by_tokens(got, kind):
        got = by_rank(got, rank)
        rows = []
        for seq in range(seqs):
            near = got[seq * ring : (seq + 1) * ring]
            rows += [block[:chunk] for block in near]
            rows += [block[chunk:] for block in near[::-1]]
        return jnp.concatenate(rows, 0).astype(kind)

    input_gradient = swap(by_feature(input_gradient), "mp")
    input_gradient, got, out_relayed = order_split(
        order, [], input_gradient, projection_sum.flying, out_relayed
    )
    projection_sum.third(*got)

    output_grad = swap(by_feature(output_grad), "mp")
    output_grad, got, out_relayed = order_split(
        order, [], output_grad, projection_sum.flying, out_relayed
    )
    output_grad = lax.all_gather(added(*output_grad), "dp", axis=0, tiled=True)
    projection_total = projection_sum.last(*got)
    down_sum.fourth(*out_relayed)

    query_total, pair_total, extra = jnp.split(
        projection_total, [QH * HD, (QH + 2 * KVH) * HD], axis=1
    )
    here = lambda weight: lax.dynamic_slice_in_dim(weight, group * rows, rows, 0).astype(full)
    product = jnp.sum(here(query_all) * query_total.astype(full), axis=1)
    product += jnp.sum(here(key_weight) * pair_total[:, : KVH * HD].astype(full), axis=1)
    product += jnp.sum(here(value_weight) * pair_total[:, KVH * HD :].astype(full), axis=1)
    product = product / lax.dynamic_slice_in_dim(attention_gain_all, group * rows, rows, 0)
    column = lax.broadcasted_iota(jnp.int32, extra.shape, 1)
    extra = jnp.where(column == 2, product[:, None].astype(low), extra)
    query_part = dot(query_total, select_near, 1, 1).astype(low)
    projection = swap(
        [
            jnp.concatenate([query_part[:, k * slots : (k + 1) * slots], pair_total, extra], 1)
            for k in ranks
        ],
        "mp",
    )
    pack, projection, flying = order_split(order, [pack], projection, down_sum.flying)

    projection = lax.all_gather(added(*projection), "dp", axis=0, tiled=True)
    output_weight_grad = mm(select, output_grad)
    output = (middle + down_sum.last(*flying).astype(full)).astype(low)
    output = swap(by_feature(output), "mp")
    gate_weight_grad, up_weight_grad, down_weight_grad = widen(pack)
    input_gradient = by_tokens(input_gradient, full)
    got = order(
        gate_weight_grad, up_weight_grad, down_weight_grad, input_gradient, output_weight_grad,
        *output
    )
    gate_weight_grad, up_weight_grad, down_weight_grad, input_gradient = got[:4]
    output_weight_grad = got[4]
    output = by_tokens(got[5:], low)
    query_weight_grad, key_weight_grad, value_weight_grad = split_projections(
        projection, slots, rows
    )
    extra = projection[:, slots + 2 * KVH * HD :]
    extra = extra.astype(full)
    own_share = lax.dynamic_slice_in_dim(extra, rank * share, share, 0)
    return (
        output,
        input_gradient,
        own_share[:, 2],
        query_weight_grad.astype(full),
        key_weight_grad.astype(full),
        value_weight_grad.astype(full),
        extra[0, EXTRA - HD :],
        extra[1, EXTRA - HD :],
        output_weight_grad,
        own_share[:, 0],
        gate_weight_grad,
        up_weight_grad,
        down_weight_grad,
    )


def solution(mesh):
    in_specs = (
        P("dp", "mp"),
        P("dp"),
        P(),
        P("mp"),
        P(None, "mp"),
        P(),
        P(),
        P(),
        P(),
        P(None, "mp"),
        P("mp"),
        P(None, "mp"),
        P(None, "mp"),
        P("mp", None),
        P("dp", "mp"),
    )
    out_specs = (
        P("dp", "mp"),
        P("dp", "mp"),
        P("mp"),
        P(None, "mp"),
        P(),
        P(),
        P(),
        P(),
        P(None, "mp"),
        P("mp"),
        P(None, "mp"),
        P(None, "mp"),
        P("mp", None),
    )
    return jax.shard_map(
        on_device, mesh=mesh, in_specs=in_specs, out_specs=out_specs, check_vma=False
    )
```

```python
import functools
import math

import jax
import jax.numpy as jnp
from jax import lax
from jax.experimental.layout import Layout, with_layout_constraint
from jax.experimental import pallas as pl
from jax.experimental.pallas import tpu as pltpu
from jax.sharding import PartitionSpec as P

D = 2048
QH = 20
KVH = 5
QPG = QH // KVH
HD = 64
LEN = 1024

epsilon = 1e-05
rope_base = 10000.0
masked_score = -1e30
low = jnp.bfloat16
full = jnp.float32


def dot(left, right, left_axis, right_axis):
    return lax.dot_general(
        left, right, (((left_axis,), (right_axis,)), ((), ())), preferred_element_type=full
    )


def swap(pieces, axis):
    n = len(pieces)
    return [pieces[0]] + [
        lax.ppermute(pieces[k], axis, [(i, i ^ k) for i in range(n)]) for k in range(1, n)
    ]


def by_rank(blocks, rank):
    bit = 1
    while bit < len(blocks):
        flag = (rank & bit) != 0
        blocks = [jnp.where(flag, blocks[j ^ bit], blocks[j]) for j in range(len(blocks))]
        bit *= 2
    return blocks


def exchange(array, axis, mask, n):
    return lax.ppermute(array, axis, [(i, i ^ mask) for i in range(n)])


def by_rows(array):
    return with_layout_constraint(array, Layout(tuple(range(array.ndim))))


def added(*terms):
    return sum(term.astype(full) for term in terms).astype(low)


class Order:
    def __init__(self, token):
        self.token = token

    def __call__(self, *arrays):
        self.token, *arrays = lax.optimization_barrier((self.token, *arrays))
        return arrays


class RelayGather:
    def __init__(self, piece, axis, n):
        self.axis, self.n, self.step, self.own = axis, n, 1, piece
        self.ups, self.downs = [], []
        self.send(piece, piece)

    def send(self, up, down):
        n, step = self.n, self.step
        right = [(i, i + 1) for i in range(step - 1, n - 1)]
        left = [(i, i - 1) for i in range(n - step, 0, -1)]
        self.flying = [lax.ppermute(up, self.axis, right), lax.ppermute(down, self.axis, left)]

    def take(self, up, down):
        self.ups.append(up)
        self.downs.append(down)
        self.step += 1
        if self.step < self.n:
            self.send(up, down)

    def finish(self, order):
        while self.step < self.n:
            self.take(*order(*self.flying))
        n = self.n
        return [self.own] + [self.ups[k - 1] + self.downs[n - k - 1] for k in range(1, n)]


CUBE = 8


def at_index(array, index):
    return lax.dynamic_index_in_dim(array, index, 0, keepdims=False)


class Spread:
    def __init__(self, piece, axis, n, group):
        self.axis, self.n, self.chip, self.piece = axis, n, group // 2, piece
        if n == CUBE:
            self.flying = [self.move(piece, 2), self.move(piece, 4)]
        else:
            self.flying = [lax.all_gather(piece, axis, axis=0, tiled=True)]
        self.buffer = []

    def move(self, array, mask):
        return exchange(array, self.axis, mask, self.n)

    def second(self, *got):
        self.flying = got
        if self.n == CUBE:
            near, far = got
            half = self.piece.shape[0] // 2
            self.flying = [self.move(near[:half], 4), self.move(far[half:], 2)]
            mine = jnp.zeros((4, *self.piece.shape), self.piece.dtype)
            for k, block in enumerate((self.piece, near, far)):
                mine = lax.dynamic_update_slice(mine, block[None], (self.chip ^ k, 0, 0))
            self.buffer = [mine]

    def third(self, *got):
        if self.n != CUBE:
            self.parts, self.flying = list(got), []
            return
        rows = self.piece.shape[0]
        (mine,) = self.buffer
        for k, block in enumerate(got):
            mine = lax.dynamic_update_slice(
                mine, block[None], (self.chip ^ 3, k * (rows // 2), 0)
            )
        mine = mine.reshape(4 * rows, -1)
        self.parts = [mine]
        self.flying = [self.move(mine, 1)]

    def last(self, *got):
        self.parts += got


TOGETHER = (((3, 0), (1, 0)), ((3, 1), (2, 1)), ((0, 0), (0, 1), (2, 0), (1, 1)))
APART = (((3, 0),), ((3, 1),), ((1, 0),), ((2, 1),), ((0, 0), (0, 1), (2, 0), (1, 1)))


def chip_sums(mine, got, chip, plan):
    half, columns = mine.shape[0] // 8, mine.shape[1]
    flat = [place for places in plan for place in places]
    index = jnp.stack([(chip ^ block) * 2 + part for block, part in flat]).astype(jnp.int32)
    firsts = [sum(len(places) for places in plan[:k]) for k in range(len(plan))]

    def kernel(index_ref, mine_ref, got_ref, *outs):
        step = pl.program_id(0)
        total = (mine_ref[...].astype(full) + got_ref[...].astype(full)).astype(low)
        for first, places, out in zip(firsts, plan, outs):

            @pl.when((step >= first) & (step < first + len(places)))
            def _():
                out[...] = total

    source = pl.BlockSpec((half, columns), lambda g, index: (index[g], 0))

    def target(first, count):
        return pl.BlockSpec(
            (half, columns), lambda g, index: (jnp.clip(g - first, 0, count - 1), 0)
        )

    return pl.pallas_call(
        kernel,
        out_shape=[
            jax.ShapeDtypeStruct((len(places) * half, columns), low) for places in plan
        ],
        grid_spec=pltpu.PrefetchScalarGridSpec(
            num_scalar_prefetch=1,
            grid=(len(flat),),
            in_specs=[source, source],
            out_specs=[target(f, len(places)) for f, places in zip(firsts, plan)],
        ),
        compiler_params=pltpu.CompilerParams(vmem_limit_bytes=40 << 20),
        cost_estimate=pl.CostEstimate(flops=0, bytes_accessed=1 << 16, transcendentals=0),
    )(index, mine, got)


class Collect:
    def __init__(self, other, axis, n, group):
        self.axis, self.n, self.chip = axis, n, group // 2
        if n == CUBE:
            self.flying = [self.move(other, 1)]
        else:
            self.flying = [lax.psum_scatter(other, axis, scatter_dimension=0, tiled=True)]

    def move(self, array, mask):
        return exchange(array, self.axis, mask, self.n)

    def second(self, mine, *got, apart=False):
        self.flying, self.held = got, []
        if self.n != CUBE:
            return
        self.half = mine.shape[0] // 8
        *sent, self.keep = chip_sums(mine, got[0], self.chip, APART if apart else TOGETHER)
        self.apart = apart
        if apart:
            self.flying, self.held = sent[:2], sent[2:]
        else:
            self.launch(*sent)

    def launch(self, *ready):
        self.flying = ready
        if self.n == CUBE:
            self.flying = [self.move(ready[0], 2), self.move(ready[1], 4)]

    def third(self, *got):
        self.flying = got
        if self.n != CUBE:
            return
        half = self.half
        if not self.apart:
            self.direct = [got[0][half:], got[1][half:]]
        self.flying = [
            self.move(added(self.keep[2 * half : 3 * half], got[0][:half]), 4),
            self.move(added(self.keep[3 * half :], got[1][:half]), 2),
        ]

    def fourth(self, *got):
        self.flying = got
        if self.n == CUBE:
            self.relayed = got
            self.flying = [self.move(self.held[0], 2), self.move(self.held[1], 4)]

    def last(self, *got):
        if self.n != CUBE:
            return got[0]
        half = self.half
        direct, got = (got, self.relayed) if self.apart else (self.direct, got)
        return jnp.concatenate(
            [
                added(self.keep[:half], direct[0], got[0]),
                added(self.keep[half : 2 * half], direct[1], got[1]),
            ],
            0,
        )


EXTRA = 128


def order_split(order, first, *lists):
    first = list(first)
    got = order(*first, *[array for arrays in lists for array in arrays])
    result, at = list(got[: len(first)]), len(first)
    for arrays in lists:
        result.append(list(got[at : at + len(arrays)]))
        at += len(arrays)
    return result


def rotary_tables(positions):
    half = HD // 2
    inverse = jnp.exp(-math.log(rope_base) * (2.0 * jnp.arange(half, dtype=full)) / HD)
    angles = inverse[:, None] * positions.astype(full)[None, :]
    cosine, sine = jnp.cos(angles), jnp.sin(angles)
    return jnp.concatenate([cosine, cosine], 0), jnp.concatenate([sine, sine], 0)


def turn(raw, gain, cosine, sine):
    half = HD // 2
    rms = lax.rsqrt(jnp.mean(raw * raw, axis=1, keepdims=True) + epsilon)
    normed = raw * rms * gain[None, :, None]
    turned = jnp.concatenate([-normed[:, half:], normed[:, :half]], axis=1)
    return normed * cosine[None] + turned * sine[None]


def mm(left, right):
    return jnp.dot(left, right, preferred_element_type=full)


BLOCK = LEN // 4
PARTS = (((0, True),), ((0, False), (BLOCK, False), (2 * BLOCK, True)))


def scores_of(key, query, lead):
    scores = mm(key, query)
    if lead is None:
        return scores
    rows = lax.broadcasted_iota(jnp.int32, scores.shape, 0)
    cols = lax.broadcasted_iota(jnp.int32, scores.shape, 1)
    return jnp.where(rows - cols <= lead, scores, masked_score)


def last_piece(starts, chunk):
    early = starts[0] >= BLOCK
    at = pl.multiple_of(jnp.where(early, BLOCK, 3 * BLOCK), BLOCK)
    span = pl.multiple_of(jnp.where(early, 0, chunk), 128)
    start = jnp.where(early, starts[0], starts[1])
    flag = jnp.where(early, 1.0, 0.0).astype(full)
    return early, pl.ds(at, BLOCK), pl.ds(span, chunk), start - at, (flag, 1.0 - flag)


def rows_kept(array):
    return array.astype(full).T.astype(low)


def attend_kernel(starts, q_ref, k_ref, v_ref, o_ref, sums_ref, key_ref):
    chunk = q_ref.shape[2] // 2
    scale = jnp.asarray(1.0 / math.sqrt(HD), low)
    key_ref[...] = rows_kept(k_ref[0])
    early, keys, columns, lead, flags = last_piece(starts, chunk)
    for head in range(QPG):
        scores, peaks = [], []
        for part, pieces in enumerate(PARTS):
            query = q_ref[head, :, part * chunk : (part + 1) * chunk] * scale
            scores.append(
                [
                    scores_of(key_ref[at : at + BLOCK], query, starts[part] - at if cut else None)
                    for at, cut in pieces
                ]
            )
            peaks.append(
                functools.reduce(
                    jnp.maximum, [jnp.max(s, axis=0, keepdims=True) for s in scores[-1]]
                )
            )
        more = scores_of(key_ref[keys], q_ref[head, :, columns] * scale, lead)
        peak = jnp.max(more, axis=0, keepdims=True)
        peaks = [
            jnp.maximum(peaks[0], jnp.where(early, peak, masked_score)),
            jnp.maximum(peaks[1], jnp.where(early, masked_score, peak)),
        ]
        more = jnp.exp(more - jnp.where(early, peaks[0], peaks[1]))
        more_total = jnp.sum(more, axis=0, keepdims=True)
        more_result = mm(v_ref[0, :, keys], more.astype(low))
        for part, pieces in enumerate(PARTS):
            total = more_total * flags[part]
            result = more_result * flags[part]
            for (at, _), s in zip(pieces, scores[part]):
                weights = jnp.exp(s - peaks[part])
                total += jnp.sum(weights, axis=0, keepdims=True)
                result += mm(v_ref[0, :, at : at + BLOCK], weights.astype(low))
            span = pl.ds(part * chunk, chunk)
            o_ref[head, :, span] = (result / total).astype(low)
            sums_ref[0, head : head + 1, span] = peaks[part] + jnp.log(total)


def attend_back_kernel(
    starts, q_ref, k_ref, v_ref, g_ref, sums_ref, dq_ref, dk_ref, dv_ref, dk_acc, dv_acc,
    key_ref, value_ref
):
    chunk = q_ref.shape[2] // 2
    scale = 1.0 / math.sqrt(HD)
    key_ref[...] = rows_kept(k_ref[0])
    value_ref[...] = rows_kept(v_ref[0])
    dk_acc[...] = jnp.zeros_like(dk_acc)
    dv_acc[...] = jnp.zeros_like(dv_acc)
    early, keys, columns, lead, flags = last_piece(starts, chunk)

    def products(at, query, grad, sums, lead):
        probs = jnp.exp(scores_of(key_ref[at], query, lead) - sums)
        return probs, probs * mm(value_ref[at], grad)

    def store(at, probs, product, delta, query_rows, grad_rows):
        score_grad = (product - probs * delta).astype(low)
        dk_acc[at, :] += mm(score_grad, query_rows)
        dv_acc[at, :] += mm(probs.astype(low), grad_rows)
        return mm(k_ref[0, :, at], score_grad)

    for head in range(QPG):
        parts = []
        for part, pieces in enumerate(PARTS):
            span = pl.ds(part * chunk, chunk)
            query = q_ref[head, :, span] * jnp.asarray(scale, low)
            grad = g_ref[head, :, span]
            sums = sums_ref[0, head : head + 1, span]
            found = [
                products(
                    pl.ds(at, BLOCK), query, grad, sums, starts[part] - at if cut else None
                )
                for at, cut in pieces
            ]
            delta = sum(jnp.sum(product, axis=0, keepdims=True) for _, product in found)
            parts.append([found, delta, rows_kept(query), rows_kept(grad)])
        probs, product = products(
            keys,
            q_ref[head, :, columns] * jnp.asarray(scale, low),
            g_ref[head, :, columns],
            sums_ref[0, head : head + 1, columns],
            lead,
        )
        more = jnp.sum(product, axis=0, keepdims=True)
        for part in range(2):
            parts[part][1] += more * flags[part]
        more = store(
            keys, probs, product, *(jnp.where(early, a, b) for a, b in zip(parts[0][1:], parts[1][1:]))
        )
        for part, pieces in enumerate(PARTS):
            found, delta, query_rows, grad_rows = parts[part]
            dq = more * flags[part]
            for (at, _), (probs, product) in zip(pieces, found):
                dq += store(pl.ds(at, BLOCK), probs, product, delta, query_rows, grad_rows)
            dq_ref[head, :, part * chunk : (part + 1) * chunk] = dq * scale
    dk_ref[0] = dk_acc[...].T
    dv_ref[0] = dv_acc[...].T


def attention_specs(tokens):
    heads = pl.BlockSpec((QPG, HD, tokens), lambda g, s: (g, 0, 0))
    keys = pl.BlockSpec((1, HD, LEN), lambda g, s: (g, 0, 0))
    sums = pl.BlockSpec((1, QPG, tokens), lambda g, s: (g, 0, 0))
    return heads, keys, sums


def attend(starts, queries, keys, values):
    tokens = queries.shape[2]
    heads, whole, sums = attention_specs(tokens)
    pairs = QH * (tokens // 2) * 5 * BLOCK
    return pl.pallas_call(
        attend_kernel,
        out_shape=(
            jax.ShapeDtypeStruct((QH, HD, tokens), low),
            jax.ShapeDtypeStruct((KVH, QPG, tokens), full),
        ),
        grid_spec=pltpu.PrefetchScalarGridSpec(
            num_scalar_prefetch=1,
            grid=(KVH,),
            in_specs=[heads, whole, whole],
            out_specs=[heads, sums],
            scratch_shapes=[pltpu.VMEM((LEN, HD), low)],
        ),
        compiler_params=pltpu.CompilerParams(vmem_limit_bytes=40 << 20),
        cost_estimate=pl.CostEstimate(
            flops=pairs, bytes_accessed=1 << 20, transcendentals=0
        ),
    )(starts, queries, keys, values)


def attend_back(starts, queries, keys, values, grads, sums_in):
    tokens = queries.shape[2]
    heads, whole, sums = attention_specs(tokens)
    pairs = QH * (tokens // 2) * 5 * BLOCK
    return pl.pallas_call(
        attend_back_kernel,
        out_shape=(
            jax.ShapeDtypeStruct((QH, HD, tokens), full),
            jax.ShapeDtypeStruct((KVH, HD, LEN), full),
            jax.ShapeDtypeStruct((KVH, HD, LEN), full),
        ),
        grid_spec=pltpu.PrefetchScalarGridSpec(
            num_scalar_prefetch=1,
            grid=(KVH,),
            in_specs=[heads, whole, whole, heads, sums],
            out_specs=[heads, whole, whole],
            scratch_shapes=[pltpu.VMEM((LEN, HD), kind) for kind in (full, full, low, low)],
        ),
        compiler_params=pltpu.CompilerParams(vmem_limit_bytes=40 << 20),
        cost_estimate=pl.CostEstimate(
            flops=pairs, bytes_accessed=1 << 20, transcendentals=0
        ),
    )(starts, queries, keys, values, grads, sums_in)


def compact_kernel(*refs):
    *pieces, select_ref, out_ref = refs
    rows, slots = out_ref.shape[0], pieces[0].shape[1]
    out_ref[...] = sum(
        mm(piece[:rows, :], select_ref[k * slots : (k + 1) * slots, :])
        for k, piece in enumerate(pieces)
    ).astype(low)


def compact(pieces, select, rows):
    if pieces[0].shape[1] % 128:
        joined = jnp.concatenate([piece[:rows] for piece in pieces], axis=1)
        return mm(joined, select).astype(low)
    return pl.pallas_call(
        compact_kernel,
        out_shape=jax.ShapeDtypeStruct((rows, select.shape[1]), low),
        compiler_params=pltpu.CompilerParams(vmem_limit_bytes=32 << 20),
        cost_estimate=pl.CostEstimate(flops=0, bytes_accessed=1 << 16, transcendentals=0),
    )(*pieces, select)


def gates_back(hidden_grad, raised):
    half = raised.shape[1] // 2
    gate, up = raised[:, :half], raised[:, half:]
    sigma = jax.nn.sigmoid(gate)
    gate_grad = hidden_grad * up * sigma * (1.0 + gate * (1.0 - sigma))
    return gate_grad.astype(low), (hidden_grad * gate * sigma).astype(low)


def units_back_whole(cotangent, raised, down, wide):
    grad = jnp.concatenate(gates_back(mm(cotangent, down), raised), 1)
    return grad, dot(grad, wide, 1, 1).astype(low)


def units_back_kernel(core, cot_ref, raised_ref, down_ref, wide_ref, grad_ref, out_ref):
    half = down_ref.shape[1]
    gate_grad, up_grad = gates_back(mm(cot_ref[0, 0], down_ref[...]), raised_ref[...])
    grad_ref[:, :half] = gate_grad
    grad_ref[:, half:] = up_grad
    out_ref[...] = dot(grad_ref[...], wide_ref[...], 1, 1).astype(low)


def units_back(cotangent, core, raised, down, wide):
    rows, columns = raised.shape[0] // 4, raised.shape[1]
    width = cotangent.shape[1]
    once = lambda array: pl.BlockSpec(
        array.shape, lambda g, core: (0, 0), pipeline_mode=pl.Buffered(1)
    )
    return pl.pallas_call(
        units_back_kernel,
        out_shape=(
            jax.ShapeDtypeStruct(raised.shape, low),
            jax.ShapeDtypeStruct((4 * rows, width), low),
        ),
        grid_spec=pltpu.PrefetchScalarGridSpec(
            num_scalar_prefetch=1,
            grid=(4,),
            in_specs=[
                pl.BlockSpec((1, 1, rows, width), lambda g, core: (g, core[0], 0, 0)),
                pl.BlockSpec((rows, columns), lambda g, core: (g, 0)),
                once(down),
                once(wide),
            ],
            out_specs=[
                pl.BlockSpec((rows, columns), lambda g, core: (g, 0)),
                pl.BlockSpec((rows, width), lambda g, core: (g, 0)),
            ],
        ),
        compiler_params=pltpu.CompilerParams(vmem_limit_bytes=44 << 20),
        cost_estimate=pl.CostEstimate(flops=0, bytes_accessed=1 << 16, transcendentals=0),
    )(core.astype(jnp.int32).reshape(1), cotangent.reshape(4, 2, rows, width), raised, down, wide)


def by_ranks(wide, down, rank, parts):
    rows, units = wide.shape[0], wide.shape[1] // (2 * parts)
    place = lambda r: (rank - r) % parts
    if units % 128:
        blocks = jnp.concatenate(
            [a.reshape(rows, -1, parts, units) for a in (wide, down)], 1
        )
        blocks = jnp.transpose(blocks, (2, 0, 1, 3)).reshape(parts, rows, 3 * units)
        return jnp.stack([blocks[place(r)] for r in range(parts)])

    def kernel(index_ref, gate_ref, up_ref, down_ref, out_ref):
        for k, ref in enumerate((gate_ref, up_ref, down_ref)):
            out_ref[0, :, k * units : (k + 1) * units] = ref[...]

    def column(first):
        return pl.BlockSpec((rows, units), lambda r, index: (0, first + index[r]))

    return pl.pallas_call(
        kernel,
        out_shape=jax.ShapeDtypeStruct((parts, rows, 3 * units), low),
        grid_spec=pltpu.PrefetchScalarGridSpec(
            num_scalar_prefetch=1,
            grid=(parts,),
            in_specs=[column(0), column(parts), column(0)],
            out_specs=pl.BlockSpec((1, rows, 3 * units), lambda r, index: (r, 0, 0)),
        ),
        compiler_params=pltpu.CompilerParams(vmem_limit_bytes=32 << 20),
        cost_estimate=pl.CostEstimate(flops=0, bytes_accessed=1 << 16, transcendentals=0),
    )(place(jnp.arange(parts, dtype=jnp.int32)), wide, wide, down)


def widen_kernel(pack_ref, gate_out, up_out, down_out):
    units = gate_out.shape[1]
    gate_out[...] = pack_ref[0, :, :units].astype(full)
    up_out[...] = pack_ref[0, :, units : 2 * units].astype(full)
    down_out[...] = pack_ref[0, :, 2 * units :].astype(full).T


def widen(pack):
    groups, rows, columns = pack.shape
    units = columns // 3
    if units % 128:
        gate, up, down = (
            jnp.transpose(pack[:, :, k * units : (k + 1) * units], (1, 0, 2))
            .reshape(rows, -1)
            .astype(full)
            for k in range(3)
        )
        return gate, up, down.T
    shape = jax.ShapeDtypeStruct((rows, groups * units), full)
    column = pl.BlockSpec((rows, units), lambda g: (0, g))
    return pl.pallas_call(
        widen_kernel,
        out_shape=(shape, shape, jax.ShapeDtypeStruct((groups * units, rows), full)),
        grid=(groups,),
        in_specs=[pl.BlockSpec((1, rows, columns), lambda g: (g, 0, 0))],
        out_specs=[column, column, pl.BlockSpec((units, rows), lambda g: (g, 0))],
        compiler_params=pltpu.CompilerParams(vmem_limit_bytes=32 << 20),
        cost_estimate=pl.CostEstimate(flops=0, bytes_accessed=1 << 16, transcendentals=0),
    )(pack)


def split_kernel(in_ref, query_out, key_out, value_out):
    slots, width = query_out.shape[1], key_out.shape[0]
    array = in_ref[...].astype(full)
    query_out[...] = array[:, :slots]
    key_out[...] = array[:, slots : slots + width].T
    value_out[...] = array[:, slots + width : slots + 2 * width].T


def split_projections(array, slots, rows):
    width = KVH * HD
    if slots % 128 or rows % 128:
        array = array.astype(full)
        return array[:, :slots], array[:, slots:][:, :width], array[:, slots + width :][:, :width]
    turned = jax.ShapeDtypeStruct((width, array.shape[0]), full)
    column = pl.BlockSpec((width, rows), lambda g: (0, g))
    query, key, value = pl.pallas_call(
        split_kernel,
        out_shape=(jax.ShapeDtypeStruct((array.shape[0], slots), full), turned, turned),
        grid=(array.shape[0] // rows,),
        in_specs=[pl.BlockSpec((rows, array.shape[1]), lambda g: (g, 0))],
        out_specs=[pl.BlockSpec((rows, slots), lambda g: (g, 0)), column, column],
        compiler_params=pltpu.CompilerParams(vmem_limit_bytes=32 << 20),
        cost_estimate=pl.CostEstimate(flops=0, bytes_accessed=1 << 16, transcendentals=0),
    )(array)
    return query, key.T, value.T


def norm_backward(values, rms, gain, normed_grad):
    weighted = normed_grad * gain
    dotted = jnp.sum(weighted * values, axis=1, keepdims=True)
    grad = weighted * rms - values * (rms * rms * rms) * dotted / D
    return grad, jnp.sum(normed_grad * values * rms, axis=0)


def on_device(
    hidden_in,
    positions,
    head_counts,
    attention_gain,
    query_projection_weight,
    key_weight,
    value_weight,
    query_gain,
    key_gain,
    output_weight,
    feedforward_gain,
    gate_weight,
    up_weight,
    down_projection_weight,
    cotangent,
):
    groups = lax.axis_size("dp")
    parts = lax.axis_size("mp")
    group = lax.axis_index("dp")
    rank = lax.axis_index("mp")
    tokens, share = hidden_in.shape
    seqs = tokens // LEN
    ring = parts // seqs
    mine = tokens // parts
    chunk = mine // 2
    units = gate_weight.shape[1] // groups
    slots = query_projection_weight.shape[1]
    place = rank % ring
    ranks = range(parts)

    lower = jnp.arange(parts)[None, :] < jnp.arange(parts)[:, None]
    offsets = jnp.sum(jnp.where(lower, head_counts[None, :], 0), axis=1)

    def selection(order):
        within = jnp.arange(slots, dtype=jnp.int32)
        column = offsets[order][:, None] * HD + within[None, :]
        column = jnp.where(within[None, :] < head_counts[order][:, None] * HD, column, -1)
        return (
            column.reshape(-1)[:, None] == jnp.arange(QH * HD, dtype=jnp.int32)[None, :]
        ).astype(low)

    select_near = selection(rank ^ jnp.arange(parts, dtype=jnp.int32))
    select = selection(jnp.arange(parts, dtype=jnp.int32))

    def rows_of(array, other):
        base = (other // ring) * LEN
        at = other % ring
        first = lax.dynamic_slice_in_dim(array, base + at * chunk, chunk, 0)
        last = lax.dynamic_slice_in_dim(array, base + (2 * ring - 1 - at) * chunk, chunk, 0)
        return jnp.concatenate([first, last], 0)

    order = Order(head_counts)
    rows = D // groups
    heads_here = QH * HD // groups

    query_slice = lax.dynamic_slice_in_dim(query_projection_weight, group * rows, rows, 0)
    gains = jnp.stack([attention_gain, feedforward_gain])
    gains_high = gains.astype(low)
    gains_low = (gains - gains_high.astype(full)).astype(low)
    lines = -(-share // slots)
    gains = jnp.pad(
        jnp.concatenate([gains_high, gains_low], 0), ((0, 0), (0, lines * slots - share))
    )
    query_slice = jnp.concatenate([query_slice, gains.reshape(4 * lines, slots)], 0)
    query_slice = swap([query_slice] * parts, "mp")
    cosine, sine = rotary_tables(rows_of(positions, rank))
    chosen = lax.dynamic_slice_in_dim(select, group * heads_here, heads_here, 1)
    output_slice = dot(chosen, output_weight, 0, 0).astype(low)
    pack = jnp.concatenate(
        [
            lax.dynamic_slice_in_dim(gate_weight, group * units, units, 1),
            lax.dynamic_slice_in_dim(up_weight, group * units, units, 1),
            lax.dynamic_slice_in_dim(down_projection_weight, group * units, units, 0).T,
        ],
        1,
    )
    inputs = [rows_of(hidden_in, rank ^ k) for k in ranks]
    late = inputs[parts - 1]
    inputs = inputs[:1] + [exchange(inputs[k], "mp", k, parts) for k in range(1, parts - 1)]
    cotangent = [rows_of(cotangent, rank ^ k) for k in ranks]
    got = order(
        select_near, select, late, cosine, sine, output_slice, pack,
        *query_slice, *cotangent, *inputs
    )
    select_near, select, late, cosine, sine, output_slice, pack = got[:7]
    query_slice, cotangent = (got[7 + k * parts : 7 + (k + 1) * parts] for k in range(2))
    inputs = got[7 + 2 * parts :]

    inputs.append(exchange(late, "mp", parts - 1, parts))
    gains = by_rank([piece[rows:].reshape(4, -1)[:, :share] for piece in query_slice], rank)
    gains = jnp.concatenate(gains, 1).astype(full)
    attention_gain_all, feedforward_gain_all = gains[0] + gains[2], gains[1] + gains[3]
    query_slice = compact(query_slice, select_near, rows)
    query_all = lax.all_gather(query_slice, "dp", axis=0, tiled=True)
    *inputs, output_slice = order(*inputs, output_slice)

    output_slice = swap([output_slice] * parts, "mp")
    inputs = jnp.concatenate(by_rank(inputs, rank), axis=1).astype(full)
    first_rms = lax.rsqrt(jnp.mean(inputs * inputs, axis=1, keepdims=True) + epsilon)
    normed = (inputs * first_rms * attention_gain_all).astype(low)
    keys = dot(key_weight, normed, 0, 1).reshape(KVH, HD, mine)
    values_mine = dot(value_weight, normed, 0, 1).astype(low).reshape(KVH, HD, mine)
    turned_keys, key_pull = jax.vjp(lambda v, g: turn(v, g, cosine, sine), keys, key_gain)
    pair_mine = jnp.concatenate([turned_keys.astype(low), values_mine], 0)
    pair_mine, normed, *output_slice = order(pair_mine, normed, *output_slice)

    near_pairs = [pair_mine] + [exchange(pair_mine, "mp", k, parts) for k in range(1, ring)]
    output_slice = jnp.concatenate(by_rank(output_slice, rank), axis=1)
    output_all = lax.all_gather(output_slice, "dp", axis=0, tiled=True)
    queries = dot(query_all, normed, 0, 1).reshape(QH, HD, mine)
    turned_queries, query_pull = jax.vjp(
        lambda v, g: turn(v, g, cosine, sine), queries, query_gain
    )
    got = order(turned_queries.astype(low), *near_pairs, *cotangent)
    turned_queries, near_pairs, cotangent = got[0], got[1 : ring + 1], got[ring + 1 :]

    cotangent = swap(cotangent, "mp")
    near_pairs = by_rank(near_pairs, place)
    pair = jnp.concatenate(
        [p[:, :, :chunk] for p in near_pairs] + [p[:, :, chunk:] for p in near_pairs[::-1]], axis=2
    )
    key_heads, value_heads = pair[:KVH], pair[KVH:]
    starts = jnp.stack([place * chunk, (2 * ring - 1 - place) * chunk]).astype(jnp.int32)
    mixed, row_totals = attend(starts, turned_queries, key_heads, value_heads)
    mixed = mixed.reshape(QH * HD, mine)
    middle = inputs + dot(mixed, output_all, 0, 0)
    second_rms = lax.rsqrt(jnp.mean(middle * middle, axis=1, keepdims=True) + epsilon)
    second_normed = (middle * second_rms * feedforward_gain_all).astype(low)
    second_normed, pack, *cotangent = order(second_normed, pack, *cotangent)

    second = Spread(second_normed, "dp", groups, group)
    weights = RelayGather(pack, "mp", parts)
    cotangent_mine = jnp.concatenate(by_rank(cotangent, rank), axis=1)
    cube = groups == CUBE
    if cube:
        flag = group % 2 != 0
        pairs = [normed[:, k * rows : (k + 1) * rows] for k in range(groups)]
        normed_own, normed_other = (
            jnp.concatenate(
                [jnp.where(flag, pairs[k ^ 1 ^ a], pairs[k ^ a]) for k in range(0, groups, 2)], 1
            )
            for a in (0, 1)
        )
        pairs = mixed.reshape(4, 2, heads_here, mine)
        mixed_own, mixed_other = (
            lax.dynamic_index_in_dim(pairs, at, 1, keepdims=False).reshape(-1, mine)
            for at in (group % 2, 1 - group % 2)
        )
    else:
        normed_own = normed_other = normed
        mixed_own = mixed_other = mixed
    *got, up, down, cotangent_mine, normed_own, normed_other, mixed_own, mixed_other = order(
        *second.flying, *weights.flying, cotangent_mine, normed_own, normed_other,
        mixed_own, mixed_other
    )
    second.second(*got)
    weights.take(up, down)
    cotangent_mine, got, (up, down), second.buffer = order_split(
        order, [cotangent_mine], second.flying, weights.flying, second.buffer
    )
    cotangent_full = lax.all_gather(cotangent_mine, "dp", axis=0, tiled=True)
    second.third(*got)
    weights.take(up, down)
    got, (up, down) = order_split(order, [], second.flying, weights.flying)
    second.last(*got)
    weights.take(up, down)
    pack = weights.finish(order)
    wide = jnp.concatenate(
        [block[:, :units] for block in pack] + [block[:, units : 2 * units] for block in pack], 1
    )
    down_here = jnp.concatenate([block[:, 2 * units :] for block in pack], 1)
    half = parts * units

    raised = [mm(part, wide) for part in second.parts]
    hidden = [
        (v[:, :half] * jax.nn.sigmoid(v[:, :half]) * v[:, half:]).astype(low) for v in raised
    ]
    down_terms = [dot(h, down_here, 1, 1).astype(low) for h in hidden]
    down_terms, raised, hidden, (cotangent_full,) = order_split(
        order, [], down_terms, raised, hidden, [cotangent_full]
    )

    core = group % 2
    if cube:
        back = lambda at, v: units_back(cotangent_full, at, v, down_here, wide)
    else:
        back = lambda at, v: units_back_whole(cotangent_full, v, down_here, wide)
    grad, other = back(1 - core, raised[-1])
    grads = [grad]
    other, grads[0], *raised = order(other, grads[0], *raised)

    second_sum = Collect(other, "dp", groups, group)
    own = other
    if len(raised) > 1:
        grad, own = back(core, raised[0])
        grads.insert(0, grad)
    own, *grads, hidden, got = order_split(order, [own, *grads], hidden, second_sum.flying)

    second_sum.second(own, *got)
    wide_grad = sum(dot(part, grad, 0, 0) for part, grad in zip(second.parts, grads)).astype(low)
    if cube:
        shape = (4, 1, mine, half)
        first, last = (h.reshape(shape) for h in hidden)
        hidden_full = jnp.concatenate(
            [jnp.where(core == 0, first, last), jnp.where(core == 0, last, first)], 1
        ).reshape(2 * 4 * mine, half)
    else:
        hidden_full = hidden[0]
    down_grad = dot(cotangent_full, hidden_full, 0, 0).astype(low)
    down_sum = Collect(down_terms[-1], "dp", groups, group)
    down_grad, wide_grad, got, flying = order_split(
        order, [down_grad, wide_grad], second_sum.flying, down_sum.flying
    )

    second_sum.third(*got)

    pack = by_ranks(wide_grad, down_grad, rank, parts)
    pack = lax.psum_scatter(pack, "mp", scatter_dimension=0, tiled=False)
    down_sum.second(down_terms[0], *flying, apart=True)
    *got, flying = order_split(order, second_sum.flying, down_sum.flying)

    normed_two_grad = second_sum.last(*got).astype(full)
    down_sum.launch(*flying)
    middle_part, feedforward_gain_grad = norm_backward(
        middle, second_rms, feedforward_gain_all, normed_two_grad
    )
    middle_grad = cotangent_mine.astype(full) + middle_part
    lane = lax.broadcasted_iota(jnp.int32, (D, EXTRA), 1)
    wide_extra = jnp.where(lane == 0, feedforward_gain_grad[:, None], 0.0)
    branch_grad = middle_grad.astype(low)
    mixed_grad = dot(output_all, branch_grad, 1, 1).astype(low).reshape(QH, HD, mine)
    output_other = mm(mixed_other, branch_grad).astype(low)
    output_own = mm(mixed_own, branch_grad).astype(low) if cube else output_other
    output_sum = Collect(output_other, "dp", groups, group)
    query_rot_grad, key_rot_grad, value_grad = attend_back(
        starts, turned_queries, key_heads, value_heads, mixed_grad, row_totals
    )
    pair_grad = jnp.concatenate([key_rot_grad, value_grad], 0)
    blocks = [
        jnp.concatenate(
            [
                pair_grad[:, :, j * chunk : (j + 1) * chunk],
                pair_grad[:, :, (2 * ring - 1 - j) * chunk : (2 * ring - j) * chunk],
            ],
            axis=2,
        )
        for j in range(ring)
    ]
    blocks = by_rank(blocks, place)
    away = [block.astype(low) for block in blocks[1:]]
    query_rot_grad, output_own, *away, got, flying = order_split(
        order, [query_rot_grad, output_own, *away], down_sum.flying, output_sum.flying
    )
    down_sum.third(*got)
    output_sum.second(output_own, *flying)

    away = [exchange(block, "mp", k + 1, parts) for k, block in enumerate(away)]
    queries_low, query_gain_grad = query_pull(query_rot_grad)
    queries_low = queries_low.astype(low).reshape(QH * HD, mine)
    queries_low, pack, wide_extra, *away, out_relayed, got = order_split(
        order, [queries_low, pack, wide_extra, *away], down_sum.flying, output_sum.flying
    )
    output_sum.third(*got)
    pack = by_rows(lax.all_gather(by_rows(pack), "dp", axis=0, tiled=False))
    pair_grad = sum([blocks[0]] + [block.astype(full) for block in away])
    keys_grad, key_gain_grad = key_pull(pair_grad[:KVH])
    pair_low = jnp.concatenate(
        [keys_grad.astype(low), pair_grad[KVH:].astype(low)], 0
    ).reshape(2 * KVH * HD, mine)
    all_low = jnp.concatenate([queries_low, pair_low], 0)
    heads_gain = jnp.stack([query_gain_grad, key_gain_grad])
    top = wide_extra[:2] + jnp.pad(heads_gain, ((0, 0), (EXTRA - HD, 0)))
    extra = jnp.concatenate([top, wide_extra[2:]], 0)
    wide_low = jnp.concatenate([all_low, jnp.zeros((EXTRA, mine), low)], 0)

    def projections(normed_part, extra_part):
        extra_part = jnp.pad(extra_part, ((0, 0), (wide_low.shape[0] - EXTRA, 0)))
        return (dot(normed_part, wide_low, 0, 1) + extra_part).astype(low)

    own = other = extra
    if cube:
        pairs = extra.reshape(4, 2, rows, EXTRA)
        own, other = (
            lax.dynamic_index_in_dim(pairs, at, 1, keepdims=False).reshape(4 * rows, EXTRA)
            for at in (group % 2, 1 - group % 2)
        )
    other = projections(normed_other, other)
    other, own, wide_low, all_low, normed_own = order(other, own, wide_low, all_low, normed_own)

    def by_feature(array):
        return by_rank([array[:, j * share : (j + 1) * share] for j in ranks], rank)

    projection_sum = Collect(other, "dp", groups, group)
    own = projections(normed_own, own) if cube else other
    queries_low, pair_low = all_low[: QH * HD], all_low[QH * HD :]
    normed_grad = (
        dot(queries_low, query_all, 0, 1)
        + dot(pair_low[: KVH * HD], key_weight, 0, 1)
        + dot(pair_low[KVH * HD :], value_weight, 0, 1)
    )
    input_part, _ = norm_backward(
        inputs, first_rms, attention_gain_all, normed_grad
    )
    input_gradient = (middle_grad + input_part).astype(low)
    input_gradient, own, got, flying = order_split(
        order, [input_gradient, own], projection_sum.flying, output_sum.flying
    )
    projection_sum.second(own, *got)
    output_grad = output_sum.last(*flying)

    def by_tokens(got, kind):
        got = by_rank(got, rank)
        rows = []
        for seq in range(seqs):
            near = got[seq * ring : (seq + 1) * ring]
            rows += [block[:chunk] for block in near]
            rows += [block[chunk:] for block in near[::-1]]
        return jnp.concatenate(rows, 0).astype(kind)

    input_gradient = swap(by_feature(input_gradient), "mp")
    input_gradient, got, out_relayed = order_split(
        order, [], input_gradient, projection_sum.flying, out_relayed
    )
    projection_sum.third(*got)

    output_grad = swap(by_feature(output_grad), "mp")
    output_grad, got, out_relayed = order_split(
        order, [], output_grad, projection_sum.flying, out_relayed
    )
    output_grad = lax.all_gather(added(*output_grad), "dp", axis=0, tiled=True)
    projection_total = projection_sum.last(*got)
    down_sum.fourth(*out_relayed)

    query_total, pair_total, extra = jnp.split(
        projection_total, [QH * HD, (QH + 2 * KVH) * HD], axis=1
    )
    here = lambda weight: lax.dynamic_slice_in_dim(weight, group * rows, rows, 0).astype(full)
    product = jnp.sum(here(query_all) * query_total.astype(full), axis=1)
    product += jnp.sum(here(key_weight) * pair_total[:, : KVH * HD].astype(full), axis=1)
    product += jnp.sum(here(value_weight) * pair_total[:, KVH * HD :].astype(full), axis=1)
    product = product / lax.dynamic_slice_in_dim(attention_gain_all, group * rows, rows, 0)
    column = lax.broadcasted_iota(jnp.int32, extra.shape, 1)
    extra = jnp.where(column == 2, product[:, None].astype(low), extra)
    query_part = dot(query_total, select_near, 1, 1).astype(low)
    projection = swap(
        [
            jnp.concatenate([query_part[:, k * slots : (k + 1) * slots], pair_total, extra], 1)
            for k in ranks
        ],
        "mp",
    )
    input_gradient = by_tokens(input_gradient, full)
    pack, input_gradient, projection, flying = order_split(
        order, [pack, input_gradient], projection, down_sum.flying
    )

    projection = lax.all_gather(added(*projection), "dp", axis=0, tiled=True)
    output_weight_grad = mm(select, output_grad)
    output = (middle + down_sum.last(*flying).astype(full)).astype(low)
    output = swap(by_feature(output), "mp")
    gate_weight_grad, up_weight_grad, down_weight_grad = widen(pack)
    query_weight_grad, key_weight_grad, value_weight_grad = split_projections(
        projection, slots, rows
    )
    (
        query_weight_grad, key_weight_grad, value_weight_grad, gate_weight_grad, up_weight_grad,
        down_weight_grad, output_weight_grad, output,
    ) = order_split(
        order,
        [
            query_weight_grad, key_weight_grad, value_weight_grad, gate_weight_grad,
            up_weight_grad, down_weight_grad, output_weight_grad,
        ],
        output,
    )
    output = by_tokens(output, low)
    extra = projection[:, slots + 2 * KVH * HD :]
    extra = extra.astype(full)
    own_share = lax.dynamic_slice_in_dim(extra, rank * share, share, 0)
    return (
        output,
        input_gradient,
        own_share[:, 2],
        query_weight_grad.astype(full),
        key_weight_grad.astype(full),
        value_weight_grad.astype(full),
        extra[0, EXTRA - HD :],
        extra[1, EXTRA - HD :],
        output_weight_grad,
        own_share[:, 0],
        gate_weight_grad,
        up_weight_grad,
        down_weight_grad,
    )


def solution(mesh):
    in_specs = (
        P("dp", "mp"),
        P("dp"),
        P(),
        P("mp"),
        P(None, "mp"),
        P(),
        P(),
        P(),
        P(),
        P(None, "mp"),
        P("mp"),
        P(None, "mp"),
        P(None, "mp"),
        P("mp", None),
        P("dp", "mp"),
    )
    out_specs = (
        P("dp", "mp"),
        P("dp", "mp"),
        P("mp"),
        P(None, "mp"),
        P(),
        P(),
        P(),
        P(),
        P(None, "mp"),
        P("mp"),
        P(None, "mp"),
        P(None, "mp"),
        P("mp", None),
    )
    return jax.shard_map(
        on_device, mesh=mesh, in_specs=in_specs, out_specs=out_specs, check_vma=False
    )
```
